32 devices in a mesh: fsdp: 4 (over x, core), ctx: 4 (over z), tp: 2 (over y).
Axes of the slice: x: 2, y: 2, z: 4, core: 2. Of those that a mesh axis runs over, the one named last changes fastest.
Arguments:
- earlier: bfloat16 [8, 8, 1024, 2048], P(None, 'fsdp', 'ctx'), may hold values from -6 to 6
- mix_in: float32 [32, 8, 1024], P(None, 'fsdp', 'ctx'), may hold values from -3 to 3
- lengths: int32 [8], P('fsdp'), may hold values from 256 to 1024, as said below
- w_query: bfloat16 [2048, 2048], P(('fsdp', 'ctx'), 'tp'), may hold values from -0.125 to 0.125
- w_key: bfloat16 [2048, 2048], P(('fsdp', 'ctx'), 'tp'), may hold values from -0.125 to 0.125
- w_value: bfloat16 [2048, 2048], P(('fsdp', 'ctx'), 'tp'), may hold values from -0.125 to 0.125
- w_proj: bfloat16 [2048, 2048], P('tp', ('fsdp', 'ctx')), may hold values from -2 to 2
- w_up: bfloat16 [2048, 8192], P(('fsdp', 'ctx'), 'tp'), may hold values from -0.125 to 0.125
- w_down: bfloat16 [8192, 2048], P('tp', ('fsdp', 'ctx')), may hold values from -0.0625 to 0.0625
- first_gain: bfloat16 [2048], P(('fsdp', 'ctx')), may hold values from 0.099609375 to 1.8984375
- first_shift: bfloat16 [2048], P(('fsdp', 'ctx')), may hold values from -3 to 3
- second_gain: bfloat16 [2048], P(('fsdp', 'ctx')), may hold values from 0.099609375 to 1.8984375
- second_shift: bfloat16 [2048], P(('fsdp', 'ctx')), may hold values from -3 to 3
- mixer_in: bfloat16 [2048, 36], P(('fsdp', 'ctx')), may hold values from -0.125 to 0.125
- mixer_out: float32 [36, 36], replicated, may hold values from -1 to 1
- mixer_bias: float32 [36], replicated, may hold values from -3 to 3
- grad_out: bfloat16 [8, 1024, 2048], P('fsdp', 'ctx'), may hold values from -6 to 6
- grad_mix: float32 [36, 8, 1024], P(None, 'fsdp', 'ctx'), may hold values from -12 to 12
Outputs:
- output: bfloat16 [8, 1024, 2048], P('fsdp', 'ctx')
- mix_out: float32 [36, 8, 1024], P(None, 'fsdp', 'ctx')
- grad_earlier: bfloat16 [8, 8, 1024, 2048], P(None, 'fsdp', 'ctx')
- grad_mix_in: float32 [32, 8, 1024], P(None, 'fsdp', 'ctx')
- grad_query: float32 [2048, 2048], P(('fsdp', 'ctx'), 'tp')
- grad_key: float32 [2048, 2048], P(('fsdp', 'ctx'), 'tp')
- grad_value: float32 [2048, 2048], P(('fsdp', 'ctx'), 'tp')
- grad_proj: float32 [2048, 2048], P('tp', ('fsdp', 'ctx'))
- grad_up: float32 [2048, 8192], P(('fsdp', 'ctx'), 'tp')
- grad_down: float32 [8192, 2048], P('tp', ('fsdp', 'ctx'))
- grad_first_gain: float32 [2048], P(('fsdp', 'ctx'))
- grad_first_shift: float32 [2048], P(('fsdp', 'ctx'))
- grad_second_gain: float32 [2048], P(('fsdp', 'ctx'))
- grad_second_shift: float32 [2048], P(('fsdp', 'ctx'))
- grad_mixer_in: float32 [2048, 36], P(('fsdp', 'ctx'))
- grad_mixer_out: float32 [36, 36], replicated
- grad_mixer_bias: float32 [36], replicated
The draws below stay inside these ranges and needn't reach their ends.
Inputs may be any that keep to these rules, and one draw needn't show every extreme that they name: `lengths`: every row is used from slot 0; some row uses all 1024 slots and some row uses a quarter of them.
All inputs are finite; a program needn't handle non-finite values.
Results may differ from the reference program's by a relative error of at most 0.012.
Values may be sent and summed in bfloat16 or wider, within the bound.
No kernel may reach another device: no remote copies, remote signals or barrier semaphores. Data moves between devices by JAX's collectives and lax.ppermute only.
A program may use at most 960 MiB of HBM per device.

```python
import math
import jax
import jax.numpy as jnp
from jax import lax

D = 2048
HEADS = 16
HD = 128
ROT = 32
FF = 8192
NPREV = 8
STREAMS = 4
MIXW = 36
SEQ = 1024
ROWS = 8


def draw_lengths(key, part):
    first, second = jax.random.split(key)
    drawn = jax.random.randint(first, (ROWS,), SEQ // 4, SEQ + 1, dtype=jnp.int32)
    order = jax.random.permutation(second, ROWS)
    drawn = drawn.at[order[0]].set(SEQ)
    drawn = drawn.at[order[1]].set(SEQ // 4)
    return drawn.astype(jnp.int32)


def steps_of(stream_key, dims, shards, smallest, high):
    level, own = 1.0, jax.random.fold_in(stream_key, 6)
    for dim, blocks in shards:
        draws = jnp.exp(jax.random.uniform(jax.random.fold_in(own, dim), (blocks,), jnp.float32, smallest / len(shards), high / len(shards)))
        level = level * jnp.repeat(draws, dims[dim] // blocks).reshape([-1 if axis == dim else 1 for axis in range(len(dims))])
    return level


def normal_values(rng, shape, scale, reach, cuts=(), kind=jnp.bfloat16):
    factor_of = steps_of(rng, shape, cuts, -0.22, 0.18) if cuts else 1.0
    array = jax.random.normal(rng, shape, jnp.float32) * scale * factor_of
    return jnp.minimum(jnp.maximum(array, -reach), reach).astype(kind)


def setup_inputs(seed: int = 0) -> dict:
    seeds = jax.random.split(jax.random.key(seed), 19)
    return {
        "earlier": normal_values(seeds[0], (NPREV, ROWS, SEQ, D), 1.0, 6.0, ((1, 4), (2, 4))),
        "mix_in": normal_values(seeds[1], (STREAMS * NPREV, ROWS, SEQ), 0.5, 3.0, ((1, 4), (2, 4)), jnp.float32),
        "lengths": draw_lengths(jax.random.fold_in(seeds[18], 71), 0),
        "w_query": normal_values(seeds[3], (D, D), D ** -0.5, 0.125, ((0, 16), (1, 2))),
        "w_key": normal_values(seeds[4], (D, D), D ** -0.5, 0.125, ((0, 16), (1, 2))),
        "w_value": normal_values(seeds[5], (D, D), D ** -0.5, 0.125, ((0, 16), (1, 2))),
        "w_proj": normal_values(seeds[6], (D, D), (max(D // 256, 1)) ** -0.5, 2.0, ((0, 2), (1, 16))),
        "w_up": normal_values(seeds[7], (D, FF), D ** -0.5, 0.125, ((0, 16), (1, 2))),
        "w_down": normal_values(seeds[8], (FF, D), FF ** -0.5, 0.0625, ((0, 2), (1, 16))),
        "first_gain": jnp.clip(1.0 + 0.18 * jax.random.normal(seeds[9], (D,), jnp.float32), 0.099609375, 1.8984375).astype(jnp.bfloat16),
        "first_shift": normal_values(seeds[10], (D,), 0.3, 3.0, ((0, 16),)),
        "second_gain": jnp.clip(1.0 + 0.18 * jax.random.normal(seeds[11], (D,), jnp.float32), 0.099609375, 1.8984375).astype(jnp.bfloat16),
        "second_shift": normal_values(seeds[12], (D,), 0.3, 3.0, ((0, 16),)),
        "mixer_in": normal_values(seeds[13], (D, MIXW), D ** -0.5, 0.125, ((0, 16),)),
        "mixer_out": normal_values(seeds[14], (MIXW, MIXW), MIXW ** -0.5, 1.0, (), jnp.float32),
        "mixer_bias": normal_values(seeds[15], (MIXW,), 0.5, 3.0, (), jnp.float32),
        "grad_out": normal_values(seeds[16], (ROWS, SEQ, D), 1.0, 6.0, ((0, 4), (1, 4))),
        "grad_mix": normal_values(seeds[17], (MIXW, ROWS, SEQ), 2.0, 12.0, ((1, 4), (2, 4)), jnp.float32),
    }


EPSILON = 1e-05
RMS_EPSILON = 1e-06
HIGHEST = lax.Precision.HIGHEST
NEGATIVE = -1e+30

@jax.custom_vjp
def low(v):
    return lax.optimization_barrier(v.astype(jnp.bfloat16)).astype(jnp.float32)

@jax.custom_vjp
def low_back(v):
    return v

def low_keep(v):
    return (low(v), None)

def low_pass(kept, grad):
    return (grad,)

def back_keep(v):
    return (v, None)

def back_low(kept, grad):
    return (low(grad),)
low.defvjp(low_keep, low_pass)
low_back.defvjp(back_keep, back_low)

def layer_norm(values, gain, shift):
    center = values - lax.optimization_barrier(jnp.mean(values, axis=-1, keepdims=True))
    spread = lax.optimization_barrier(jnp.mean(center * center, axis=-1, keepdims=True))
    return center * lax.rsqrt(spread + EPSILON) * gain + shift

def rotate(values, positions):
    half = ROT // 2
    frequency = 10000.0 ** (-2.0 * jnp.arange(half, dtype=jnp.float32) / ROT)
    angles = positions.astype(jnp.float32)[:, None] * frequency[None, :]
    cosine = jnp.cos(angles)[:, None, :]
    sine = jnp.sin(angles)[:, None, :]
    first = values[..., :half]
    second = values[..., half:ROT]
    return jnp.concatenate([first * cosine - second * sine, second * cosine + first * sine, values[..., ROT:]], axis=-1)

def activate(values):
    return jax.nn.gelu(values, approximate=False)

def matmul(left, right):
    return jnp.dot(left, right, precision=HIGHEST, preferred_element_type=jnp.float32)

def mixer(final, weight_in, weight_out, bias):
    normed = final * lax.rsqrt(lax.optimization_barrier(jnp.mean(final * final, axis=-1, keepdims=True)) + RMS_EPSILON)
    hidden = activate(matmul(normed, weight_in))
    return matmul(hidden, weight_out) + bias

def attend_row(items):
    query, keys, values, length = items
    seq = query.shape[0]
    slots = jnp.arange(seq, dtype=jnp.int32)
    scores = low_back(jnp.einsum('shd,thd->hst', query, keys, precision=HIGHEST)) * (1.0 / math.sqrt(HD))
    allowed = (slots[None, :] <= slots[:, None]) & (slots[None, :] < length)
    masked = jnp.where(allowed[None], scores, NEGATIVE)
    top = lax.optimization_barrier(jnp.max(masked, axis=-1, keepdims=True))
    expo = jnp.exp(masked - top)
    probs = expo / lax.optimization_barrier(jnp.sum(expo, axis=-1, keepdims=True))
    return jnp.einsum('hst,thd->shd', low(probs), values, precision=HIGHEST)

def forward(inputs, coeff, lengths, w_query, w_key, w_value, w_proj, w_up, w_down, first_gain, first_shift, second_gain, second_shift, mixer_in, mixer_out, mixer_bias):
    group, seq = (inputs.shape[1], inputs.shape[2])
    streams = jnp.einsum('sjgt,jgtd->sgtd', coeff.reshape(STREAMS, NPREV, group, seq), inputs, precision=HIGHEST)
    slots = jnp.arange(seq, dtype=jnp.int32)
    query_in = low(layer_norm(streams[0], first_gain, first_shift))
    key_in = low(layer_norm(streams[1], first_gain, first_shift))
    value_in = low(layer_norm(streams[2], first_gain, first_shift))
    query_pre = low_back(matmul(query_in, w_query)).reshape(group, seq, HEADS, HD)
    key_pre = low_back(matmul(key_in, w_key)).reshape(group, seq, HEADS, HD)
    query_rot = low(rotate(query_pre, slots))
    key_rot = low(rotate(key_pre, slots))
    value_all = low(low_back(matmul(value_in, w_value))).reshape(group, seq, HEADS, HD)
    attended = lax.map(jax.checkpoint(attend_row), (query_rot, key_rot, value_all, lengths))
    attended = low(low_back(attended.reshape(group, seq, D)))
    branch = low_back(matmul(attended, w_proj))
    residual = streams[3] + branch
    normed = low(layer_norm(residual, second_gain, second_shift))
    upward = low_back(matmul(normed, w_up))
    active = low(activate(upward))
    downward = low_back(matmul(active, w_down))
    final = residual + downward
    mixes = mixer(final, mixer_in, mixer_out, mixer_bias)
    return (final, jnp.transpose(mixes, (2, 0, 1)))

def reference(earlier, mix_in, lengths, w_query, w_key, w_value, w_proj, w_up, w_down, first_gain, first_shift, second_gain, second_shift, mixer_in, mixer_out, mixer_bias, grad_out, grad_mix):
    weights = tuple((w.astype(jnp.float32) for w in (w_query, w_key, w_value, w_proj, w_up, w_down, first_gain, first_shift, second_gain, second_shift, mixer_in, mixer_out, mixer_bias)))
    group = math.gcd(ROWS, max(1, 4096 // SEQ))
    group_count = ROWS // group
    slots = jnp.arange(SEQ, dtype=jnp.int32)

    def step(totals, index):
        start = (index * group).astype(jnp.int32)
        inputs = lax.dynamic_slice_in_dim(earlier, start, group, 1).astype(jnp.float32)
        coeff = lax.dynamic_slice_in_dim(mix_in, start, group, 1)
        row_lengths = lax.dynamic_slice_in_dim(lengths, start, group, 0)
        cotangent = lax.dynamic_slice_in_dim(grad_out, start, group, 0).astype(jnp.float32)
        mix_cotangent = lax.dynamic_slice_in_dim(grad_mix, start, group, 1)
        valid = (slots[None, :] < row_lengths[:, None]).astype(jnp.float32)

        def run(inputs_f, coeff_f, *params):
            return forward(inputs_f, coeff_f, row_lengths, *params)
        (final, mixes), pull = jax.vjp(run, inputs, coeff, *weights)
        grads = pull((cotangent * valid[:, :, None], mix_cotangent * valid[None]))
        new_totals = tuple((a + b for a, b in zip(totals, grads[2:])))
        return (new_totals, (final.astype(jnp.bfloat16), mixes, grads[0].astype(jnp.bfloat16), grads[1]))
    start_totals = tuple((jnp.zeros(w.shape, jnp.float32) for w in weights))
    totals, stacked = lax.scan(step, start_totals, jnp.arange(group_count, dtype=jnp.int32))
    final_all, mix_all, grad_inputs, grad_coeff = stacked
    output = final_all.reshape(ROWS, SEQ, D)
    mix_out = jnp.transpose(mix_all, (1, 0, 2, 3)).reshape(MIXW, ROWS, SEQ)
    grad_earlier = jnp.transpose(grad_inputs, (1, 0, 2, 3, 4)).reshape(NPREV, ROWS, SEQ, D)
    grad_mix_in = jnp.transpose(grad_coeff, (1, 0, 2, 3)).reshape(STREAMS * NPREV, ROWS, SEQ)
    return (output, mix_out, grad_earlier, grad_mix_in, totals[0], totals[1], totals[2], totals[3], totals[4], totals[5], totals[6], totals[7], totals[8], totals[9], totals[10], totals[11], totals[12])
```

```python
from functools import partial
import math

import jax
import jax.numpy as jnp
from jax import lax
from jax.experimental import pallas as pl
from jax.experimental.pallas import tpu as pltpu
from jax.sharding import PartitionSpec as P

HD = 128
ROT = 32
STREAMS = 4
MIXW = 36
EPSILON = 1e-05
RMS_EPSILON = 1e-06
HIGHEST = lax.Precision.HIGHEST
NEGATIVE = -1e30
F32 = jnp.float32
BF16 = jnp.bfloat16
GROUP = 16


def params(grid_rank):
    return pltpu.CompilerParams(
        dimension_semantics=("arbitrary",) * grid_rank, vmem_limit_bytes=56 * 1024 * 1024
    )


def xor_pairs(size, mask):
    return [(i, i ^ mask) for i in range(size)]


def over_fsdp(values, mask):
    return lax.ppermute(values, "fsdp", xor_pairs(lax.axis_size("fsdp"), mask))


def over_tp(values):
    return lax.ppermute(values, "tp", xor_pairs(lax.axis_size("tp"), 1))


def shift_ctx(values, step):
    size = lax.axis_size("ctx")
    return lax.ppermute(values, "ctx", [(i, (i + step) % size) for i in range(size)])


def bits_of(size):
    return [1 << b for b in reversed(range(size.bit_length() - 1))]


def block_masks(size):
    masks = [0]
    for bit in bits_of(size):
        masks = masks + [m ^ bit for m in masks]
    return masks


def gather_blocks(shard):
    parts = [lax.all_gather(shard, "ctx", axis=0, tiled=True)]
    for bit in bits_of(lax.axis_size("fsdp")):
        parts = parts + [over_fsdp(p, bit) for p in parts]
    return parts


def scatter_blocks(blocks):
    for bit in reversed(bits_of(lax.axis_size("fsdp"))):
        half = len(blocks) // 2
        masks = block_masks(len(blocks))
        keep, send = blocks[:half], blocks[half:]
        blocks = [k + over_fsdp(s.astype(BF16), bit).astype(F32) for k, s in zip(keep, send)]
    return lax.psum_scatter(
        blocks[0].astype(BF16), "ctx", scatter_dimension=0, tiled=True
    ).astype(F32)


def tp_sum(part):
    mine = lax.optimization_barrier(part.astype(BF16))
    return mine.astype(F32) + over_tp(mine).astype(F32)


def mix_kernel(perm_ref, earlier_ref, coeff_ref, gain_ref, shift_ref, a_ref, z_ref):
    prev = earlier_ref.shape[0]
    width = earlier_ref.shape[2]
    parts = perm_ref.shape[0]
    block = width // parts
    step = min(block, 256)

    def group(i, carry):
        rows = pl.ds(pl.multiple_of(i * GROUP, GROUP), GROUP)
        coeff = coeff_ref[rows, :]
        for p in range(parts):
            for c in range(0, block, step):
                source = pl.ds(pl.multiple_of(perm_ref[p] * block + c, 128), step)
                sums = [None] * STREAMS
                for j in range(prev):
                    x = earlier_ref[j, rows, source].astype(F32)
                    for s in range(STREAMS):
                        k = s * prev + j
                        term = coeff[:, k : k + 1] * x
                        sums[s] = term if sums[s] is None else sums[s] + term
                for s in range(STREAMS):
                    z_ref[s, rows, p * block + c : p * block + c + step] = sums[s]
        for s in range(STREAMS - 1):
            z = z_ref[s, rows, :]
            center = z - jnp.mean(z, axis=-1, keepdims=True)
            spread = jnp.mean(center * center, axis=-1, keepdims=True)
            a_ref[s, rows, :] = (
                center * lax.rsqrt(spread + EPSILON) * gain_ref[...] + shift_ref[...]
            ).astype(BF16)
        return carry

    lax.fori_loop(0, earlier_ref.shape[1] // GROUP, group, 0)


def mix_streams(perm, inputs, coeff, gain, shift, tile=64):
    prev, tokens, width = inputs.shape
    return pl.pallas_call(
        mix_kernel,
        name="mix",
        grid_spec=pltpu.PrefetchScalarGridSpec(
            num_scalar_prefetch=1,
            grid=(tokens // tile,),
            in_specs=[
                pl.BlockSpec((prev, tile, width), lambda t, *_: (0, t, 0)),
                pl.BlockSpec((tile, coeff.shape[1]), lambda t, *_: (t, 0)),
                pl.BlockSpec((1, width), lambda t, *_: (0, 0)),
                pl.BlockSpec((1, width), lambda t, *_: (0, 0)),
            ],
            out_specs=[
                pl.BlockSpec((STREAMS - 1, tile, width), lambda t, *_: (0, t, 0)),
                pl.BlockSpec((STREAMS, tile, width), lambda t, *_: (0, t, 0)),
            ],
        ),
        out_shape=[
            jax.ShapeDtypeStruct((STREAMS - 1, tokens, width), BF16),
            jax.ShapeDtypeStruct((STREAMS, tokens, width), F32),
        ],
        compiler_params=params(1),
    )(perm, inputs, coeff, gain, shift)


def turn(values, tables, sign):
    base, up, down = tables
    return (
        values * base
        + sign * (pltpu.roll(values, ROT // 2, 1) * up)
        + sign * (pltpu.roll(values, HD - ROT // 2, 1) * down)
    )


def blocks_kernel(place_ref, a_ref, *refs, parts, turned):
    weights = refs[:parts]
    tables = refs[parts : parts + 3]
    out_ref = refs[-1]
    block = a_ref.shape[1] // parts
    total = None
    for p in range(parts):
        term = jnp.dot(
            a_ref[:, p * block : (p + 1) * block], weights[p][...], preferred_element_type=F32
        )
        total = term if total is None else total + term
    if turned:
        tabs = [t[...] for t in tables]
        for h in range(total.shape[1] // HD):
            cols = slice(h * HD, (h + 1) * HD)
            out_ref[0, :, cols] = turn(total[:, cols], tabs, 1.0).astype(BF16)
    else:
        out_ref[0] = total.astype(BF16)


def blocks_product(place, a, weights, tables, turned):
    tokens, width = a.shape
    parts = len(weights)
    chunks = place.shape[0]
    columns = weights[0].shape[1] // chunks
    block = width // parts
    return pl.pallas_call(
        partial(blocks_kernel, parts=parts, turned=turned),
        name="heads",
        grid_spec=pltpu.PrefetchScalarGridSpec(
            num_scalar_prefetch=1,
            grid=(chunks,),
            in_specs=[pl.BlockSpec((tokens, width), lambda n, *_: (0, 0))]
            + [pl.BlockSpec((block, columns), lambda n, *_: (0, n))] * parts
            + [pl.BlockSpec((tokens, HD), lambda n, *_: (0, 0))] * 3,
            out_specs=pl.BlockSpec((1, tokens, columns), lambda n, place: (place[n], 0, 0)),
        ),
        out_shape=jax.ShapeDtypeStruct((chunks, tokens, columns), BF16),
        compiler_params=params(1),
    )(place, a, *weights, *tables)


def weights_of(query, keys, tile_index, tile, length, scale):
    count = keys.shape[0]
    scores = (
        lax.dot_general(query, keys, (((1,), (1,)), ((), ())), preferred_element_type=F32) * scale
    )
    row = tile_index * tile + lax.broadcasted_iota(jnp.int32, (tile, count), 0)
    col = lax.broadcasted_iota(jnp.int32, (tile, count), 1)
    masked = jnp.where((col <= row) & (col < length), scores, NEGATIVE)
    expo = jnp.exp(masked - jnp.max(masked, axis=-1, keepdims=True))
    return expo / jnp.sum(expo, axis=-1, keepdims=True)


def collect(source_ref, pieces, scratch, span):
    for s, piece in enumerate(pieces):
        at = pl.ds(pl.multiple_of(source_ref[s] * span, span), span)
        scratch[at, :] = piece[...]


def spread_out(source_ref, scratch, pieces, span):
    for s, piece in enumerate(pieces):
        at = pl.ds(pl.multiple_of(source_ref[s] * span, span), span)
        piece[...] = scratch[at, :]


def attend_kernel(source_ref, length_ref, *refs, chunks):
    q_in, k_in, v_in = refs[:chunks], refs[chunks : 2 * chunks], refs[2 * chunks : 3 * chunks]
    outs = refs[3 * chunks : 4 * chunks]
    q_all, k_all, v_all, o_all = refs[4 * chunks :]
    span = q_in[0].shape[0]
    length = length_ref[pl.program_id(0)]
    scale = 1.0 / math.sqrt(HD)
    collect(source_ref, q_in, q_all, span)
    collect(source_ref, k_in, k_all, span)
    collect(source_ref, v_in, v_all, span)
    for h in range(q_all.shape[1] // HD):
        cols = slice(h * HD, (h + 1) * HD)
        for i in range(chunks):
            rows = slice(i * span, (i + 1) * span)
            seen = slice(0, (i + 1) * span)
            probs = weights_of(q_all[rows, cols], k_all[seen, cols], i, span, length, scale)
            o_all[rows, cols] = jnp.dot(
                probs.astype(BF16), v_all[seen, cols], preferred_element_type=F32
            ).astype(BF16)
    spread_out(source_ref, o_all, outs, span)


def attend(source, lengths, queries, keys, values):
    chunks = len(queries)
    rows = lengths.shape[0]
    tokens, columns = queries[0].shape
    span = tokens // rows
    spec = pl.BlockSpec((span, columns), lambda r, *_: (r, 0))
    return pl.pallas_call(
        partial(attend_kernel, chunks=chunks),
        name="attend",
        grid_spec=pltpu.PrefetchScalarGridSpec(
            num_scalar_prefetch=2,
            grid=(rows,),
            in_specs=[spec] * (3 * chunks),
            out_specs=[spec] * chunks,
            scratch_shapes=[pltpu.VMEM((span * chunks, columns), BF16)] * 4,
        ),
        out_shape=[jax.ShapeDtypeStruct((tokens, columns), BF16)] * chunks,
        compiler_params=params(1),
    )(source, lengths, *queries, *keys, *values)


def attend_back_kernel(source_ref, length_ref, *refs, chunks):
    q_in, k_in, v_in, g_in = [refs[n * chunks : (n + 1) * chunks] for n in range(4)]
    tabs = refs[4 * chunks : 4 * chunks + 3]
    outs = refs[4 * chunks + 3 : 7 * chunks + 3]
    q_all, k_all, v_all, g_all, dk_sum, dv_sum, dq_all, dk_all, dv_all = refs[7 * chunks + 3 :]
    span = q_in[0].shape[0]
    length = length_ref[pl.program_id(0)]
    scale = 1.0 / math.sqrt(HD)
    collect(source_ref, q_in, q_all, span)
    collect(source_ref, k_in, k_all, span)
    collect(source_ref, v_in, v_all, span)
    collect(source_ref, g_in, g_all, span)
    by_rows = (((0,), (0,)), ((), ()))
    for h in range(q_all.shape[1] // HD):
        cols = slice(h * HD, (h + 1) * HD)
        for i in reversed(range(chunks)):
            rows = slice(i * span, (i + 1) * span)
            seen = slice(0, (i + 1) * span)
            query, grad = q_all[rows, cols], g_all[rows, cols]
            keys, values = k_all[seen, cols], v_all[seen, cols]
            probs = weights_of(query, keys, i, span, length, scale)
            grad_probs = lax.dot_general(
                grad, values, (((1,), (1,)), ((), ())), preferred_element_type=F32
            )
            delta = jnp.sum(probs * grad_probs, axis=-1, keepdims=True)
            scores = (probs * (grad_probs - delta) * scale).astype(BF16)
            turned = [t[rows, :] for t in tabs]
            dq_all[rows, cols] = turn(
                jnp.dot(scores, keys, preferred_element_type=F32), turned, -1.0
            ).astype(BF16)
            dk = lax.dot_general(scores, query, by_rows, preferred_element_type=F32)
            dv = lax.dot_general(probs.astype(BF16), grad, by_rows, preferred_element_type=F32)
            if i == chunks - 1:
                dk_sum[...] = dk
                dv_sum[...] = dv
            else:
                dk_sum[seen, :] += dk
                dv_sum[seen, :] += dv
        dk_all[:, cols] = turn(dk_sum[...], [t[...] for t in tabs], -1.0).astype(BF16)
        dv_all[:, cols] = dv_sum[...].astype(BF16)
    spread_out(source_ref, dq_all, outs[:chunks], span)
    spread_out(source_ref, dk_all, outs[chunks : 2 * chunks], span)
    spread_out(source_ref, dv_all, outs[2 * chunks :], span)


def attend_back(source, lengths, queries, keys, values, grads, tables):
    chunks = len(queries)
    rows = lengths.shape[0]
    tokens, columns = queries[0].shape
    span = tokens // rows
    seq = span * chunks
    spec = pl.BlockSpec((span, columns), lambda r, *_: (r, 0))
    whole = pl.BlockSpec((seq, HD), lambda r, *_: (0, 0))
    wide = pltpu.VMEM((seq, columns), BF16)
    outs = pl.pallas_call(
        partial(attend_back_kernel, chunks=chunks),
        name="attend_back",
        grid_spec=pltpu.PrefetchScalarGridSpec(
            num_scalar_prefetch=2,
            grid=(rows,),
            in_specs=[spec] * (4 * chunks) + [whole] * 3,
            out_specs=[spec] * (3 * chunks),
            scratch_shapes=[wide] * 4 + [pltpu.VMEM((seq, HD), F32)] * 2 + [wide] * 3,
        ),
        out_shape=[jax.ShapeDtypeStruct((tokens, columns), BF16)] * (3 * chunks),
        compiler_params=params(1),
    )(source, lengths, *queries, *keys, *values, *grads, *tables)
    return outs[:chunks], outs[chunks : 2 * chunks], outs[2 * chunks :]


def last_kernel(
    perm_ref,
    earlier_ref,
    coeff_ref,
    z_ref,
    mine_ref,
    theirs_ref,
    grad_ref,
    gain_ref,
    out_ref,
    mix_ref,
    dz_ref,
    acc_ref,
):
    prev = earlier_ref.shape[0]
    width = earlier_ref.shape[2]
    parts = perm_ref.shape[0]
    block = width // parts
    step = min(block, 256)

    def group(i, carry):
        rows = pl.ds(pl.multiple_of(i * GROUP, GROUP), GROUP)
        coeff = coeff_ref[rows, :]
        for s in range(STREAMS - 1):
            z = z_ref[s, rows, :]
            center = z - jnp.mean(z, axis=-1, keepdims=True)
            spread = jnp.mean(center * center, axis=-1, keepdims=True)
            inverse = lax.rsqrt(spread + EPSILON)
            hat = center * inverse
            e = (mine_ref[s, rows, :].astype(F32) + theirs_ref[s, rows, :].astype(F32)) * gain_ref[
                ...
            ]
            first = jnp.mean(e, axis=-1, keepdims=True)
            second = jnp.mean(e * hat, axis=-1, keepdims=True)
            dz_ref[s] = (e - first - hat * second) * inverse
        dz_ref[STREAMS - 1] = grad_ref[rows, :]
        acc_ref[...] = jnp.zeros_like(acc_ref)
        for p in range(parts):
            for c in range(0, block, step):
                here = slice(p * block + c, p * block + c + step)
                there = pl.ds(pl.multiple_of(perm_ref[p] * block + c, 128), step)
                grads = [dz_ref[s, :, here] for s in range(STREAMS)]
                for j in range(prev):
                    x = earlier_ref[j, rows, there].astype(F32)
                    total = None
                    for s in range(STREAMS):
                        k = s * prev + j
                        term = coeff[:, k : k + 1] * grads[s]
                        total = term if total is None else total + term
                        both = x * grads[s]
                        folded = both[:, :128]
                        for f in range(128, step, 128):
                            folded = folded + both[:, f : f + 128]
                        acc_ref[k] += folded
                    out_ref[j, rows, there] = total.astype(BF16)
        lane = lax.broadcasted_iota(jnp.int32, (GROUP, 128), 1)
        mixed = jnp.zeros((GROUP, 128), F32)
        for k in range(STREAMS * prev):
            mixed = jnp.where(lane == k, jnp.sum(acc_ref[k], axis=-1, keepdims=True), mixed)
        mix_ref[rows, :] = mixed
        return carry

    lax.fori_loop(0, earlier_ref.shape[1] // GROUP, group, 0)


def last_stage(perm, inputs, coeff, streams, mine, theirs, grad, gain, tile=64):
    prev, tokens, width = inputs.shape
    three = pl.BlockSpec((STREAMS - 1, tile, width), lambda t, *_: (0, t, 0))
    return pl.pallas_call(
        last_kernel,
        name="last",
        grid_spec=pltpu.PrefetchScalarGridSpec(
            num_scalar_prefetch=1,
            grid=(tokens // tile,),
            in_specs=[
                pl.BlockSpec((prev, tile, width), lambda t, *_: (0, t, 0)),
                pl.BlockSpec((tile, coeff.shape[1]), lambda t, *_: (t, 0)),
                three,
                three,
                three,
                pl.BlockSpec((tile, width), lambda t, *_: (t, 0)),
                pl.BlockSpec((1, width), lambda t, *_: (0, 0)),
            ],
            out_specs=[
                pl.BlockSpec((prev, tile, width), lambda t, *_: (0, t, 0)),
                pl.BlockSpec((tile, 128), lambda t, *_: (t, 0)),
            ],
            scratch_shapes=[
                pltpu.VMEM((STREAMS, GROUP, width), F32),
                pltpu.VMEM((STREAMS * prev, GROUP, 128), F32),
            ],
        ),
        out_shape=[
            jax.ShapeDtypeStruct((prev, tokens, width), BF16),
            jax.ShapeDtypeStruct((tokens, 128), F32),
        ],
        compiler_params=params(1),
    )(perm, inputs, coeff, streams, mine, theirs, grad, gain)


def layer_norm(values, gain, shift):
    center = values - jnp.mean(values, axis=-1, keepdims=True)
    spread = jnp.mean(center * center, axis=-1, keepdims=True)
    return center * lax.rsqrt(spread + EPSILON) * gain + shift


def activate(values):
    return jax.nn.gelu(values, approximate=False)


def mixer(final, weight_in, weight_out, bias):
    normed = final * lax.rsqrt(jnp.mean(final * final, axis=-1, keepdims=True) + RMS_EPSILON)
    hidden = activate(
        lax.dot_general(
            normed,
            weight_in,
            (((1,), (1,)), ((), ())),
            precision=HIGHEST,
            preferred_element_type=F32,
        )
    )
    return jnp.dot(hidden, weight_out, precision=HIGHEST, preferred_element_type=F32) + bias


def times_transposed(left, right):
    return lax.dot_general(left, right, (((1,), (1,)), ((), ())), preferred_element_type=F32)


def over_tokens(left, right):
    return lax.dot_general(left, right, (((0,), (0,)), ((), ())), preferred_element_type=F32)


def turn_tables(positions):
    half = ROT // 2
    frequency = 10000.0 ** (-2.0 * jnp.arange(half, dtype=F32) / ROT)
    angles = positions.astype(F32)[:, None] * frequency[None, :]
    cosine, sine = jnp.cos(angles), jnp.sin(angles)
    count = positions.shape[0]
    rest = HD - ROT
    base = jnp.concatenate([cosine, cosine, jnp.ones((count, rest), F32)], axis=1)
    up = jnp.concatenate([jnp.zeros((count, half), F32), sine, jnp.zeros((count, rest), F32)], 1)
    down = jnp.concatenate([-sine, jnp.zeros((count, half + rest), F32)], axis=1)
    return base, up, down


def body(
    earlier,
    mix_in,
    lengths,
    w_query,
    w_key,
    w_value,
    w_proj,
    w_up,
    w_down,
    first_gain,
    first_shift,
    second_gain,
    second_shift,
    mixer_in,
    mixer_out,
    mixer_bias,
    grad_out,
    grad_mix,
):
    count_prev, rows, span, width = earlier.shape
    tokens = rows * span
    fsdp, ctx = lax.axis_size("fsdp"), lax.axis_size("ctx")
    me, z = lax.axis_index("fsdp"), lax.axis_index("ctx")
    masks = block_masks(fsdp)
    place_of = [masks.index(m) for m in range(fsdp)]
    block = width // fsdp
    piece = block // ctx
    perm = jnp.stack([me ^ m for m in masks]).astype(jnp.int32)
    table = jnp.array(place_of, jnp.int32)
    ring = jnp.arange(ctx, dtype=jnp.int32)
    source = (z - ring + ctx) % ctx
    chunk_place = (ring - z + ctx) % ctx
    slots = z * span + jnp.arange(span, dtype=jnp.int32)
    valid = (slots[None, :] < lengths[:, None]).astype(F32).reshape(tokens)

    def relative(values):
        return jnp.concatenate(
            [
                lax.dynamic_slice_in_dim(values, perm[p] * block, block, values.ndim - 1)
                for p in range(fsdp)
            ],
            axis=-1,
        )

    def absolute(values):
        return jnp.concatenate(
            [
                lax.dynamic_slice_in_dim(values, table[a ^ me] * block, block, values.ndim - 1)
                for a in range(fsdp)
            ],
            axis=-1,
        )

    def part(values, p):
        return values[:, p * block : (p + 1) * block]

    small = jnp.concatenate(
        [mixer_in.T, first_gain[None], first_shift[None], second_gain[None], second_shift[None]], 0
    )
    small_all = lax.all_gather(small, ("fsdp", "ctx"), axis=0, tiled=False)
    small_all = small_all.transpose(1, 0, 2).reshape(small.shape[0], width)
    small_all = relative(small_all).astype(F32)
    mixer_full = small_all[:MIXW]
    gain_first, shift_first, gain_second, shift_second = [
        small_all[MIXW + n : MIXW + n + 1] for n in range(4)
    ]
    blocks_query = gather_blocks(w_query)
    blocks_key = gather_blocks(w_key)
    blocks_value = gather_blocks(w_value)
    blocks_proj = gather_blocks(w_proj.T)
    blocks_up = gather_blocks(w_up)
    blocks_down = gather_blocks(w_down.T)

    inputs = earlier.reshape(count_prev, tokens, width)
    coeff = mix_in.reshape(STREAMS * count_prev, tokens).T
    normed_in, streams = mix_streams(perm, inputs, coeff, gain_first, shift_first)

    tables_here = turn_tables(jnp.tile(slots, rows))
    tables_all = turn_tables(jnp.arange(span * ctx, dtype=jnp.int32))

    def to_heads(chunks):
        return [chunks[0]] + [shift_ctx(chunks[s], s) for s in range(1, ctx)]

    def to_slots(pieces):
        back = [pieces[0]] + [shift_ctx(pieces[s], -s) for s in range(1, ctx)]
        columns = back[0].shape[1]
        whole = jnp.zeros((tokens, columns * ctx), back[0].dtype)
        for s in range(ctx):
            whole = lax.dynamic_update_slice(whole, back[s], (0, ((z + s) % ctx) * columns))
        return whole

    queries = to_heads(
        blocks_product(chunk_place, normed_in[0], blocks_query, tables_here, True)
    )
    keys = to_heads(blocks_product(chunk_place, normed_in[1], blocks_key, tables_here, True))
    values = to_heads(blocks_product(chunk_place, normed_in[2], blocks_value, tables_here, False))
    attended = to_slots(attend(source, lengths, queries, keys, values))
    branch = tp_sum(
        jnp.concatenate([times_transposed(attended, w) for w in blocks_proj], axis=1)
    )
    residual = streams[STREAMS - 1] + branch

    normed = layer_norm(residual, gain_second, shift_second).astype(BF16)
    upward = sum(
        jnp.dot(part(normed, p), w, preferred_element_type=F32) for p, w in enumerate(blocks_up)
    )
    active = activate(upward).astype(BF16)
    downward = tp_sum(
        jnp.concatenate([times_transposed(active, w) for w in blocks_down], axis=1)
    )
    final = residual + downward
    output = absolute(final.astype(BF16)).reshape(rows, span, width)

    mix_value, mix_pull = jax.vjp(mixer, final, mixer_full, mixer_out, mixer_bias)
    mix_out = mix_value.T.reshape(MIXW, rows, span)
    mix_cotangent = (grad_mix.reshape(MIXW, tokens) * valid[None]).T
    grad_final_mix, grad_mixer_first, grad_mixer_second, grad_mixer_shift = mix_pull(mix_cotangent)
    grad_final = (
        relative(grad_out.reshape(tokens, width)).astype(F32) * valid[:, None] + grad_final_mix
    )

    grad_down_b = grad_final.astype(BF16)
    grad_active = sum(
        jnp.dot(part(grad_down_b, p), w, preferred_element_type=F32)
        for p, w in enumerate(blocks_down)
    )
    unused_up, gelu_pull = jax.vjp(activate, upward)
    grad_upward_b = gelu_pull(grad_active)[0].astype(BF16)
    grad_normed = tp_sum(
        jnp.concatenate([times_transposed(grad_upward_b, w) for w in blocks_up], axis=1)
    )
    grad_down = scatter_blocks([over_tokens(part(grad_down_b, p), active) for p in range(fsdp)]).T
    grad_up = scatter_blocks([over_tokens(part(normed, p), grad_upward_b) for p in range(fsdp)])
    unused_norm, norm_pull = jax.vjp(layer_norm, residual, gain_second, shift_second)
    grad_residual_norm, grad_gain_second, grad_shift_second = norm_pull(grad_normed)
    grad_residual = grad_final + grad_residual_norm
    grad_branch_b = grad_residual.astype(BF16)

    grad_proj = scatter_blocks(
        [over_tokens(part(grad_branch_b, p), attended) for p in range(fsdp)]
    ).T
    grad_heads = to_heads(
        blocks_product(chunk_place, grad_branch_b, blocks_proj, tables_here, False)
    )
    grad_q, grad_k, grad_v = attend_back(
        source, lengths, queries, keys, values, grad_heads, tables_all
    )
    grad_query_b, grad_key_b, grad_value_b = to_slots(grad_q), to_slots(grad_k), to_slots(grad_v)

    weight_blocks = (blocks_query, blocks_key, blocks_value)
    grads_b = (grad_query_b, grad_key_b, grad_value_b)
    mine = lax.optimization_barrier(
        jnp.stack(
            [
                jnp.concatenate([times_transposed(g, w) for w in ws], axis=1).astype(BF16)
                for g, ws in zip(grads_b, weight_blocks)
            ]
        )
    )
    theirs = over_tp(mine)
    weight_grads = [
        scatter_blocks([over_tokens(part(normed_in[s], p), grads_b[s]) for p in range(fsdp)])
        for s in range(3)
    ]

    center = streams[:3] - jnp.mean(streams[:3], axis=-1, keepdims=True)
    hats = center * lax.rsqrt(jnp.mean(center * center, axis=-1, keepdims=True) + EPSILON)
    mine_wide = mine.astype(F32)
    first_own = jnp.stack([jnp.sum(mine_wide * hats, (0, 1)), jnp.sum(mine_wide, (0, 1))])
    first_pair = first_own + over_tp(first_own)
    packed = jnp.concatenate(
        [grad_mixer_first, first_pair, grad_gain_second, grad_shift_second], axis=0
    )
    packed = packed.reshape(packed.shape[0], fsdp, ctx, piece).transpose(1, 2, 0, 3)
    for bit in reversed(bits_of(fsdp)):
        half = packed.shape[0] // 2
        packed = packed[:half] + over_fsdp(packed[half:], bit)
    packed = packed[0]
    own = lax.dynamic_index_in_dim(packed, z, 0, keepdims=False)
    for s in range(1, ctx):
        own = own + shift_ctx(
            lax.dynamic_index_in_dim(packed, (z + s) % ctx, 0, keepdims=False), s
        )
    tail = jnp.concatenate([grad_mixer_second, grad_mixer_shift[None]], axis=0)
    for bit in reversed(bits_of(fsdp)):
        tail = tail + over_fsdp(tail, bit)
    for bit in reversed(bits_of(ctx)):
        tail = tail + lax.ppermute(tail, "ctx", xor_pairs(ctx, bit))

    grad_inputs, grad_coeff = last_stage(
        perm, inputs, coeff, streams, mine, theirs, grad_residual, gain_first
    )
    grad_earlier = grad_inputs.reshape(earlier.shape)
    grad_mix_in = grad_coeff[:, : STREAMS * count_prev].T.reshape(mix_in.shape)
    return (
        output,
        mix_out,
        grad_earlier,
        grad_mix_in,
        weight_grads[0],
        weight_grads[1],
        weight_grads[2],
        grad_proj,
        grad_up,
        grad_down,
        own[MIXW],
        own[MIXW + 1],
        own[MIXW + 2],
        own[MIXW + 3],
        own[:MIXW].T,
        tail[:MIXW],
        tail[MIXW],
    )


def solution(mesh):
    placed = (
        P(None, "fsdp", "ctx", None),
        P(None, "fsdp", "ctx"),
        P("fsdp"),
        P(("fsdp", "ctx"), "tp"),
        P(("fsdp", "ctx"), "tp"),
        P(("fsdp", "ctx"), "tp"),
        P("tp", ("fsdp", "ctx")),
        P(("fsdp", "ctx"), "tp"),
        P("tp", ("fsdp", "ctx")),
        P(("fsdp", "ctx")),
        P(("fsdp", "ctx")),
        P(("fsdp", "ctx")),
        P(("fsdp", "ctx")),
        P(("fsdp", "ctx"), None),
        P(),
        P(),
        P("fsdp", "ctx", None),
        P(None, "fsdp", "ctx"),
    )
    return jax.shard_map(
        body,
        mesh=mesh,
        in_specs=placed,
        out_specs=(
            P("fsdp", "ctx", None),
            P(None, "fsdp", "ctx"),
            P(None, "fsdp", "ctx", None),
            P(None, "fsdp", "ctx"),
            P(("fsdp", "ctx"), "tp"),
            P(("fsdp", "ctx"), "tp"),
            P(("fsdp", "ctx"), "tp"),
            P("tp", ("fsdp", "ctx")),
            P(("fsdp", "ctx"), "tp"),
            P("tp", ("fsdp", "ctx")),
            P(("fsdp", "ctx")),
            P(("fsdp", "ctx")),
            P(("fsdp", "ctx")),
            P(("fsdp", "ctx")),
            P(("fsdp", "ctx"), None),
            P(),
            P(),
        ),
        check_vma=False,
    )
```

```python
from functools import partial
import math

import jax
import jax.numpy as jnp
from jax import lax
from jax.experimental import pallas as pl
from jax.experimental.pallas import tpu as pltpu
from jax.sharding import PartitionSpec as P

HD = 128
ROT = 32
STREAMS = 4
MIXW = 36
EPSILON = 1e-05
RMS_EPSILON = 1e-06
HIGHEST = lax.Precision.HIGHEST
NEGATIVE = -1e30
F32 = jnp.float32
BF16 = jnp.bfloat16
GROUP = 32
FORWARD_PACE = 3.0e7
BACKWARD_PACE = 1.5e9


def params(grid_rank):
    return pltpu.CompilerParams(
        dimension_semantics=("arbitrary",) * grid_rank, vmem_limit_bytes=56 * 1024 * 1024
    )


class Pace:
    value = FORWARD_PACE


def cost(time):
    return pl.CostEstimate(flops=int(time * Pace.value), transcendentals=0, bytes_accessed=1024)


def xor_pairs(size, mask):
    return [(i, i ^ mask) for i in range(size)]


def over_fsdp(values, mask):
    return lax.ppermute(values, "fsdp", xor_pairs(lax.axis_size("fsdp"), mask))


def over_tp(values):
    return lax.ppermute(values, "tp", xor_pairs(lax.axis_size("tp"), 1))


def shift_ctx(values, step):
    size = lax.axis_size("ctx")
    return lax.ppermute(values, "ctx", [(i, (i + step) % size) for i in range(size)])


def bits_of(size):
    return [1 << b for b in reversed(range(size.bit_length() - 1))]


def block_masks(size):
    masks = [0]
    for bit in bits_of(size):
        masks = masks + [m ^ bit for m in masks]
    return masks


def after(values, *earlier):
    return lax.optimization_barrier((values, earlier))[0]


class Order:
    def __init__(self):
        self.last = ()

    def __call__(self, values):
        return after(values, self.last)

    def keep(self, values):
        self.last = values
        return values

    def wait(self, values):
        return self.keep(self(values))


def gather_ctx(shard):
    return lax.all_gather(shard, "ctx", axis=0, tiled=True)


def cross(own):
    parts = [own]
    for bit in bits_of(lax.axis_size("fsdp"))[:-1]:
        parts = parts + [over_fsdp(p, bit) for p in parts]
    return parts


class Scatter:
    def __init__(self, order, left, rights, left_far, rights_far):
        self.order, self.left, self.far, self.rights = order, left, left_far, (rights, rights_far)
        self.count = lax.axis_size("fsdp")
        self.received = [[] for _ in range(self.count)]

    def blocks(self, chosen, first, kinds):
        near, far = self.order(self.rights)
        added = [[r for r in self.received[p] if r[2] == first] for p in chosen]
        made = grad_blocks(self.left, self.far, near, far, self.count, chosen, added, first, kinds)
        return self.order.keep(made)

    def make(self, level, first=0, kinds=None):
        half = self.count >> (level + 1)
        chosen = list(range(half, 2 * half))
        return self.blocks(chosen, first, kinds or self.left.shape[0])

    def send(self, level, made, first=0):
        half = self.count >> (level + 1)
        bit = bits_of(self.count)[::-1][level]
        got = over_fsdp(made, bit)
        for n in range(half):
            self.received[n].append((got, n, first))
        return got

    def launch(self, first=0, kinds=None, made=None):
        for level in range(1, len(bits_of(self.count))):
            if made is None:
                made = self.make(level, first, kinds)
            self.send(level, made, first)
            made = None

    def finish(self, first=0, kinds=None):
        return self.blocks([0], first, kinds or self.left.shape[0])[0]


def scatter_ctx(total):
    return lax.psum_scatter(total, "ctx", scatter_dimension=0, tiled=True).astype(F32)


def tp_sum(mine, theirs):
    return mine.astype(F32) + theirs.astype(F32)


NT = (((1,), (1,)), ((), ()))
TN = (((0,), (0,)), ((), ()))


def spread(coeff):
    count = coeff.shape[0]
    token = lax.broadcasted_iota(jnp.int32, (count, STREAMS * GROUP), 0) % GROUP
    lane = lax.broadcasted_iota(jnp.int32, (count, STREAMS * GROUP), 1)
    out = jnp.zeros((count, STREAMS * GROUP), F32)
    for s in range(STREAMS):
        out = jnp.where(lane == token + s * GROUP, coeff[:, s : s + 1], out)
    high = out.astype(BF16)
    return high, (out - high.astype(F32)).astype(BF16)


def mix_kernel(perm_ref, earlier_ref, coeff_ref, gain_ref, shift_ref, a_ref, z_ref):
    prev, tile, width = earlier_ref.shape
    parts = perm_ref.shape[0]
    block = width // parts
    for g in range(tile // GROUP):
        rows = slice(g * GROUP, (g + 1) * GROUP)
        high, low = spread(coeff_ref[g])
        for p in range(parts):
            source = pl.ds(pl.multiple_of(perm_ref[p] * block, 128), block)
            x = earlier_ref[:, rows, source].reshape(prev * GROUP, block)
            z_ref[:, rows, p * block : (p + 1) * block] = (
                lax.dot_general(high, x, TN, preferred_element_type=F32)
                + lax.dot_general(low, x, TN, preferred_element_type=F32)
            ).reshape(STREAMS, GROUP, block)
        for s in range(STREAMS - 1):
            z = z_ref[s, rows, :]
            center = z - jnp.mean(z, axis=-1, keepdims=True)
            spread_of = jnp.mean(center * center, axis=-1, keepdims=True)
            a_ref[s, rows, :] = (
                center * lax.rsqrt(spread_of + EPSILON) * gain_ref[...] + shift_ref[...]
            ).astype(BF16)


def mix_streams(perm, inputs, coeff, gain, shift, tile=64):
    prev, tokens, width = inputs.shape
    return pl.pallas_call(
        mix_kernel,
        name="mix",
        grid_spec=pltpu.PrefetchScalarGridSpec(
            num_scalar_prefetch=1,
            grid=(tokens // tile,),
            in_specs=[
                pl.BlockSpec((prev, tile, width), lambda t, *_: (0, t, 0)),
                pl.BlockSpec((tile // GROUP,) + coeff.shape[1:], lambda t, *_: (t, 0, 0)),
                pl.BlockSpec((1, width), lambda t, *_: (0, 0)),
                pl.BlockSpec((1, width), lambda t, *_: (0, 0)),
            ],
            out_specs=[
                pl.BlockSpec((STREAMS - 1, tile, width), lambda t, *_: (0, t, 0)),
                pl.BlockSpec((STREAMS, tile, width), lambda t, *_: (0, t, 0)),
            ],
        ),
        out_shape=[
            jax.ShapeDtypeStruct((STREAMS - 1, tokens, width), BF16),
            jax.ShapeDtypeStruct((STREAMS, tokens, width), F32),
        ],
        cost_estimate=cost(14),
        compiler_params=params(1),
    )(perm, inputs, coeff, gain, shift)


def turn(values, tables, sign):
    base, up, down = tables
    return (
        values * base
        + sign * (pltpu.roll(values, ROT // 2, 1) * up)
        + sign * (pltpu.roll(values, HD - ROT // 2, 1) * down)
    )


def blocks_dot(a_ref, weights):
    parts = len(weights)
    block = a_ref.shape[-1] // parts
    total = None
    for p in range(parts):
        term = jnp.dot(
            a_ref[:, p * block : (p + 1) * block], weights[p][...], preferred_element_type=F32
        )
        total = term if total is None else total + term
    return total


def block_specs(weights, rows, columns, at):
    return [pl.BlockSpec((rows, columns), lambda *ids: (0, at(*ids)))] * len(weights)


def heads_kernel(target_ref, perm_ref, a_ref, *refs, parts, turned):
    weights = refs[:parts]
    tables = refs[parts : parts + 3]
    outs = refs[parts + 3 :]
    total = blocks_dot(a_ref.at[0], weights)
    kind, step = pl.program_id(0), pl.program_id(1)
    for s, out_ref in enumerate(outs):

        @pl.when((step == s) & (kind < turned))
        def _():
            tabs = [t[...] for t in tables]
            for h in range(total.shape[1] // HD):
                cols = slice(h * HD, (h + 1) * HD)
                out_ref[0, :, cols] = turn(total[:, cols], tabs, 1.0).astype(BF16)

        @pl.when((step == s) & (kind >= turned))
        def _():
            out_ref[0] = total.astype(BF16)


def to_chunks(target, perm, a, weights, tables, turned):
    kinds, tokens, width = a.shape
    parts = perm.shape[0]
    chunks = target.shape[0]
    columns = weights[0].shape[1] // chunks // kinds
    specs = block_specs(
        weights, width // parts, columns, lambda s, n, target, _: s * chunks + target[n]
    )
    return pl.pallas_call(
        partial(heads_kernel, parts=parts, turned=turned),
        name="heads",
        grid_spec=pltpu.PrefetchScalarGridSpec(
            num_scalar_prefetch=2,
            grid=(kinds, chunks),
            in_specs=[pl.BlockSpec((1, tokens, width), lambda s, n, *_: (s, 0, 0))]
            + specs
            + [pl.BlockSpec((tokens, HD), lambda s, n, *_: (0, 0))] * 3,
            out_specs=[pl.BlockSpec((1, tokens, columns), lambda s, n, *_: (s, 0, 0))] * chunks,
        ),
        out_shape=[jax.ShapeDtypeStruct((kinds, tokens, columns), BF16)] * chunks,
        cost_estimate=cost(2 * kinds * chunks),
        compiler_params=params(2),
    )(target, perm, a, *weights, *tables)


def join_kernel(target_ref, *refs):
    for s in range(len(refs) - 1):

        @pl.when(pl.program_id(0) == s)
        def _():
            refs[-1][...] = refs[s][...]


def join(target, pieces):
    kinds, count, columns = pieces[0].shape
    chunks = len(pieces)
    return pl.pallas_call(
        join_kernel,
        name="join",
        grid_spec=pltpu.PrefetchScalarGridSpec(
            num_scalar_prefetch=1,
            grid=(chunks,),
            in_specs=[pl.BlockSpec((kinds, count, columns), lambda n, _: (0, 0, 0))] * chunks,
            out_specs=pl.BlockSpec((kinds, count, columns), lambda n, target: (0, 0, target[n])),
        ),
        out_shape=jax.ShapeDtypeStruct((kinds, count, columns * chunks), BF16),
        cost_estimate=cost(2),
        compiler_params=params(1),
    )(target, *pieces)


def weights_of(query, keys, tile_index, tile, length, scale):
    count = keys.shape[0]
    scores = (
        lax.dot_general(query, keys, (((1,), (1,)), ((), ())), preferred_element_type=F32) * scale
    )
    row = tile_index * tile + lax.broadcasted_iota(jnp.int32, (tile, count), 0)
    col = lax.broadcasted_iota(jnp.int32, (tile, count), 1)
    masked = jnp.where((col <= row) & (col < length), scores, NEGATIVE)
    expo = jnp.exp(masked - jnp.max(masked, axis=-1, keepdims=True))
    return expo / jnp.sum(expo, axis=-1, keepdims=True)


def collect(source_ref, pieces, scratch, span):
    for s, piece in enumerate(pieces):
        at = pl.ds(pl.multiple_of(source_ref[s] * span, span), span)
        scratch[at, :] = piece[...]


def spread_out(source_ref, scratch, pieces, span):
    for s, piece in enumerate(pieces):
        at = pl.ds(pl.multiple_of(source_ref[s] * span, span), span)
        piece[...] = scratch[at, :]


def collect(source_ref, pieces, kind, scratch):
    span = pieces[0].shape[1]
    for s, piece in enumerate(pieces):
        at = pl.ds(pl.multiple_of(source_ref[s] * span, span), span)
        scratch[at, :] = piece[kind]


def spread_out(source_ref, scratch, pieces, kind):
    span = pieces[0].shape[1]
    for s, piece in enumerate(pieces):
        at = pl.ds(pl.multiple_of(source_ref[s] * span, span), span)
        piece[kind] = scratch[at, :]


def attend_kernel(source_ref, length_ref, *refs, chunks):
    ins, outs = refs[:chunks], refs[chunks : 2 * chunks]
    q_all, k_all, v_all, o_all = refs[2 * chunks :]
    span = ins[0].shape[1]
    length = length_ref[pl.program_id(0)]
    scale = 1.0 / math.sqrt(HD)
    for kind, scratch in enumerate((q_all, k_all, v_all)):
        collect(source_ref, ins, kind, scratch)
    for h in range(q_all.shape[1] // HD):
        cols = slice(h * HD, (h + 1) * HD)
        for i in range(chunks):
            rows = slice(i * span, (i + 1) * span)
            seen = slice(0, (i + 1) * span)
            probs = weights_of(q_all[rows, cols], k_all[seen, cols], i, span, length, scale)
            o_all[rows, cols] = jnp.dot(
                probs.astype(BF16), v_all[seen, cols], preferred_element_type=F32
            ).astype(BF16)
    spread_out(source_ref, o_all, outs, 0)


def attend(source, lengths, pieces):
    chunks = len(pieces)
    rows = lengths.shape[0]
    kinds, tokens, columns = pieces[0].shape
    span = tokens // rows
    return pl.pallas_call(
        partial(attend_kernel, chunks=chunks),
        name="attend",
        grid_spec=pltpu.PrefetchScalarGridSpec(
            num_scalar_prefetch=2,
            grid=(rows,),
            in_specs=[pl.BlockSpec((kinds, span, columns), lambda r, *_: (0, r, 0))] * chunks,
            out_specs=[pl.BlockSpec((1, span, columns), lambda r, *_: (0, r, 0))] * chunks,
            scratch_shapes=[pltpu.VMEM((span * chunks, columns), BF16)] * 4,
        ),
        out_shape=[jax.ShapeDtypeStruct((1, tokens, columns), BF16)] * chunks,
        cost_estimate=cost(6 * rows),
        compiler_params=params(1),
    )(source, lengths, *pieces)


def attend_back_kernel(source_ref, length_ref, *refs, chunks, row):
    ins, grads = refs[:chunks], refs[chunks : 2 * chunks]
    tabs = refs[2 * chunks : 2 * chunks + 3]
    outs = refs[2 * chunks + 3 : 3 * chunks + 3]
    q_all, k_all, v_all, g_all, dk_sum, dv_sum, dq_all, dk_all, dv_all = refs[3 * chunks + 3 :]
    span = ins[0].shape[1]
    length = length_ref[row]
    scale = 1.0 / math.sqrt(HD)
    for kind, scratch in enumerate((q_all, k_all, v_all)):
        collect(source_ref, ins, kind, scratch)
    collect(source_ref, grads, 0, g_all)
    for h in range(q_all.shape[1] // HD):
        cols = slice(h * HD, (h + 1) * HD)
        for i in reversed(range(chunks)):
            rows = slice(i * span, (i + 1) * span)
            seen = slice(0, (i + 1) * span)
            query, grad = q_all[rows, cols], g_all[rows, cols]
            keys, values = k_all[seen, cols], v_all[seen, cols]
            probs = weights_of(query, keys, i, span, length, scale)
            grad_probs = lax.dot_general(grad, values, NT, preferred_element_type=F32)
            delta = jnp.sum(probs * grad_probs, axis=-1, keepdims=True)
            scores = (probs * (grad_probs - delta) * scale).astype(BF16)
            turned = [t[rows, :] for t in tabs]
            dq_all[rows, cols] = turn(
                jnp.dot(scores, keys, preferred_element_type=F32), turned, -1.0
            ).astype(BF16)
            dk = lax.dot_general(scores, query, TN, preferred_element_type=F32)
            dv = lax.dot_general(probs.astype(BF16), grad, TN, preferred_element_type=F32)
            if i == chunks - 1:
                dk_sum[...] = dk
                dv_sum[...] = dv
            else:
                dk_sum[seen, :] += dk
                dv_sum[seen, :] += dv
        dk_all[:, cols] = turn(dk_sum[...], [t[...] for t in tabs], -1.0).astype(BF16)
        dv_all[:, cols] = dv_sum[...].astype(BF16)
    for kind, scratch in enumerate((dq_all, dk_all, dv_all)):
        spread_out(source_ref, scratch, outs, kind)


def attend_back(source, lengths, pieces, grads, tables, row):
    chunks = len(pieces)
    rows = lengths.shape[0]
    kinds, tokens, columns = pieces[0].shape
    span = tokens // rows
    seq = span * chunks
    wide = pltpu.VMEM((seq, columns), BF16)
    return pl.pallas_call(
        partial(attend_back_kernel, chunks=chunks, row=row),
        name="attend_back",
        grid_spec=pltpu.PrefetchScalarGridSpec(
            num_scalar_prefetch=2,
            grid=(1,),
            in_specs=[pl.BlockSpec((kinds, span, columns), lambda r, *_: (0, row, 0))] * chunks
            + [pl.BlockSpec((1, span, columns), lambda r, *_: (0, row, 0))] * chunks
            + [pl.BlockSpec((seq, HD), lambda r, *_: (0, 0))] * 3,
            out_specs=[pl.BlockSpec((kinds, span, columns), lambda r, *_: (0, 0, 0))] * chunks,
            scratch_shapes=[wide] * 4 + [pltpu.VMEM((seq, HD), F32)] * 2 + [wide] * 3,
        ),
        out_shape=[jax.ShapeDtypeStruct((kinds, span, columns), BF16)] * chunks,
        cost_estimate=cost(12),
        compiler_params=params(1),
    )(source, lengths, *pieces, *grads, *tables)


def up_kernel(perm_ref, a_ref, *refs, parts):
    weights = refs[:parts]
    active_ref, slope_ref = refs[parts:]
    u = blocks_dot(a_ref, weights)
    half = 0.5 * (1.0 + lax.erf(u * math.sqrt(0.5)))
    active_ref[...] = (u * half).astype(BF16)
    slope_ref[...] = half + u * jnp.exp(-0.5 * u * u) * (1.0 / math.sqrt(2.0 * math.pi))


def up_stage(perm, a, weights, tile=512):
    tokens, width = a.shape
    parts = perm.shape[0]
    columns = weights[0].shape[1]
    tile = min(tile, columns)
    specs = block_specs(weights, width // parts, tile, lambda n, *_: n)
    out = pl.BlockSpec((tokens, tile), lambda n, *_: (0, n))
    return pl.pallas_call(
        partial(up_kernel, parts=parts),
        name="up",
        grid_spec=pltpu.PrefetchScalarGridSpec(
            num_scalar_prefetch=1,
            grid=(columns // tile,),
            in_specs=[pl.BlockSpec((tokens, width), lambda n, *_: (0, 0))] + specs,
            out_specs=[out, out],
        ),
        out_shape=[
            jax.ShapeDtypeStruct((tokens, columns), BF16),
            jax.ShapeDtypeStruct((tokens, columns), F32),
        ],
        cost_estimate=cost(columns / 200),
        compiler_params=params(1),
    )(perm, a, *weights)


def up_back_kernel(perm_ref, a_ref, slope_ref, *refs, parts):
    weights = refs[:parts]
    refs[parts][...] = (blocks_dot(a_ref, weights) * slope_ref[...]).astype(BF16)


def up_back(perm, a, slope, weights, offset, tile=512):
    tokens, width = a.shape
    parts = perm.shape[0]
    columns = slope.shape[1]
    tile = min(tile, columns)
    specs = block_specs(
        weights, width // parts, tile, lambda n, *_: offset // tile + n
    )
    out = pl.BlockSpec((tokens, tile), lambda n, *_: (0, n))
    return pl.pallas_call(
        partial(up_back_kernel, parts=parts),
        name="up_back",
        grid_spec=pltpu.PrefetchScalarGridSpec(
            num_scalar_prefetch=1,
            grid=(columns // tile,),
            in_specs=[pl.BlockSpec((tokens, width), lambda n, *_: (0, 0)), out] + specs,
            out_specs=out,
        ),
        out_shape=jax.ShapeDtypeStruct((tokens, columns), BF16),
        cost_estimate=cost(columns / 200),
        compiler_params=params(1),
    )(perm, a, slope, *weights)


def back_kernel(*refs, lefts, parts, adds):
    out_ref = refs[-1]
    block = out_ref.shape[1] // parts
    tile = refs[lefts].shape[0]
    n = pl.program_id(0)
    for p in range(parts):
        at = pl.ds(pl.multiple_of(p * block + n * tile, 128), tile)
        total = refs[-2][:, at] if adds else None
        for h in range(lefts):
            term = lax.dot_general(
                refs[h][...], refs[lefts + h * parts + p][...], NT, preferred_element_type=F32
            )
            total = term if total is None else total + term
        out_ref[:, at] = total.astype(out_ref.dtype)


def to_width(lefts, weights, width, added=(), dtype=BF16):
    parts = len(weights[0])
    block = width // parts
    tile = min(block, 256)
    tokens = lefts[0].shape[0]
    left_specs, specs, arrays = [], [], []
    for left, weight in zip(lefts, weights):
        columns = left.shape[1]
        left_specs.append(pl.BlockSpec((tokens, columns), lambda n: (0, 0)))
        specs += [pl.BlockSpec((tile, columns), lambda n: (n, 0))] * parts
        arrays += weight
    whole = pl.BlockSpec((tokens, width), lambda n: (0, 0))
    return pl.pallas_call(
        partial(back_kernel, lefts=len(lefts), parts=parts, adds=len(added)),
        name="to_width",
        grid=(block // tile,),
        in_specs=left_specs + specs + [whole] * len(added),
        out_specs=whole,
        out_shape=jax.ShapeDtypeStruct((tokens, width), dtype),
        cost_estimate=cost(sum(a.shape[1] for a in lefts) / 256),
        compiler_params=params(1),
    )(*lefts, *arrays, *added)


def grad_kernel(*refs, count, rights, adds):
    lefts, fars = refs[:count], refs[count : 2 * count]
    sides = refs[2 * count : 2 * count + rights], refs[2 * count + rights : 2 * count + 2 * rights]
    add_refs, out_ref = refs[2 * count + 2 * rights : -1], refs[-1]
    at = 0
    for b in range(count):
        total = None
        for left, right_refs in zip((lefts[b], fars[b]), sides):
            start = 0
            for right in right_refs:
                size = right.shape[1]
                term = lax.dot_general(
                    left[0, start : start + size, :], right[0], TN, preferred_element_type=F32
                )
                total = term if total is None else total + term
                start += size
        for n in range(adds[b]):
            total = total + add_refs[at + n][0].astype(F32)
        at += adds[b]
        out_ref[b] = total.astype(BF16)


def grad_blocks(left, left_far, near, far, parts, chosen, added, first, kinds, tile=512):
    _, tokens, width = left.shape
    columns = near[0].shape[2]
    tile = min(tile, columns)
    steps = columns // tile
    block = width // parts

    def place(start, row):
        return lambda s, n: (row, 0, (first - start + s) * steps + n)

    flat = [a for arrays in added for a in arrays]
    left_specs = [
        pl.BlockSpec((1, tokens, block), lambda s, n, p=p: (first + s, 0, p)) for p in chosen
    ]
    return pl.pallas_call(
        partial(
            grad_kernel,
            count=len(chosen),
            rights=len(near),
            adds=tuple(len(a) for a in added),
        ),
        name="grad",
        grid=(kinds, steps),
        in_specs=left_specs * 2
        + [
            pl.BlockSpec((1, r.shape[1], tile), lambda s, n: (first + s, 0, n))
            for r in (*near, *far)
        ]
        + [pl.BlockSpec((1, block, tile), place(start, row)) for _, row, start in flat],
        out_specs=pl.BlockSpec((len(chosen), block, tile), lambda s, n: (0, 0, s * steps + n)),
        out_shape=jax.ShapeDtypeStruct((len(chosen), block, kinds * columns), BF16),
        cost_estimate=cost(len(chosen) * kinds * columns / 512),
        compiler_params=params(2),
    )(*[left] * len(chosen), *[left_far] * len(chosen), *near, *far, *[a for a, _, _ in flat])


def part_kernel(in_ref, out_ref, *, turned):
    values = in_ref[...]
    out_ref[...] = values.astype(F32).T.astype(BF16) if turned else values


def shard_part(shard, n, size, turned):
    short = shard.shape[1] if turned else shard.shape[0]
    spec = pl.BlockSpec((size, short), lambda i: (n, 0))
    if not turned:
        spec = pl.BlockSpec((short, size), lambda i: (0, n))
    return pl.pallas_call(
        partial(part_kernel, turned=turned),
        name="part",
        grid=(1,),
        in_specs=[spec],
        out_specs=pl.BlockSpec((short, size), lambda i: (0, 0)),
        out_shape=jax.ShapeDtypeStruct((short, size), BF16),
        cost_estimate=cost(1),
        compiler_params=params(1),
    )(shard)


def hat_of(z):
    center = z - jnp.mean(z, axis=-1, keepdims=True)
    inverse = lax.rsqrt(jnp.mean(center * center, axis=-1, keepdims=True) + EPSILON)
    return center * inverse, inverse


def own_kernel(perm_ref, grad_ref, z_ref, *refs, parts):
    weights = refs[:parts]
    out_ref, sum_ref = refs[parts:]
    block = weights[0].shape[0]
    for p in range(parts):
        out_ref[0, :, p * block : (p + 1) * block] = lax.dot_general(
            grad_ref[0], weights[p][...], NT, preferred_element_type=F32
        )
    tile = 32
    tokens, width = out_ref.shape[1:]
    gain = jnp.zeros((8, width), F32)
    shift = jnp.zeros((8, width), F32)
    for t in range(0, tokens, tile):
        d = out_ref[0, t : t + tile, :]
        hat, _ = hat_of(z_ref[0, t : t + tile, :])
        gain = gain + jnp.sum((d * hat).reshape(tile // 8, 8, width), axis=0)
        shift = shift + jnp.sum(d.reshape(tile // 8, 8, width), axis=0)
    sum_ref[0, :8] = gain
    sum_ref[0, 8:] = shift


def own_part(perm, grads, streams, weights, row):
    kinds, span, columns = grads.shape
    width = streams.shape[2]
    parts = perm.shape[0]
    specs = block_specs(weights, width // parts, columns, lambda s, *_: s)
    return pl.pallas_call(
        partial(own_kernel, parts=parts),
        name="own",
        grid_spec=pltpu.PrefetchScalarGridSpec(
            num_scalar_prefetch=1,
            grid=(kinds,),
            in_specs=[
                pl.BlockSpec((1, span, columns), lambda s, *_: (s, 0, 0)),
                pl.BlockSpec((1, span, width), lambda s, *_: (s, row, 0)),
            ]
            + specs,
            out_specs=[
                pl.BlockSpec((1, span, width), lambda s, *_: (s, 0, 0)),
                pl.BlockSpec((1, 16, width), lambda s, *_: (s, 0, 0)),
            ],
        ),
        out_shape=[
            jax.ShapeDtypeStruct((kinds, span, width), F32),
            jax.ShapeDtypeStruct((kinds, 16, width), F32),
        ],
        cost_estimate=cost(12),
        compiler_params=params(1),
    )(perm, grads, streams, *weights)


def other_kernel(grad_ref, part_ref, z_ref, gain_ref, *refs, parts):
    weights = refs[:parts]
    out_ref, total_ref = refs[parts:]
    block = weights[0].shape[0]
    for p in range(parts):
        cols = slice(p * block, (p + 1) * block)
        total_ref[:, cols] = part_ref[0, :, cols] + lax.dot_general(
            grad_ref[0], weights[p][...], NT, preferred_element_type=F32
        )
    tile = 32
    for t in range(0, total_ref.shape[0], tile):
        rows = slice(t, t + tile)
        hat, inverse = hat_of(z_ref[0, rows, :])
        e = total_ref[rows, :] * gain_ref[...]
        first = jnp.mean(e, axis=-1, keepdims=True)
        second = jnp.mean(e * hat, axis=-1, keepdims=True)
        out_ref[0, rows, :] = ((e - first - hat * second) * inverse).astype(BF16)


def other_part(grads, own, streams, gain, weights, row):
    kinds, span, columns = grads.shape
    width = streams.shape[2]
    parts = len(weights)
    block = width // parts
    return pl.pallas_call(
        partial(other_kernel, parts=parts),
        name="other",
        grid=(kinds,),
        in_specs=[
            pl.BlockSpec((1, span, columns), lambda s: (s, 0, 0)),
            pl.BlockSpec((1, span, width), lambda s: (s, 0, 0)),
            pl.BlockSpec((1, span, width), lambda s: (s, row, 0)),
            pl.BlockSpec((1, width), lambda s: (0, 0)),
        ]
        + [pl.BlockSpec((block, columns), lambda s: (0, s))] * parts,
        out_specs=pl.BlockSpec((1, span, width), lambda s: (s, 0, 0)),
        out_shape=jax.ShapeDtypeStruct((kinds, span, width), BF16),
        scratch_shapes=[pltpu.VMEM((span, width), F32)],
        cost_estimate=cost(14),
        compiler_params=params(1),
    )(grads, own, streams, gain, *weights)


def last_kernel(perm_ref, earlier_ref, coeff_ref, dz_ref, dr_ref, *refs):
    out_ref, mix_ref = refs[-2:]
    prev, tile, width = earlier_ref.shape
    parts = perm_ref.shape[0]
    block = width // parts
    count, half = prev * GROUP, STREAMS * GROUP
    for g in range(tile // GROUP):
        rows = slice(g * GROUP, (g + 1) * GROUP)
        high, low = spread(coeff_ref[g])
        pairs = jnp.zeros((count, half), F32)
        for p in range(parts):
            here = slice(p * block, (p + 1) * block)
            there = pl.ds(pl.multiple_of(perm_ref[p] * block, 128), block)
            grads = jnp.concatenate(
                [dz_ref[s, rows, here] for s in range(STREAMS - 1)] + [dr_ref[rows, here]], axis=0
            )
            x = earlier_ref[:, rows, there].reshape(count, block)
            pairs = pairs + lax.dot_general(x, grads, NT, preferred_element_type=F32)
            total = jnp.dot(high, grads, preferred_element_type=F32) + jnp.dot(
                low, grads, preferred_element_type=F32
            )
            out_ref[:, rows, there] = total.astype(BF16).reshape(prev, GROUP, block)
        token = lax.broadcasted_iota(jnp.int32, (count, half), 0) % GROUP
        lane = lax.broadcasted_iota(jnp.int32, (count, half), 1)
        wide = lax.broadcasted_iota(jnp.int32, (count, 128), 1)
        mixed = jnp.zeros((count, 128), F32)
        for s in range(STREAMS):
            own = jnp.where(lane == token + s * GROUP, pairs, 0.0)
            mixed = jnp.where(wide == s, jnp.sum(own, axis=-1, keepdims=True), mixed)
        mix_ref[g] = mixed


def last_stage(perm, inputs, coeff, dz, dr, row, rows, before, tile=64):
    prev, tokens, width = inputs.shape
    steps = tokens // rows // tile
    count = prev * GROUP
    here = lambda t, *_: (0, row * steps + t, 0)
    return pl.pallas_call(
        last_kernel,
        name="last",
        grid_spec=pltpu.PrefetchScalarGridSpec(
            num_scalar_prefetch=1,
            grid=(steps,),
            in_specs=[
                pl.BlockSpec((prev, tile, width), here),
                pl.BlockSpec(
                    (tile // GROUP,) + coeff.shape[1:], lambda t, *_: (row * steps + t, 0, 0)
                ),
                pl.BlockSpec((STREAMS - 1, tile, width), lambda t, *_: (0, t, 0)),
                pl.BlockSpec((tile, width), lambda t, *_: (row * steps + t, 0)),
            ]
            + [pl.BlockSpec(memory_space=pl.ANY)] * len(before),
            out_specs=[
                pl.BlockSpec((prev, tile, width), here),
                pl.BlockSpec(
                    (tile // GROUP, count, 128), lambda t, *_: (row * steps + t, 0, 0)
                ),
            ],
        ),
        out_shape=[
            jax.ShapeDtypeStruct((prev, tokens, width), BF16),
            jax.ShapeDtypeStruct((tokens // GROUP, count, 128), F32),
        ],
        input_output_aliases={5 + n: n for n in range(len(before))},
        cost_estimate=cost(12),
        compiler_params=params(1),
    )(perm, inputs, coeff, dz, dr, *before)


def layer_norm(values, gain, shift):
    center = values - jnp.mean(values, axis=-1, keepdims=True)
    spread = jnp.mean(center * center, axis=-1, keepdims=True)
    return center * lax.rsqrt(spread + EPSILON) * gain + shift


def activate(values):
    return jax.nn.gelu(values, approximate=False)


def mixer(final, weight_in, weight_out, bias):
    normed = final * lax.rsqrt(jnp.mean(final * final, axis=-1, keepdims=True) + RMS_EPSILON)
    hidden = activate(
        lax.dot_general(
            normed, weight_in, NT, precision=HIGHEST, preferred_element_type=F32
        )
    )
    return jnp.dot(hidden, weight_out, precision=HIGHEST, preferred_element_type=F32) + bias


def turn_tables(positions):
    half = ROT // 2
    frequency = 10000.0 ** (-2.0 * jnp.arange(half, dtype=F32) / ROT)
    angles = positions.astype(F32)[:, None] * frequency[None, :]
    cosine, sine = jnp.cos(angles), jnp.sin(angles)
    count = positions.shape[0]
    rest = HD - ROT
    base = jnp.concatenate([cosine, cosine, jnp.ones((count, rest), F32)], axis=1)
    up = jnp.concatenate([jnp.zeros((count, half), F32), sine, jnp.zeros((count, rest), F32)], 1)
    down = jnp.concatenate([-sine, jnp.zeros((count, half + rest), F32)], axis=1)
    return base, up, down


def group_coeff(mix_in, count_prev, tokens):
    groups = tokens // GROUP
    c = mix_in.reshape(STREAMS, count_prev, groups, GROUP).transpose(2, 1, 3, 0)
    return c.reshape(groups, count_prev * GROUP, STREAMS)


def body(
    earlier,
    mix_in,
    lengths,
    w_query,
    w_key,
    w_value,
    w_proj,
    w_up,
    w_down,
    first_gain,
    first_shift,
    second_gain,
    second_shift,
    mixer_in,
    mixer_out,
    mixer_bias,
    grad_out,
    grad_mix,
):
    count_prev, rows, span, width = earlier.shape
    tokens = rows * span
    fsdp, ctx = lax.axis_size("fsdp"), lax.axis_size("ctx")
    me, z = lax.axis_index("fsdp"), lax.axis_index("ctx")
    masks = block_masks(fsdp)
    place_of = [masks.index(m) for m in range(fsdp)]
    block = width // fsdp
    piece = block // ctx
    heads_width = w_query.shape[1]
    hidden = w_up.shape[1]
    perm = jnp.stack([me ^ m for m in masks]).astype(jnp.int32)
    table = jnp.array(place_of, jnp.int32)
    ring = jnp.arange(ctx, dtype=jnp.int32)
    source = (z - ring + ctx) % ctx
    slots = z * span + jnp.arange(span, dtype=jnp.int32)
    valid = (slots[None, :] < lengths[:, None]).astype(F32).reshape(tokens)

    def relative(values):
        return jnp.concatenate(
            [
                lax.dynamic_slice_in_dim(values, perm[p] * block, block, values.ndim - 1)
                for p in range(fsdp)
            ],
            axis=-1,
        )

    def absolute(values):
        return jnp.concatenate(
            [
                lax.dynamic_slice_in_dim(values, table[a ^ me] * block, block, values.ndim - 1)
                for a in range(fsdp)
            ],
            axis=-1,
        )

    def part(values, p):
        return values[:, p * block : (p + 1) * block]

    small = jnp.concatenate(
        [mixer_in.T, first_gain[None], first_shift[None], second_gain[None], second_shift[None]], 0
    )
    around = jnp.zeros((ctx,) + small.shape, BF16)
    for s in range(ctx):
        got = small if s == 0 else shift_ctx(small, s)
        around = lax.dynamic_update_slice(around, got[None], (source[s], 0, 0))
    around = cross(around)
    around = jnp.stack(around + [over_fsdp(a, 1) for a in around])
    small_all = around.transpose(2, 0, 1, 3).reshape(small.shape[0], width).astype(F32)
    mixer_full = small_all[:MIXW]
    gain_first, shift_first, gain_second, shift_second = [
        small_all[MIXW + n : MIXW + n + 1] for n in range(4)
    ]

    half = hidden // 2
    ctx_qkv = gather_ctx(jnp.concatenate([w_query, w_key, w_value], axis=1))
    ctx_up = [gather_ctx(shard_part(w_up, 0, half, False))]

    order = Order()
    Pace.value = FORWARD_PACE
    inputs = earlier.reshape(count_prev, tokens, width)
    coeff = group_coeff(mix_in, count_prev, tokens)
    normed_in, streams = order.keep(
        mix_streams(perm, inputs, coeff, gain_first, shift_first)
    )
    tables_here = turn_tables(jnp.tile(slots, rows))
    tables_all = turn_tables(jnp.arange(span * ctx, dtype=jnp.int32))
    target = (z + ring) % ctx
    tables_here, tables_all = order.wait((tables_here, tables_all))

    def to_heads(chunks):
        return [chunks[0]] + [shift_ctx(chunks[s], s) for s in range(1, ctx)]

    def to_slots(pieces):
        return [pieces[0]] + [shift_ctx(pieces[s], -s) for s in range(1, ctx)]

    def to_core(parts):
        return [over_fsdp(p, 1) for p in parts]

    near_qkv = cross(order.wait(ctx_qkv))
    ctx_up.append(gather_ctx(order.keep(shard_part(order(w_up), 1, half, False))))
    far_qkv = to_core(near_qkv[:1])
    other = [over_tp(near_qkv[0])]
    near_up = [cross(order.wait(ctx_up[0]))]
    ctx_proj = gather_ctx(order.keep(shard_part(order(w_proj), 0, heads_width, True)))
    far_qkv = order.wait(far_qkv)
    other = order.wait(other)
    near_qkv = order.wait(near_qkv)
    far_qkv = order.wait(far_qkv + to_core(near_qkv[1:]))
    blocks_qkv = near_qkv + far_qkv
    pieces = to_heads(
        order.keep(to_chunks(target, perm, order(normed_in), blocks_qkv, tables_here, 2))
    )
    near_up.append(cross(order.wait(ctx_up[1])))
    ctx_down = [gather_ctx(order.keep(shard_part(order(w_down), 0, half, True)))]
    pieces = order.wait(pieces)
    near_up = order.wait(near_up)
    far_up = [to_core(order(near)) for near in near_up]
    near_proj = cross(order.wait(ctx_proj))
    outs = order.keep(attend(source, lengths, order(pieces)))
    far_up = order.wait(far_up)
    outs = to_slots(order(outs))
    ctx_down.append(gather_ctx(order.keep(shard_part(order(w_down), 1, half, True))))
    outs = order.wait(outs)
    attended = order.keep(join(target, order(outs)))[0]
    near_proj = order.wait(near_proj)
    blocks_proj = near_proj + order.wait(to_core(near_proj))
    branch_mine = order.keep(to_width([order(attended)], [blocks_proj], width))
    branch_theirs = over_tp(branch_mine)
    near_down = [cross(order.wait(ctx_down[0]))]
    branch_theirs = order.wait(branch_theirs)
    blocks_up = [near + far for near, far in zip(near_up, far_up)]
    residual = streams[STREAMS - 1] + tp_sum(branch_mine, branch_theirs)

    def far_half(values):
        return over_fsdp(values[..., width // 2 :], 1)

    normed = layer_norm(residual, gain_second, shift_second).astype(BF16)
    normed = order.wait(normed)
    near_down.append(cross(order.wait(ctx_down[1])))
    near_down[0] = order.wait(near_down[0])
    far_down = [to_core(near_down[0])]
    active, slope = [], []
    for w in blocks_up:
        a, b = order.keep(up_stage(perm, order(normed), w))
        active.append(a)
        slope.append(b)
    other = other + [over_tp(p) for p in order(near_qkv[1:])]
    far_down[0] = order.wait(far_down[0])
    down_first = order.keep(
        to_width([order(active[0])], [near_down[0] + far_down[0]], width, (), F32)
    )
    near_down[1] = order.wait(near_down[1])
    far_down.append(order.wait(to_core(near_down[1])))
    blocks_down = [near + far for near, far in zip(near_down, far_down)]
    other = order.wait(other)
    down_mine = order.keep(
        to_width([order(active[1])], blocks_down[1:], width, (down_first,))
    )
    other_far = to_core(other)
    down_theirs = over_tp(down_mine)
    active_far = [over_fsdp(a, 1) for a in order(active)]
    grad_out_here = order.wait(relative(grad_out.reshape(tokens, width)))
    active_far = order.wait(active_far)
    normed_far = order.wait(far_half(normed))
    attended_far = order.wait(over_fsdp(attended, 1))
    normed_in_far = order.wait(far_half(normed_in))
    other = other + order.wait(other_far)
    final = residual + tp_sum(down_mine, order.wait(down_theirs))
    output = absolute(final.astype(BF16)).reshape(rows, span, width)

    mix_value, mix_pull = jax.vjp(mixer, final, mixer_full, mixer_out, mixer_bias)
    mix_out = mix_value.T.reshape(MIXW, rows, span)
    mix_cotangent = (grad_mix.reshape(MIXW, tokens) * valid[None]).T
    grad_final_mix, grad_mixer_first, grad_mixer_second, grad_mixer_shift = mix_pull(mix_cotangent)
    grad_final = grad_out_here.astype(F32) * valid[:, None] + grad_final_mix

    Pace.value = BACKWARD_PACE
    grad_down_b = order.wait(grad_final.astype(BF16))
    grad_down_far = order.wait(far_half(grad_down_b))
    down = [
        Scatter(order, grad_down_b[None], [a[None]], grad_down_far[None], [f[None]])
        for a, f in zip(active, active_far)
    ]
    for d in down:
        d.launch()
    grad_upward, upward_far = [], []
    for n in range(2):
        grad_upward.append(
            order.keep(up_back(perm, order(grad_down_b), slope[n], blocks_down[n], 0))
        )
        upward_far.append(over_fsdp(grad_upward[n], 1))
    normed_mine = order.keep(to_width(order(grad_upward), blocks_up, width))
    normed_theirs = over_tp(normed_mine)
    grad_down = [scatter_ctx(down[0].finish())]
    upward_far = order.wait(upward_far)
    up = [
        Scatter(order, normed[None], [u[None]], normed_far[None], [f[None]])
        for u, f in zip(grad_upward, upward_far)
    ]
    up[0].launch()
    tail = jnp.concatenate([grad_mixer_second, grad_mixer_shift[None]], axis=0)
    tail, grad_mixer_first, output, mix_out = order.wait(
        (tail, grad_mixer_first, output, mix_out)
    )
    normed_theirs = order.wait(normed_theirs)
    grad_normed = tp_sum(normed_mine, normed_theirs)
    unused_norm, norm_pull = jax.vjp(layer_norm, residual, gain_second, shift_second)
    grad_residual_norm, grad_gain_second, grad_shift_second = norm_pull(grad_normed)
    grad_branch_b = order.wait((grad_final + grad_residual_norm).astype(BF16))

    grad_branch_far = far_half(grad_branch_b)
    grad_chunks = order.keep(
        to_chunks(target, perm, order(grad_branch_b)[None], blocks_proj, tables_here, 0)
    )
    grad_branch_far = order.wait(grad_branch_far)
    grad_pieces = to_heads(grad_chunks)
    grad_down.append(scatter_ctx(down[1].finish()))
    up[1].launch()
    proj = Scatter(
        order, grad_branch_b[None], [attended[None]], grad_branch_far[None], [attended_far[None]]
    )
    made_proj = proj.make(1)
    grad_up = [scatter_ctx(up[0].finish())]
    proj.launch(0, None, order(made_proj))
    grad_pieces = order.wait(grad_pieces)
    back = [
        order.keep(attend_back(source, lengths, pieces, order(grad_pieces), tables_all, 0))
    ]
    sent = [to_slots(back[0])]
    back.append(
        order.keep(attend_back(source, lengths, pieces, order(grad_pieces), tables_all, 1))
    )
    grad_down[0] = order.wait(grad_down[0])
    mine, theirs, own = [], [], []
    grad_up.append(scatter_ctx(up[1].finish()))
    sent[0] = order.wait(sent[0])
    mine.append(order.keep(join(target, sent[0])))
    theirs.append(over_tp(mine[0]))
    sent.append(to_slots(order(back[1])))
    own.append(order.keep(own_part(perm, order(mine[0]), streams, blocks_qkv, 0)))
    grad_down[1] = order.wait(grad_down[1])
    grad_proj = scatter_ctx(proj.finish())
    sent[1] = order.wait(sent[1])
    mine.append(order.keep(join(target, sent[1])))
    theirs.append(over_tp(mine[1]))
    mine_far = order.wait([over_fsdp(m, 1) for m in order(mine)])
    qkv = Scatter(order, normed_in, mine, normed_in_far, mine_far)
    qkv.launch(0, 1)
    qkv.launch(1, 2)
    own.append(order.keep(own_part(perm, order(mine[1]), streams, blocks_qkv, 1)))
    grad_up[0] = order.wait(grad_up[0])
    theirs[0] = order.wait(theirs[0])
    grad_query = scatter_ctx(qkv.finish(0, 1))
    sums = (own[0][1] + own[1][1]).sum(0).reshape(2, 8, width).sum(1)
    sums = order.wait(sums)

    dz = order.keep(other_part(order(theirs[0]), own[0][0], streams, gain_first, other, 0))
    done = order.keep(
        last_stage(perm, inputs, coeff, order(dz), grad_branch_b, 0, rows, ())
    )
    theirs[1] = order.wait(theirs[1])
    sums_far = over_tp(order(sums))
    dz = order.keep(other_part(order(theirs[1]), own[1][0], streams, gain_first, other, 1))
    sums_far = order.wait(sums_far)
    packed = jnp.concatenate(
        [grad_mixer_first, sums + sums_far, grad_gain_second, grad_shift_second], axis=0
    )
    packed = packed.reshape(packed.shape[0], fsdp, ctx, piece)
    packed = jnp.stack(
        [lax.dynamic_index_in_dim(packed, z ^ m, 2, keepdims=False) for m in block_masks(ctx)]
    ).transpose(0, 2, 1, 3)
    tail = jnp.pad(tail, ((0, 0), (0, HD - MIXW)))
    packed, tail = order.wait((packed, tail))

    def fold(packed, tail, move):
        split = packed.shape[0] // 2
        return packed[:split], tail, move(packed[split:]), move(tail)

    def landed(packed, tail, got_packed, got_tail):
        got_packed, got_tail = order.wait((got_packed, got_tail))
        return packed + got_packed, tail + got_tail

    ctx_steps = [
        (lambda v, bit=bit: lax.ppermute(v, "ctx", xor_pairs(ctx, bit)))
        for bit in reversed(bits_of(ctx))
    ]
    fsdp_steps = [(lambda v, bit=bit: over_fsdp(v, bit)) for bit in reversed(bits_of(fsdp))]
    moving = fold(packed, tail, ctx_steps[0])
    grad_rest = scatter_ctx(qkv.finish(1, 2))
    grad_up[1] = order.wait(grad_up[1])
    for step in ctx_steps[1:]:
        moving = fold(*landed(*moving), step)
    grad_inputs, grad_coeff = order.keep(
        last_stage(perm, inputs, coeff, order(dz), grad_branch_b, 1, rows, done)
    )
    packed, tail = landed(*moving)
    moving = fold(packed[0], tail, fsdp_steps[0])
    grad_proj = order.wait(grad_proj)
    for step in fsdp_steps[1:]:
        moving = fold(*landed(*moving), step)
    packed, tail = landed(*moving)
    norms = packed[0]
    grad_key, grad_value = jnp.split(grad_rest, 2, axis=1)
    grad_proj = grad_proj.T
    grad_earlier = grad_inputs.reshape(earlier.shape)
    grad_mix_in = (
        grad_coeff[:, :, :STREAMS]
        .reshape(tokens // GROUP, count_prev, GROUP, STREAMS)
        .transpose(3, 1, 0, 2)
        .reshape(mix_in.shape)
    )
    return (
        output,
        mix_out,
        grad_earlier,
        grad_mix_in,
        grad_query,
        grad_key,
        grad_value,
        grad_proj,
        jnp.concatenate(grad_up, axis=1),
        jnp.concatenate(grad_down, axis=1).T,
        norms[MIXW],
        norms[MIXW + 1],
        norms[MIXW + 2],
        norms[MIXW + 3],
        norms[:MIXW].T,
        tail[:MIXW, :MIXW],
        tail[MIXW, :MIXW],
    )


def solution(mesh):
    placed = (
        P(None, "fsdp", "ctx", None),
        P(None, "fsdp", "ctx"),
        P("fsdp"),
        P(("fsdp", "ctx"), "tp"),
        P(("fsdp", "ctx"), "tp"),
        P(("fsdp", "ctx"), "tp"),
        P("tp", ("fsdp", "ctx")),
        P(("fsdp", "ctx"), "tp"),
        P("tp", ("fsdp", "ctx")),
        P(("fsdp", "ctx")),
        P(("fsdp", "ctx")),
        P(("fsdp", "ctx")),
        P(("fsdp", "ctx")),
        P(("fsdp", "ctx"), None),
        P(),
        P(),
        P("fsdp", "ctx", None),
        P(None, "fsdp", "ctx"),
    )
    return jax.shard_map(
        body,
        mesh=mesh,
        in_specs=placed,
        out_specs=(
            P("fsdp", "ctx", None),
            P(None, "fsdp", "ctx"),
            P(None, "fsdp", "ctx", None),
            P(None, "fsdp", "ctx"),
            P(("fsdp", "ctx"), "tp"),
            P(("fsdp", "ctx"), "tp"),
            P(("fsdp", "ctx"), "tp"),
            P("tp", ("fsdp", "ctx")),
            P(("fsdp", "ctx"), "tp"),
            P("tp", ("fsdp", "ctx")),
            P(("fsdp", "ctx")),
            P(("fsdp", "ctx")),
            P(("fsdp", "ctx")),
            P(("fsdp", "ctx")),
            P(("fsdp", "ctx"), None),
            P(),
            P(),
        ),
        check_vma=False,
    )
```

```python
from functools import partial
import math

import jax
import jax.numpy as jnp
from jax import lax
from jax.experimental import pallas as pl
from jax.experimental.pallas import tpu as pltpu
from jax.sharding import PartitionSpec as P

HD = 128
ROT = 32
STREAMS = 4
MIXW = 36
EPSILON = 1e-05
RMS_EPSILON = 1e-06
HIGHEST = lax.Precision.HIGHEST
NEGATIVE = -1e30
F32 = jnp.float32
BF16 = jnp.bfloat16
GROUP = 32
FORWARD_PACE = 3.0e7
BACKWARD_PACE = 1.5e9


def params(grid_rank):
    return pltpu.CompilerParams(
        dimension_semantics=("arbitrary",) * grid_rank, vmem_limit_bytes=56 * 1024 * 1024
    )


class Pace:
    value = FORWARD_PACE


def cost(time):
    return pl.CostEstimate(flops=int(time * Pace.value), transcendentals=0, bytes_accessed=1024)


def xor_pairs(size, mask):
    return [(i, i ^ mask) for i in range(size)]


def over_fsdp(values, mask):
    return lax.ppermute(values, "fsdp", xor_pairs(lax.axis_size("fsdp"), mask))


def over_tp(values):
    return lax.ppermute(values, "tp", xor_pairs(lax.axis_size("tp"), 1))


def shift_ctx(values, step):
    size = lax.axis_size("ctx")
    return lax.ppermute(values, "ctx", [(i, (i + step) % size) for i in range(size)])


def bits_of(size):
    return [1 << b for b in reversed(range(size.bit_length() - 1))]


def block_masks(size):
    masks = [0]
    for bit in bits_of(size):
        masks = masks + [m ^ bit for m in masks]
    return masks


def after(values, *earlier):
    return lax.optimization_barrier((values, earlier))[0]


class Order:
    def __init__(self):
        self.last = ()

    def __call__(self, values):
        return after(values, self.last)

    def keep(self, values):
        self.last = values
        return values

    def wait(self, values):
        return self.keep(self(values))


def gather_ctx(shard):
    return lax.all_gather(shard, "ctx", axis=0, tiled=True)


def cross(own):
    parts = [own]
    for bit in bits_of(lax.axis_size("fsdp"))[:-1]:
        parts = parts + [over_fsdp(p, bit) for p in parts]
    return parts


class Scatter:
    def __init__(self, order, left, rights, left_far, rights_far):
        self.order, self.left, self.far, self.rights = order, left, left_far, (rights, rights_far)
        self.count = lax.axis_size("fsdp")
        self.received = [[] for _ in range(self.count)]

    def blocks(self, chosen, first, kinds):
        near, far = self.order(self.rights)
        added = [[r for r in self.received[p] if r[2] == first] for p in chosen]
        made = grad_blocks(self.left, self.far, near, far, self.count, chosen, added, first, kinds)
        return self.order.keep(made)

    def make(self, level, first=0, kinds=None):
        half = self.count >> (level + 1)
        chosen = list(range(half, 2 * half))
        return self.blocks(chosen, first, kinds or self.left.shape[0])

    def send(self, level, made, first=0):
        half = self.count >> (level + 1)
        bit = bits_of(self.count)[::-1][level]
        got = over_fsdp(made, bit)
        for n in range(half):
            self.received[n].append((got, n, first))
        return got

    def launch(self, first=0, kinds=None, made=None):
        for level in range(1, len(bits_of(self.count))):
            if made is None:
                made = self.make(level, first, kinds)
            self.send(level, made, first)
            made = None

    def finish(self, first=0, kinds=None):
        return self.blocks([0], first, kinds or self.left.shape[0])[0]


def scatter_ctx(total):
    return lax.psum_scatter(total, "ctx", scatter_dimension=0, tiled=True).astype(F32)


def tp_sum(mine, theirs):
    return mine.astype(F32) + theirs.astype(F32)


NT = (((1,), (1,)), ((), ()))
TN = (((0,), (0,)), ((), ()))


def spread(coeff):
    count = coeff.shape[0]
    token = lax.broadcasted_iota(jnp.int32, (count, STREAMS * GROUP), 0) % GROUP
    lane = lax.broadcasted_iota(jnp.int32, (count, STREAMS * GROUP), 1)
    out = jnp.zeros((count, STREAMS * GROUP), F32)
    for s in range(STREAMS):
        out = jnp.where(lane == token + s * GROUP, coeff[:, s : s + 1], out)
    high = out.astype(BF16)
    return high, (out - high.astype(F32)).astype(BF16)


def mix_kernel(perm_ref, earlier_ref, coeff_ref, gain_ref, shift_ref, a_ref, z_ref):
    prev, tile, width = earlier_ref.shape
    parts = perm_ref.shape[0]
    block = width // parts
    for g in range(tile // GROUP):
        rows = slice(g * GROUP, (g + 1) * GROUP)
        high, low = spread(coeff_ref[g])
        for p in range(parts):
            source = pl.ds(pl.multiple_of(perm_ref[p] * block, 128), block)
            x = earlier_ref[:, rows, source].reshape(prev * GROUP, block)
            z_ref[:, rows, p * block : (p + 1) * block] = (
                lax.dot_general(high, x, TN, preferred_element_type=F32)
                + lax.dot_general(low, x, TN, preferred_element_type=F32)
            ).reshape(STREAMS, GROUP, block)
        for s in range(STREAMS - 1):
            z = z_ref[s, rows, :]
            center = z - jnp.mean(z, axis=-1, keepdims=True)
            spread_of = jnp.mean(center * center, axis=-1, keepdims=True)
            a_ref[s, rows, :] = (
                center * lax.rsqrt(spread_of + EPSILON) * gain_ref[...] + shift_ref[...]
            ).astype(BF16)


def mix_streams(perm, inputs, coeff, gain, shift, tile=64):
    prev, tokens, width = inputs.shape
    return pl.pallas_call(
        mix_kernel,
        name="mix",
        grid_spec=pltpu.PrefetchScalarGridSpec(
            num_scalar_prefetch=1,
            grid=(tokens // tile,),
            in_specs=[
                pl.BlockSpec((prev, tile, width), lambda t, *_: (0, t, 0)),
                pl.BlockSpec((tile // GROUP,) + coeff.shape[1:], lambda t, *_: (t, 0, 0)),
                pl.BlockSpec((1, width), lambda t, *_: (0, 0)),
                pl.BlockSpec((1, width), lambda t, *_: (0, 0)),
            ],
            out_specs=[
                pl.BlockSpec((STREAMS - 1, tile, width), lambda t, *_: (0, t, 0)),
                pl.BlockSpec((STREAMS, tile, width), lambda t, *_: (0, t, 0)),
            ],
        ),
        out_shape=[
            jax.ShapeDtypeStruct((STREAMS - 1, tokens, width), BF16),
            jax.ShapeDtypeStruct((STREAMS, tokens, width), F32),
        ],
        cost_estimate=cost(14),
        compiler_params=params(1),
    )(perm, inputs, coeff, gain, shift)


def turn(values, tables, sign):
    base, up, down = tables
    return (
        values * base
        + sign * (pltpu.roll(values, ROT // 2, 1) * up)
        + sign * (pltpu.roll(values, HD - ROT // 2, 1) * down)
    )


def blocks_dot(a_ref, weights):
    parts = len(weights)
    block = a_ref.shape[-1] // parts
    total = None
    for p in range(parts):
        term = jnp.dot(
            a_ref[:, p * block : (p + 1) * block], weights[p][...], preferred_element_type=F32
        )
        total = term if total is None else total + term
    return total


def block_specs(weights, rows, columns, at):
    return [pl.BlockSpec((rows, columns), lambda *ids: (0, at(*ids)))] * len(weights)


def heads_kernel(target_ref, perm_ref, a_ref, *refs, parts, turned):
    weights = refs[:parts]
    tables = refs[parts : parts + 3]
    outs = refs[parts + 3 :]
    total = blocks_dot(a_ref.at[0], weights)
    kind, step = pl.program_id(0), pl.program_id(1)
    for s, out_ref in enumerate(outs):

        @pl.when((step == s) & (kind < turned))
        def _():
            tabs = [t[...] for t in tables]
            for h in range(total.shape[1] // HD):
                cols = slice(h * HD, (h + 1) * HD)
                out_ref[0, :, cols] = turn(total[:, cols], tabs, 1.0).astype(BF16)

        @pl.when((step == s) & (kind >= turned))
        def _():
            out_ref[0] = total.astype(BF16)


def to_chunks(target, perm, a, weights, tables, turned):
    kinds, tokens, width = a.shape
    parts = perm.shape[0]
    chunks = target.shape[0]
    columns = weights[0].shape[1] // chunks // kinds
    specs = block_specs(
        weights, width // parts, columns, lambda s, n, target, _: s * chunks + target[n]
    )
    return pl.pallas_call(
        partial(heads_kernel, parts=parts, turned=turned),
        name="heads",
        grid_spec=pltpu.PrefetchScalarGridSpec(
            num_scalar_prefetch=2,
            grid=(kinds, chunks),
            in_specs=[pl.BlockSpec((1, tokens, width), lambda s, n, *_: (s, 0, 0))]
            + specs
            + [pl.BlockSpec((tokens, HD), lambda s, n, *_: (0, 0))] * 3,
            out_specs=[pl.BlockSpec((1, tokens, columns), lambda s, n, *_: (s, 0, 0))] * chunks,
        ),
        out_shape=[jax.ShapeDtypeStruct((kinds, tokens, columns), BF16)] * chunks,
        cost_estimate=cost(2 * kinds * chunks),
        compiler_params=params(2),
    )(target, perm, a, *weights, *tables)


def join_kernel(target_ref, *refs):
    for s in range(len(refs) - 1):

        @pl.when(pl.program_id(0) == s)
        def _():
            refs[-1][...] = refs[s][...]


def join(target, pieces):
    kinds, count, columns = pieces[0].shape
    chunks = len(pieces)
    return pl.pallas_call(
        join_kernel,
        name="join",
        grid_spec=pltpu.PrefetchScalarGridSpec(
            num_scalar_prefetch=1,
            grid=(chunks,),
            in_specs=[pl.BlockSpec((kinds, count, columns), lambda n, _: (0, 0, 0))] * chunks,
            out_specs=pl.BlockSpec((kinds, count, columns), lambda n, target: (0, 0, target[n])),
        ),
        out_shape=jax.ShapeDtypeStruct((kinds, count, columns * chunks), BF16),
        cost_estimate=cost(2),
        compiler_params=params(1),
    )(target, *pieces)


def weights_of(query, keys, tile_index, tile, length, scale):
    count = keys.shape[0]
    scores = (
        lax.dot_general(query, keys, (((1,), (1,)), ((), ())), preferred_element_type=F32) * scale
    )
    row = tile_index * tile + lax.broadcasted_iota(jnp.int32, (tile, count), 0)
    col = lax.broadcasted_iota(jnp.int32, (tile, count), 1)
    masked = jnp.where((col <= row) & (col < length), scores, NEGATIVE)
    expo = jnp.exp(masked - jnp.max(masked, axis=-1, keepdims=True))
    return expo / jnp.sum(expo, axis=-1, keepdims=True)


def collect(source_ref, pieces, scratch, span):
    for s, piece in enumerate(pieces):
        at = pl.ds(pl.multiple_of(source_ref[s] * span, span), span)
        scratch[at, :] = piece[...]


def spread_out(source_ref, scratch, pieces, span):
    for s, piece in enumerate(pieces):
        at = pl.ds(pl.multiple_of(source_ref[s] * span, span), span)
        piece[...] = scratch[at, :]


def collect(source_ref, pieces, kind, scratch):
    span = pieces[0].shape[1]
    for s, piece in enumerate(pieces):
        at = pl.ds(pl.multiple_of(source_ref[s] * span, span), span)
        scratch[at, :] = piece[kind]


def spread_out(source_ref, scratch, pieces, kind):
    span = pieces[0].shape[1]
    for s, piece in enumerate(pieces):
        at = pl.ds(pl.multiple_of(source_ref[s] * span, span), span)
        piece[kind] = scratch[at, :]


def attend_kernel(source_ref, length_ref, *refs, chunks):
    ins, outs = refs[:chunks], refs[chunks : 2 * chunks]
    q_all, k_all, v_all, o_all = refs[2 * chunks :]
    span = ins[0].shape[1]
    length = length_ref[pl.program_id(0)]
    scale = 1.0 / math.sqrt(HD)
    for kind, scratch in enumerate((q_all, k_all, v_all)):
        collect(source_ref, ins, kind, scratch)
    for h in range(q_all.shape[1] // HD):
        cols = slice(h * HD, (h + 1) * HD)
        for i in range(chunks):
            rows = slice(i * span, (i + 1) * span)
            seen = slice(0, (i + 1) * span)
            probs = weights_of(q_all[rows, cols], k_all[seen, cols], i, span, length, scale)
            o_all[rows, cols] = jnp.dot(
                probs.astype(BF16), v_all[seen, cols], preferred_element_type=F32
            ).astype(BF16)
    spread_out(source_ref, o_all, outs, 0)


def attend(source, lengths, pieces):
    chunks = len(pieces)
    rows = lengths.shape[0]
    kinds, tokens, columns = pieces[0].shape
    span = tokens // rows
    return pl.pallas_call(
        partial(attend_kernel, chunks=chunks),
        name="attend",
        grid_spec=pltpu.PrefetchScalarGridSpec(
            num_scalar_prefetch=2,
            grid=(rows,),
            in_specs=[pl.BlockSpec((kinds, span, columns), lambda r, *_: (0, r, 0))] * chunks,
            out_specs=[pl.BlockSpec((1, span, columns), lambda r, *_: (0, r, 0))] * chunks,
            scratch_shapes=[pltpu.VMEM((span * chunks, columns), BF16)] * 4,
        ),
        out_shape=[jax.ShapeDtypeStruct((1, tokens, columns), BF16)] * chunks,
        cost_estimate=cost(6 * rows),
        compiler_params=params(1),
    )(source, lengths, *pieces)


def attend_back_kernel(source_ref, length_ref, *refs, chunks, row):
    ins, grads = refs[:chunks], refs[chunks : 2 * chunks]
    tabs = refs[2 * chunks : 2 * chunks + 3]
    outs = refs[2 * chunks + 3 : 3 * chunks + 3]
    q_all, k_all, v_all, g_all, dk_sum, dv_sum, dq_all, dk_all, dv_all = refs[3 * chunks + 3 :]
    span = ins[0].shape[1]
    length = length_ref[row]
    scale = 1.0 / math.sqrt(HD)
    for kind, scratch in enumerate((q_all, k_all, v_all)):
        collect(source_ref, ins, kind, scratch)
    collect(source_ref, grads, 0, g_all)
    for h in range(q_all.shape[1] // HD):
        cols = slice(h * HD, (h + 1) * HD)
        for i in reversed(range(chunks)):
            rows = slice(i * span, (i + 1) * span)
            seen = slice(0, (i + 1) * span)
            query, grad = q_all[rows, cols], g_all[rows, cols]
            keys, values = k_all[seen, cols], v_all[seen, cols]
            probs = weights_of(query, keys, i, span, length, scale)
            grad_probs = lax.dot_general(grad, values, NT, preferred_element_type=F32)
            delta = jnp.sum(probs * grad_probs, axis=-1, keepdims=True)
            scores = (probs * (grad_probs - delta) * scale).astype(BF16)
            turned = [t[rows, :] for t in tabs]
            dq_all[rows, cols] = turn(
                jnp.dot(scores, keys, preferred_element_type=F32), turned, -1.0
            ).astype(BF16)
            dk = lax.dot_general(scores, query, TN, preferred_element_type=F32)
            dv = lax.dot_general(probs.astype(BF16), grad, TN, preferred_element_type=F32)
            if i == chunks - 1:
                dk_sum[...] = dk
                dv_sum[...] = dv
            else:
                dk_sum[seen, :] += dk
                dv_sum[seen, :] += dv
        dk_all[:, cols] = turn(dk_sum[...], [t[...] for t in tabs], -1.0).astype(BF16)
        dv_all[:, cols] = dv_sum[...].astype(BF16)
    for kind, scratch in enumerate((dq_all, dk_all, dv_all)):
        spread_out(source_ref, scratch, outs, kind)


def attend_back(source, lengths, pieces, grads, tables, row):
    chunks = len(pieces)
    rows = lengths.shape[0]
    kinds, tokens, columns = pieces[0].shape
    span = tokens // rows
    seq = span * chunks
    wide = pltpu.VMEM((seq, columns), BF16)
    return pl.pallas_call(
        partial(attend_back_kernel, chunks=chunks, row=row),
        name="attend_back",
        grid_spec=pltpu.PrefetchScalarGridSpec(
            num_scalar_prefetch=2,
            grid=(1,),
            in_specs=[pl.BlockSpec((kinds, span, columns), lambda r, *_: (0, row, 0))] * chunks
            + [pl.BlockSpec((1, span, columns), lambda r, *_: (0, row, 0))] * chunks
            + [pl.BlockSpec((seq, HD), lambda r, *_: (0, 0))] * 3,
            out_specs=[pl.BlockSpec((kinds, span, columns), lambda r, *_: (0, 0, 0))] * chunks,
            scratch_shapes=[wide] * 4 + [pltpu.VMEM((seq, HD), F32)] * 2 + [wide] * 3,
        ),
        out_shape=[jax.ShapeDtypeStruct((kinds, span, columns), BF16)] * chunks,
        cost_estimate=cost(12),
        compiler_params=params(1),
    )(source, lengths, *pieces, *grads, *tables)


def up_kernel(perm_ref, a_ref, *refs, parts):
    weights = refs[:parts]
    active_ref, slope_ref = refs[parts:]
    u = blocks_dot(a_ref, weights)
    half = 0.5 * (1.0 + lax.erf(u * math.sqrt(0.5)))
    active_ref[...] = (u * half).astype(BF16)
    slope_ref[...] = half + u * jnp.exp(-0.5 * u * u) * (1.0 / math.sqrt(2.0 * math.pi))


def up_stage(perm, a, weights, part, columns, tile=512):
    tokens, width = a.shape
    parts = perm.shape[0]
    tile = min(tile, columns)
    specs = block_specs(weights, width // parts, tile, lambda n, *_: part * (columns // tile) + n)
    out = pl.BlockSpec((tokens, tile), lambda n, *_: (0, n))
    return pl.pallas_call(
        partial(up_kernel, parts=parts),
        name="up",
        grid_spec=pltpu.PrefetchScalarGridSpec(
            num_scalar_prefetch=1,
            grid=(columns // tile,),
            in_specs=[pl.BlockSpec((tokens, width), lambda n, *_: (0, 0))] + specs,
            out_specs=[out, out],
        ),
        out_shape=[
            jax.ShapeDtypeStruct((tokens, columns), BF16),
            jax.ShapeDtypeStruct((tokens, columns), F32),
        ],
        cost_estimate=cost(columns / 200),
        compiler_params=params(1),
    )(perm, a, *weights)


def up_back_kernel(perm_ref, a_ref, slope_ref, *refs, parts):
    weights = refs[:parts]
    refs[parts][...] = (blocks_dot(a_ref, weights) * slope_ref[...]).astype(BF16)


def up_back(perm, a, slope, weights, offset, tile=512):
    tokens, width = a.shape
    parts = perm.shape[0]
    columns = slope.shape[1]
    tile = min(tile, columns)
    specs = block_specs(
        weights, width // parts, tile, lambda n, *_: offset // tile + n
    )
    out = pl.BlockSpec((tokens, tile), lambda n, *_: (0, n))
    return pl.pallas_call(
        partial(up_back_kernel, parts=parts),
        name="up_back",
        grid_spec=pltpu.PrefetchScalarGridSpec(
            num_scalar_prefetch=1,
            grid=(columns // tile,),
            in_specs=[pl.BlockSpec((tokens, width), lambda n, *_: (0, 0)), out] + specs,
            out_specs=out,
        ),
        out_shape=jax.ShapeDtypeStruct((tokens, columns), BF16),
        cost_estimate=cost(columns / 200),
        compiler_params=params(1),
    )(perm, a, slope, *weights)


def back_kernel(*refs, lefts, parts, adds):
    out_ref = refs[-1]
    block = out_ref.shape[1] // parts
    tile = refs[lefts].shape[0]
    n = pl.program_id(0)
    for p in range(parts):
        at = pl.ds(pl.multiple_of(p * block + n * tile, 128), tile)
        total = refs[-2][:, at] if adds else None
        for h in range(lefts):
            term = lax.dot_general(
                refs[h][...], refs[lefts + h * parts + p][...], NT, preferred_element_type=F32
            )
            total = term if total is None else total + term
        out_ref[:, at] = total.astype(out_ref.dtype)


def to_width(lefts, weights, width, added=(), dtype=BF16, across=(0,)):
    parts = len(weights[0])
    block = width // parts
    tile = min(block, 256)
    tokens = lefts[0].shape[0]
    left_specs, specs, arrays = [], [], []
    for left, weight, at in zip(lefts, weights, across):
        columns = left.shape[1]
        left_specs.append(pl.BlockSpec((tokens, columns), lambda n: (0, 0)))
        specs += [pl.BlockSpec((tile, columns), lambda n, at=at: (n, at))] * parts
        arrays += weight
    whole = pl.BlockSpec((tokens, width), lambda n: (0, 0))
    return pl.pallas_call(
        partial(back_kernel, lefts=len(lefts), parts=parts, adds=len(added)),
        name="to_width",
        grid=(block // tile,),
        in_specs=left_specs + specs + [whole] * len(added),
        out_specs=whole,
        out_shape=jax.ShapeDtypeStruct((tokens, width), dtype),
        cost_estimate=cost(sum(a.shape[1] for a in lefts) / 256),
        compiler_params=params(1),
    )(*lefts, *arrays, *added)


def grad_kernel(*refs, count, rights, adds):
    lefts, fars = refs[:count], refs[count : 2 * count]
    sides = refs[2 * count : 2 * count + rights], refs[2 * count + rights : 2 * count + 2 * rights]
    add_refs, out_ref = refs[2 * count + 2 * rights : -1], refs[-1]
    at = 0
    for b in range(count):
        total = None
        for left, right_refs in zip((lefts[b], fars[b]), sides):
            start = 0
            for right in right_refs:
                size = right.shape[1]
                term = lax.dot_general(
                    left[0, start : start + size, :], right[0], TN, preferred_element_type=F32
                )
                total = term if total is None else total + term
                start += size
        for n in range(adds[b]):
            total = total + add_refs[at + n][0].astype(F32)
        at += adds[b]
        out_ref[b] = total.astype(BF16)


def grad_blocks(left, left_far, near, far, parts, chosen, added, first, kinds, tile=512):
    _, tokens, width = left.shape
    columns = near[0].shape[2]
    tile = min(tile, columns)
    steps = columns // tile
    block = width // parts

    def place(start, row):
        return lambda s, n: (row, 0, (first - start + s) * steps + n)

    flat = [a for arrays in added for a in arrays]
    left_specs = [
        pl.BlockSpec((1, tokens, block), lambda s, n, p=p: (first + s, 0, p)) for p in chosen
    ]
    return pl.pallas_call(
        partial(
            grad_kernel,
            count=len(chosen),
            rights=len(near),
            adds=tuple(len(a) for a in added),
        ),
        name="grad",
        grid=(kinds, steps),
        in_specs=left_specs * 2
        + [
            pl.BlockSpec((1, r.shape[1], tile), lambda s, n: (first + s, 0, n))
            for r in (*near, *far)
        ]
        + [pl.BlockSpec((1, block, tile), place(start, row)) for _, row, start in flat],
        out_specs=pl.BlockSpec((len(chosen), block, tile), lambda s, n: (0, 0, s * steps + n)),
        out_shape=jax.ShapeDtypeStruct((len(chosen), block, kinds * columns), BF16),
        cost_estimate=cost(len(chosen) * kinds * columns / 512),
        compiler_params=params(2),
    )(*[left] * len(chosen), *[left_far] * len(chosen), *near, *far, *[a for a, _, _ in flat])


def part_kernel(in_ref, out_ref, *, turned):
    values = in_ref[...]
    out_ref[...] = values.astype(F32).T.astype(BF16) if turned else values


def shard_part(shard, n, size, turned):
    short = shard.shape[1] if turned else shard.shape[0]
    spec = pl.BlockSpec((size, short), lambda i: (n, 0))
    if not turned:
        spec = pl.BlockSpec((short, size), lambda i: (0, n))
    return pl.pallas_call(
        partial(part_kernel, turned=turned),
        name="part",
        grid=(1,),
        in_specs=[spec],
        out_specs=pl.BlockSpec((short, size), lambda i: (0, 0)),
        out_shape=jax.ShapeDtypeStruct((short, size), BF16),
        cost_estimate=cost(1),
        compiler_params=params(1),
    )(shard)


def hat_of(z):
    center = z - jnp.mean(z, axis=-1, keepdims=True)
    inverse = lax.rsqrt(jnp.mean(center * center, axis=-1, keepdims=True) + EPSILON)
    return center * inverse, inverse


def own_kernel(perm_ref, grad_ref, z_ref, *refs, parts):
    weights = refs[:parts]
    out_ref, sum_ref = refs[parts:]
    block = weights[0].shape[0]
    for p in range(parts):
        out_ref[0, :, p * block : (p + 1) * block] = lax.dot_general(
            grad_ref[0], weights[p][...], NT, preferred_element_type=F32
        )
    tile = 32
    tokens, width = out_ref.shape[1:]
    gain = jnp.zeros((8, width), F32)
    shift = jnp.zeros((8, width), F32)
    for t in range(0, tokens, tile):
        d = out_ref[0, t : t + tile, :]
        hat, _ = hat_of(z_ref[0, t : t + tile, :])
        gain = gain + jnp.sum((d * hat).reshape(tile // 8, 8, width), axis=0)
        shift = shift + jnp.sum(d.reshape(tile // 8, 8, width), axis=0)
    sum_ref[0, :8] = gain
    sum_ref[0, 8:] = shift


def own_part(perm, grads, streams, weights, row):
    kinds, span, columns = grads.shape
    width = streams.shape[2]
    parts = perm.shape[0]
    specs = block_specs(weights, width // parts, columns, lambda s, *_: s)
    return pl.pallas_call(
        partial(own_kernel, parts=parts),
        name="own",
        grid_spec=pltpu.PrefetchScalarGridSpec(
            num_scalar_prefetch=1,
            grid=(kinds,),
            in_specs=[
                pl.BlockSpec((1, span, columns), lambda s, *_: (s, 0, 0)),
                pl.BlockSpec((1, span, width), lambda s, *_: (s, row, 0)),
            ]
            + specs,
            out_specs=[
                pl.BlockSpec((1, span, width), lambda s, *_: (s, 0, 0)),
                pl.BlockSpec((1, 16, width), lambda s, *_: (s, 0, 0)),
            ],
        ),
        out_shape=[
            jax.ShapeDtypeStruct((kinds, span, width), F32),
            jax.ShapeDtypeStruct((kinds, 16, width), F32),
        ],
        cost_estimate=cost(12),
        compiler_params=params(1),
    )(perm, grads, streams, *weights)


def other_kernel(grad_ref, part_ref, z_ref, gain_ref, *refs, parts):
    weights = refs[:parts]
    out_ref, total_ref = refs[parts:]
    block = weights[0].shape[0]
    for p in range(parts):
        cols = slice(p * block, (p + 1) * block)
        total_ref[:, cols] = part_ref[0, :, cols] + lax.dot_general(
            grad_ref[0], weights[p][...], NT, preferred_element_type=F32
        )
    tile = 32
    for t in range(0, total_ref.shape[0], tile):
        rows = slice(t, t + tile)
        hat, inverse = hat_of(z_ref[0, rows, :])
        e = total_ref[rows, :] * gain_ref[...]
        first = jnp.mean(e, axis=-1, keepdims=True)
        second = jnp.mean(e * hat, axis=-1, keepdims=True)
        out_ref[0, rows, :] = ((e - first - hat * second) * inverse).astype(BF16)


def other_part(grads, own, streams, gain, weights, row):
    kinds, span, columns = grads.shape
    width = streams.shape[2]
    parts = len(weights)
    block = width // parts
    return pl.pallas_call(
        partial(other_kernel, parts=parts),
        name="other",
        grid=(kinds,),
        in_specs=[
            pl.BlockSpec((1, span, columns), lambda s: (s, 0, 0)),
            pl.BlockSpec((1, span, width), lambda s: (s, 0, 0)),
            pl.BlockSpec((1, span, width), lambda s: (s, row, 0)),
            pl.BlockSpec((1, width), lambda s: (0, 0)),
        ]
        + [pl.BlockSpec((block, columns), lambda s: (0, s))] * parts,
        out_specs=pl.BlockSpec((1, span, width), lambda s: (s, 0, 0)),
        out_shape=jax.ShapeDtypeStruct((kinds, span, width), BF16),
        scratch_shapes=[pltpu.VMEM((span, width), F32)],
        cost_estimate=cost(14),
        compiler_params=params(1),
    )(grads, own, streams, gain, *weights)


def last_kernel(perm_ref, earlier_ref, coeff_ref, dz_ref, dr_ref, *refs):
    out_ref, mix_ref = refs[-2:]
    prev, tile, width = earlier_ref.shape
    parts = perm_ref.shape[0]
    block = width // parts
    count, half = prev * GROUP, STREAMS * GROUP
    for g in range(tile // GROUP):
        rows = slice(g * GROUP, (g + 1) * GROUP)
        high, low = spread(coeff_ref[g])
        pairs = jnp.zeros((count, half), F32)
        for p in range(parts):
            here = slice(p * block, (p + 1) * block)
            there = pl.ds(pl.multiple_of(perm_ref[p] * block, 128), block)
            grads = jnp.concatenate(
                [dz_ref[s, rows, here] for s in range(STREAMS - 1)] + [dr_ref[rows, here]], axis=0
            )
            x = earlier_ref[:, rows, there].reshape(count, block)
            pairs = pairs + lax.dot_general(x, grads, NT, preferred_element_type=F32)
            total = jnp.dot(high, grads, preferred_element_type=F32) + jnp.dot(
                low, grads, preferred_element_type=F32
            )
            out_ref[:, rows, there] = total.astype(BF16).reshape(prev, GROUP, block)
        token = lax.broadcasted_iota(jnp.int32, (count, half), 0) % GROUP
        lane = lax.broadcasted_iota(jnp.int32, (count, half), 1)
        wide = lax.broadcasted_iota(jnp.int32, (count, 128), 1)
        mixed = jnp.zeros((count, 128), F32)
        for s in range(STREAMS):
            own = jnp.where(lane == token + s * GROUP, pairs, 0.0)
            mixed = jnp.where(wide == s, jnp.sum(own, axis=-1, keepdims=True), mixed)
        mix_ref[g] = mixed


def last_stage(perm, inputs, coeff, dz, dr, row, rows, before, tile=64):
    prev, tokens, width = inputs.shape
    steps = tokens // rows // tile
    count = prev * GROUP
    here = lambda t, *_: (0, row * steps + t, 0)
    return pl.pallas_call(
        last_kernel,
        name="last",
        grid_spec=pltpu.PrefetchScalarGridSpec(
            num_scalar_prefetch=1,
            grid=(steps,),
            in_specs=[
                pl.BlockSpec((prev, tile, width), here),
                pl.BlockSpec(
                    (tile // GROUP,) + coeff.shape[1:], lambda t, *_: (row * steps + t, 0, 0)
                ),
                pl.BlockSpec((STREAMS - 1, tile, width), lambda t, *_: (0, t, 0)),
                pl.BlockSpec((tile, width), lambda t, *_: (row * steps + t, 0)),
            ]
            + [pl.BlockSpec(memory_space=pl.ANY)] * len(before),
            out_specs=[
                pl.BlockSpec((prev, tile, width), here),
                pl.BlockSpec(
                    (tile // GROUP, count, 128), lambda t, *_: (row * steps + t, 0, 0)
                ),
            ],
        ),
        out_shape=[
            jax.ShapeDtypeStruct((prev, tokens, width), BF16),
            jax.ShapeDtypeStruct((tokens // GROUP, count, 128), F32),
        ],
        input_output_aliases={5 + n: n for n in range(len(before))},
        cost_estimate=cost(12),
        compiler_params=params(1),
    )(perm, inputs, coeff, dz, dr, *before)


def layer_norm(values, gain, shift):
    center = values - jnp.mean(values, axis=-1, keepdims=True)
    spread = jnp.mean(center * center, axis=-1, keepdims=True)
    return center * lax.rsqrt(spread + EPSILON) * gain + shift


def activate(values):
    return jax.nn.gelu(values, approximate=False)


def mixer(final, weight_in, weight_out, bias):
    normed = final * lax.rsqrt(jnp.mean(final * final, axis=-1, keepdims=True) + RMS_EPSILON)
    hidden = activate(
        lax.dot_general(
            normed, weight_in, NT, precision=HIGHEST, preferred_element_type=F32
        )
    )
    return jnp.dot(hidden, weight_out, precision=HIGHEST, preferred_element_type=F32) + bias


def turn_tables(positions):
    half = ROT // 2
    frequency = 10000.0 ** (-2.0 * jnp.arange(half, dtype=F32) / ROT)
    angles = positions.astype(F32)[:, None] * frequency[None, :]
    cosine, sine = jnp.cos(angles), jnp.sin(angles)
    count = positions.shape[0]
    rest = HD - ROT
    base = jnp.concatenate([cosine, cosine, jnp.ones((count, rest), F32)], axis=1)
    up = jnp.concatenate([jnp.zeros((count, half), F32), sine, jnp.zeros((count, rest), F32)], 1)
    down = jnp.concatenate([-sine, jnp.zeros((count, half + rest), F32)], axis=1)
    return base, up, down


def group_coeff(mix_in, count_prev, tokens):
    groups = tokens // GROUP
    c = mix_in.reshape(STREAMS, count_prev, groups, GROUP).transpose(2, 1, 3, 0)
    return c.reshape(groups, count_prev * GROUP, STREAMS)


def body(
    earlier,
    mix_in,
    lengths,
    w_query,
    w_key,
    w_value,
    w_proj,
    w_up,
    w_down,
    first_gain,
    first_shift,
    second_gain,
    second_shift,
    mixer_in,
    mixer_out,
    mixer_bias,
    grad_out,
    grad_mix,
):
    count_prev, rows, span, width = earlier.shape
    tokens = rows * span
    fsdp, ctx = lax.axis_size("fsdp"), lax.axis_size("ctx")
    me, z = lax.axis_index("fsdp"), lax.axis_index("ctx")
    masks = block_masks(fsdp)
    place_of = [masks.index(m) for m in range(fsdp)]
    block = width // fsdp
    piece = block // ctx
    heads_width = w_query.shape[1]
    hidden = w_up.shape[1]
    perm = jnp.stack([me ^ m for m in masks]).astype(jnp.int32)
    table = jnp.array(place_of, jnp.int32)
    ring = jnp.arange(ctx, dtype=jnp.int32)
    source = (z - ring + ctx) % ctx
    slots = z * span + jnp.arange(span, dtype=jnp.int32)
    valid = (slots[None, :] < lengths[:, None]).astype(F32).reshape(tokens)

    def relative(values):
        return jnp.concatenate(
            [
                lax.dynamic_slice_in_dim(values, perm[p] * block, block, values.ndim - 1)
                for p in range(fsdp)
            ],
            axis=-1,
        )

    def absolute(values):
        return jnp.concatenate(
            [
                lax.dynamic_slice_in_dim(values, table[a ^ me] * block, block, values.ndim - 1)
                for a in range(fsdp)
            ],
            axis=-1,
        )

    def part(values, p):
        return values[:, p * block : (p + 1) * block]

    small = jnp.concatenate(
        [mixer_in.T, first_gain[None], first_shift[None], second_gain[None], second_shift[None]], 0
    )
    around = jnp.zeros((ctx,) + small.shape, BF16)
    for s in range(ctx):
        got = small if s == 0 else shift_ctx(small, s)
        around = lax.dynamic_update_slice(around, got[None], (source[s], 0, 0))
    around = cross(around)
    around = jnp.stack(around + [over_fsdp(a, 1) for a in around])
    small_all = around.transpose(2, 0, 1, 3).reshape(small.shape[0], width).astype(F32)
    mixer_full = small_all[:MIXW]
    gain_first, shift_first, gain_second, shift_second = [
        small_all[MIXW + n : MIXW + n + 1] for n in range(4)
    ]

    half = hidden // 2
    ctx_qkv = gather_ctx(jnp.concatenate([w_query, w_key, w_value], axis=1))
    ctx_both = gather_ctx(jnp.concatenate([w_up, w_proj.T], axis=1))

    order = Order()
    Pace.value = FORWARD_PACE
    inputs = earlier.reshape(count_prev, tokens, width)
    coeff = group_coeff(mix_in, count_prev, tokens)
    normed_in, streams = order.keep(
        mix_streams(perm, inputs, coeff, gain_first, shift_first)
    )
    tables_here = turn_tables(jnp.tile(slots, rows))
    tables_all = turn_tables(jnp.arange(span * ctx, dtype=jnp.int32))
    target = (z + ring) % ctx
    tables_here, tables_all = order.wait((tables_here, tables_all))

    def to_heads(chunks):
        return [chunks[0]] + [shift_ctx(chunks[s], s) for s in range(1, ctx)]

    def to_slots(pieces):
        return [pieces[0]] + [shift_ctx(pieces[s], -s) for s in range(1, ctx)]

    def to_core(parts):
        return [over_fsdp(p, 1) for p in parts]

    near_qkv = cross(order.wait(ctx_qkv))
    far_qkv = to_core(near_qkv[:1])
    other = [over_tp(near_qkv[0])]
    far_qkv = order.wait(far_qkv)
    other = order.wait(other)
    near_qkv = order.wait(near_qkv)
    far_qkv = order.wait(far_qkv + to_core(near_qkv[1:]))
    blocks_qkv = near_qkv + far_qkv
    pieces = to_heads(
        order.keep(to_chunks(target, perm, order(normed_in), blocks_qkv, tables_here, 2))
    )
    other = other + [over_tp(p) for p in near_qkv[1:]]
    near_both = cross(order.wait(ctx_both))
    pieces = order.wait(pieces)
    other = order.wait(other)
    outs = to_slots(order.keep(attend(source, lengths, order(pieces))))
    ctx_down = [
        gather_ctx(order.keep(shard_part(order(w_down), n, half, True))) for n in range(2)
    ]
    outs = order.wait(outs)
    attended = order.keep(join(target, order(outs)))[0]
    near_both = order.wait(near_both)
    near_proj = order.wait([b[:, hidden:] for b in near_both])
    blocks_proj = near_proj + order.wait(to_core(near_proj))
    branch_mine = order.keep(to_width([order(attended)], [blocks_proj], width))
    branch_theirs = over_tp(branch_mine)
    near_down = [cross(order.wait(ctx_down[0]))]
    blocks_up = near_both + order.wait(to_core(order(near_both)))
    near_down.append(cross(order.wait(ctx_down[1])))
    branch_theirs = order.wait(branch_theirs)
    residual = streams[STREAMS - 1] + tp_sum(branch_mine, branch_theirs)

    def far_half(values):
        return over_fsdp(values[..., width // 2 :], 1)

    normed = layer_norm(residual, gain_second, shift_second).astype(BF16)
    normed = order.wait(normed)
    near_down[0] = order.wait(near_down[0])
    far_down = [to_core(near_down[0])]
    active, slope = [], []
    for n in range(2):
        a, b = order.keep(up_stage(perm, order(normed), blocks_up, n, half))
        active.append(a)
        slope.append(b)
    far_down[0] = order.wait(far_down[0])
    down_first = order.keep(
        to_width([order(active[0])], [near_down[0] + far_down[0]], width, (), F32)
    )
    near_down[1] = order.wait(near_down[1])
    far_down.append(order.wait(to_core(near_down[1])))
    blocks_down = [near + far for near, far in zip(near_down, far_down)]
    down_mine = order.keep(
        to_width([order(active[1])], blocks_down[1:], width, (down_first,))
    )
    other_far = to_core(other)
    down_theirs = over_tp(down_mine)
    active_far = [over_fsdp(a, 1) for a in order(active)]
    grad_out_here = order.wait(relative(grad_out.reshape(tokens, width)))
    active_far = order.wait(active_far)
    normed_far = order.wait(far_half(normed))
    attended_far = order.wait(over_fsdp(attended, 1))
    normed_in_far = order.wait(far_half(normed_in))
    other = other + order.wait(other_far)
    final = residual + tp_sum(down_mine, order.wait(down_theirs))
    output = absolute(final.astype(BF16)).reshape(rows, span, width)

    mix_value, mix_pull = jax.vjp(mixer, final, mixer_full, mixer_out, mixer_bias)
    mix_out = mix_value.T.reshape(MIXW, rows, span)
    mix_cotangent = (grad_mix.reshape(MIXW, tokens) * valid[None]).T
    grad_final_mix, grad_mixer_first, grad_mixer_second, grad_mixer_shift = mix_pull(mix_cotangent)
    grad_final = grad_out_here.astype(F32) * valid[:, None] + grad_final_mix

    Pace.value = BACKWARD_PACE
    grad_down_b = order.wait(grad_final.astype(BF16))
    grad_down_far = order.wait(far_half(grad_down_b))
    down = [
        Scatter(order, grad_down_b[None], [a[None]], grad_down_far[None], [f[None]])
        for a, f in zip(active, active_far)
    ]
    for d in down:
        d.launch()
    grad_upward, upward_far = [], []
    for n in range(2):
        grad_upward.append(
            order.keep(up_back(perm, order(grad_down_b), slope[n], blocks_down[n], 0))
        )
        upward_far.append(over_fsdp(grad_upward[n], 1))
    normed_mine = order.keep(to_width(order(grad_upward), [blocks_up] * 2, width, (), BF16, (0, 1)))
    normed_theirs = over_tp(normed_mine)
    grad_down = [scatter_ctx(down[0].finish())]
    upward_far = order.wait(upward_far)
    up = [
        Scatter(order, normed[None], [u[None]], normed_far[None], [f[None]])
        for u, f in zip(grad_upward, upward_far)
    ]
    up[0].launch()
    tail = jnp.concatenate([grad_mixer_second, grad_mixer_shift[None]], axis=0)
    tail, grad_mixer_first, output, mix_out = order.wait(
        (tail, grad_mixer_first, output, mix_out)
    )
    normed_theirs = order.wait(normed_theirs)
    grad_normed = tp_sum(normed_mine, normed_theirs)
    unused_norm, norm_pull = jax.vjp(layer_norm, residual, gain_second, shift_second)
    grad_residual_norm, grad_gain_second, grad_shift_second = norm_pull(grad_normed)
    grad_branch_b = order.wait((grad_final + grad_residual_norm).astype(BF16))

    grad_branch_far = far_half(grad_branch_b)
    grad_chunks = order.keep(
        to_chunks(target, perm, order(grad_branch_b)[None], blocks_proj, tables_here, 0)
    )
    grad_branch_far = order.wait(grad_branch_far)
    grad_pieces = to_heads(grad_chunks)
    grad_down.append(scatter_ctx(down[1].finish()))
    up[1].launch()
    proj = Scatter(
        order, grad_branch_b[None], [attended[None]], grad_branch_far[None], [attended_far[None]]
    )
    made_proj = proj.make(1)
    grad_up = [scatter_ctx(up[0].finish())]
    proj.launch(0, None, order(made_proj))
    grad_pieces = order.wait(grad_pieces)
    back = [
        order.keep(attend_back(source, lengths, pieces, order(grad_pieces), tables_all, 0))
    ]
    sent = [to_slots(back[0])]
    back.append(
        order.keep(attend_back(source, lengths, pieces, order(grad_pieces), tables_all, 1))
    )
    grad_down[0] = order.wait(grad_down[0])
    mine, theirs, own = [], [], []
    sent[0] = order.wait(sent[0])
    mine.append(order.keep(join(target, sent[0])))
    theirs.append(over_tp(mine[0]))
    sent.append(to_slots(order(back[1])))
    own.append(order.keep(own_part(perm, order(mine[0]), streams, blocks_qkv, 0)))
    grad_down[1] = order.wait(grad_down[1])
    sent[1] = order.wait(sent[1])
    mine.append(order.keep(join(target, sent[1])))
    theirs.append(over_tp(mine[1]))
    mine_far = [over_fsdp(m, 1) for m in order(mine)]
    grad_proj = scatter_ctx(proj.finish())
    grad_up.append(scatter_ctx(up[1].finish()))
    mine_far = order.wait(mine_far)
    qkv = Scatter(order, normed_in, mine, normed_in_far, mine_far)
    qkv.launch(0, 1)
    qkv.launch(1, 2)
    own.append(order.keep(own_part(perm, order(mine[1]), streams, blocks_qkv, 1)))
    grad_up[0] = order.wait(grad_up[0])
    theirs[0] = order.wait(theirs[0])
    grad_query = scatter_ctx(qkv.finish(0, 1))
    sums = (own[0][1] + own[1][1]).sum(0).reshape(2, 8, width).sum(1)
    sums = order.wait(sums)

    dz = order.keep(other_part(order(theirs[0]), own[0][0], streams, gain_first, other, 0))
    done = order.keep(
        last_stage(perm, inputs, coeff, order(dz), grad_branch_b, 0, rows, ())
    )
    grad_proj = order.wait(grad_proj)
    theirs[1] = order.wait(theirs[1])
    grad_rest = scatter_ctx(qkv.finish(1, 2))
    Pace.value = FORWARD_PACE
    sums_far = over_tp(order(sums))
    dz = order.keep(other_part(order(theirs[1]), own[1][0], streams, gain_first, other, 1))
    sums_far = order.wait(sums_far)
    packed = jnp.concatenate(
        [grad_mixer_first, sums + sums_far, grad_gain_second, grad_shift_second], axis=0
    )
    packed = packed.reshape(packed.shape[0], fsdp, ctx, piece)
    packed = jnp.stack(
        [lax.dynamic_index_in_dim(packed, z ^ m, 2, keepdims=False) for m in block_masks(ctx)]
    ).transpose(0, 2, 1, 3)
    tail = jnp.pad(tail, ((0, 0), (0, HD - MIXW)))
    packed, tail = order.wait((packed, tail))

    def fold(packed, tail, move):
        split = packed.shape[0] // 2
        return packed[:split], tail, move(packed[split:]), move(tail)

    def landed(packed, tail, got_packed, got_tail):
        got_packed, got_tail = order.wait((got_packed, got_tail))
        return packed + got_packed, tail + got_tail

    ctx_steps = [
        (lambda v, bit=bit: lax.ppermute(v, "ctx", xor_pairs(ctx, bit)))
        for bit in reversed(bits_of(ctx))
    ]
    fsdp_steps = [(lambda v, bit=bit: over_fsdp(v, bit)) for bit in reversed(bits_of(fsdp))]
    moving = fold(packed, tail, ctx_steps[0])
    grad_up[1] = order.wait(grad_up[1])
    for step in ctx_steps[1:]:
        moving = fold(*landed(*moving), step)
    grad_inputs, grad_coeff = order.keep(
        last_stage(perm, inputs, coeff, order(dz), grad_branch_b, 1, rows, done)
    )
    packed, tail = landed(*moving)
    moving = fold(packed[0], tail, fsdp_steps[0])
    for step in fsdp_steps[1:]:
        moving = fold(*landed(*moving), step)
    packed, tail = landed(*moving)
    norms = packed[0]
    grad_key, grad_value = jnp.split(grad_rest, 2, axis=1)
    grad_proj = grad_proj.T
    grad_earlier = grad_inputs.reshape(earlier.shape)
    grad_mix_in = (
        grad_coeff[:, :, :STREAMS]
        .reshape(tokens // GROUP, count_prev, GROUP, STREAMS)
        .transpose(3, 1, 0, 2)
        .reshape(mix_in.shape)
    )
    return (
        output,
        mix_out,
        grad_earlier,
        grad_mix_in,
        grad_query,
        grad_key,
        grad_value,
        grad_proj,
        jnp.concatenate(grad_up, axis=1),
        jnp.concatenate(grad_down, axis=1).T,
        norms[MIXW],
        norms[MIXW + 1],
        norms[MIXW + 2],
        norms[MIXW + 3],
        norms[:MIXW].T,
        tail[:MIXW, :MIXW],
        tail[MIXW, :MIXW],
    )


def solution(mesh):
    placed = (
        P(None, "fsdp", "ctx", None),
        P(None, "fsdp", "ctx"),
        P("fsdp"),
        P(("fsdp", "ctx"), "tp"),
        P(("fsdp", "ctx"), "tp"),
        P(("fsdp", "ctx"), "tp"),
        P("tp", ("fsdp", "ctx")),
        P(("fsdp", "ctx"), "tp"),
        P("tp", ("fsdp", "ctx")),
        P(("fsdp", "ctx")),
        P(("fsdp", "ctx")),
        P(("fsdp", "ctx")),
        P(("fsdp", "ctx")),
        P(("fsdp", "ctx"), None),
        P(),
        P(),
        P("fsdp", "ctx", None),
        P(None, "fsdp", "ctx"),
    )
    return jax.shard_map(
        body,
        mesh=mesh,
        in_specs=placed,
        out_specs=(
            P("fsdp", "ctx", None),
            P(None, "fsdp", "ctx"),
            P(None, "fsdp", "ctx", None),
            P(None, "fsdp", "ctx"),
            P(("fsdp", "ctx"), "tp"),
            P(("fsdp", "ctx"), "tp"),
            P(("fsdp", "ctx"), "tp"),
            P("tp", ("fsdp", "ctx")),
            P(("fsdp", "ctx"), "tp"),
            P("tp", ("fsdp", "ctx")),
            P(("fsdp", "ctx")),
            P(("fsdp", "ctx")),
            P(("fsdp", "ctx")),
            P(("fsdp", "ctx")),
            P(("fsdp", "ctx"), None),
            P(),
            P(),
        ),
        check_vma=False,
    )
```

```python
from functools import partial
import math

import jax
import jax.numpy as jnp
from jax import lax
from jax.experimental import pallas as pl
from jax.experimental.pallas import tpu as pltpu
from jax.sharding import PartitionSpec as P

HD = 128
ROT = 32
STREAMS = 4
MIXW = 36
EPSILON = 1e-05
RMS_EPSILON = 1e-06
HIGHEST = lax.Precision.HIGHEST
NEGATIVE = -1e30
F32 = jnp.float32
BF16 = jnp.bfloat16
GROUP = 32
FORWARD_PACE = 3.0e7
BACKWARD_PACE = 1.5e9


def params(grid_rank):
    return pltpu.CompilerParams(
        dimension_semantics=("arbitrary",) * grid_rank, vmem_limit_bytes=56 * 1024 * 1024
    )


class Pace:
    value = FORWARD_PACE


def cost(time):
    return pl.CostEstimate(flops=int(time * Pace.value), transcendentals=0, bytes_accessed=1024)


def xor_pairs(size, mask):
    return [(i, i ^ mask) for i in range(size)]


def over_fsdp(values, mask):
    return lax.ppermute(values, "fsdp", xor_pairs(lax.axis_size("fsdp"), mask))


def over_tp(values):
    return lax.ppermute(values, "tp", xor_pairs(lax.axis_size("tp"), 1))


def shift_ctx(values, step):
    size = lax.axis_size("ctx")
    return lax.ppermute(values, "ctx", [(i, (i + step) % size) for i in range(size)])


def bits_of(size):
    return [1 << b for b in reversed(range(size.bit_length() - 1))]


def block_masks(size):
    masks = [0]
    for bit in bits_of(size):
        masks = masks + [m ^ bit for m in masks]
    return masks


def after(values, *earlier):
    return lax.optimization_barrier((values, earlier))[0]


class Order:
    def __init__(self):
        self.last = ()

    def __call__(self, values):
        return after(values, self.last)

    def keep(self, values):
        self.last = values
        return values

    def wait(self, values):
        return self.keep(self(values))


def gather_ctx(shard):
    return lax.all_gather(shard, "ctx", axis=0, tiled=True)


def cross(own):
    parts = [own]
    for bit in bits_of(lax.axis_size("fsdp"))[:-1]:
        parts = parts + [over_fsdp(p, bit) for p in parts]
    return parts


class Scatter:
    def __init__(self, order, left, rights, left_far, rights_far):
        self.order, self.left, self.far, self.rights = order, left, left_far, (rights, rights_far)
        self.count = lax.axis_size("fsdp")
        self.received = [[] for _ in range(self.count)]

    def blocks(self, chosen, first, kinds):
        near, far = self.order(self.rights)
        added = [[r for r in self.received[p] if r[2] == first] for p in chosen]
        made = grad_blocks(self.left, self.far, near, far, self.count, chosen, added, first, kinds)
        return self.order.keep(made)

    def make(self, level, first=0, kinds=None):
        half = self.count >> (level + 1)
        chosen = list(range(half, 2 * half))
        return self.blocks(chosen, first, kinds or self.left.shape[0])

    def send(self, level, made, first=0):
        half = self.count >> (level + 1)
        bit = bits_of(self.count)[::-1][level]
        got = over_fsdp(made, bit)
        for n in range(half):
            self.received[n].append((got, n, first))
        return got

    def launch(self, first=0, kinds=None, made=None):
        for level in range(1, len(bits_of(self.count))):
            if made is None:
                made = self.make(level, first, kinds)
            self.send(level, made, first)
            made = None

    def finish(self, first=0, kinds=None):
        return self.blocks([0], first, kinds or self.left.shape[0])[0]


def scatter_ctx(total):
    return lax.psum_scatter(total, "ctx", scatter_dimension=0, tiled=True).astype(F32)


def tp_sum(mine, theirs):
    return mine.astype(F32) + theirs.astype(F32)


NT = (((1,), (1,)), ((), ()))
TN = (((0,), (0,)), ((), ()))


def spread(coeff):
    count = coeff.shape[0]
    token = lax.broadcasted_iota(jnp.int32, (count, STREAMS * GROUP), 0) % GROUP
    lane = lax.broadcasted_iota(jnp.int32, (count, STREAMS * GROUP), 1)
    out = jnp.zeros((count, STREAMS * GROUP), F32)
    for s in range(STREAMS):
        out = jnp.where(lane == token + s * GROUP, coeff[:, s : s + 1], out)
    high = out.astype(BF16)
    return high, (out - high.astype(F32)).astype(BF16)


def mix_kernel(perm_ref, earlier_ref, coeff_ref, gain_ref, shift_ref, a_ref, z_ref):
    prev, tile, width = earlier_ref.shape
    parts = perm_ref.shape[0]
    block = width // parts
    for g in range(tile // GROUP):
        rows = slice(g * GROUP, (g + 1) * GROUP)
        high, low = spread(coeff_ref[g])
        for p in range(parts):
            source = pl.ds(pl.multiple_of(perm_ref[p] * block, 128), block)
            x = earlier_ref[:, rows, source].reshape(prev * GROUP, block)
            z_ref[:, rows, p * block : (p + 1) * block] = (
                lax.dot_general(high, x, TN, preferred_element_type=F32)
                + lax.dot_general(low, x, TN, preferred_element_type=F32)
            ).reshape(STREAMS, GROUP, block)
        for s in range(STREAMS - 1):
            z = z_ref[s, rows, :]
            center = z - jnp.mean(z, axis=-1, keepdims=True)
            spread_of = jnp.mean(center * center, axis=-1, keepdims=True)
            a_ref[s, rows, :] = (
                center * lax.rsqrt(spread_of + EPSILON) * gain_ref[...] + shift_ref[...]
            ).astype(BF16)


def mix_streams(perm, inputs, coeff, gain, shift, tile=64):
    prev, tokens, width = inputs.shape
    return pl.pallas_call(
        mix_kernel,
        name="mix",
        grid_spec=pltpu.PrefetchScalarGridSpec(
            num_scalar_prefetch=1,
            grid=(tokens // tile,),
            in_specs=[
                pl.BlockSpec((prev, tile, width), lambda t, *_: (0, t, 0)),
                pl.BlockSpec((tile // GROUP,) + coeff.shape[1:], lambda t, *_: (t, 0, 0)),
                pl.BlockSpec((1, width), lambda t, *_: (0, 0)),
                pl.BlockSpec((1, width), lambda t, *_: (0, 0)),
            ],
            out_specs=[
                pl.BlockSpec((STREAMS - 1, tile, width), lambda t, *_: (0, t, 0)),
                pl.BlockSpec((STREAMS, tile, width), lambda t, *_: (0, t, 0)),
            ],
        ),
        out_shape=[
            jax.ShapeDtypeStruct((STREAMS - 1, tokens, width), BF16),
            jax.ShapeDtypeStruct((STREAMS, tokens, width), F32),
        ],
        cost_estimate=cost(14),
        compiler_params=params(1),
    )(perm, inputs, coeff, gain, shift)


def turn(values, tables, sign):
    base, up, down = tables
    return (
        values * base
        + sign * (pltpu.roll(values, ROT // 2, 1) * up)
        + sign * (pltpu.roll(values, HD - ROT // 2, 1) * down)
    )


def blocks_dot(a_ref, weights):
    parts = len(weights)
    block = a_ref.shape[-1] // parts
    total = None
    for p in range(parts):
        term = jnp.dot(
            a_ref[:, p * block : (p + 1) * block], weights[p][...], preferred_element_type=F32
        )
        total = term if total is None else total + term
    return total


def block_specs(weights, rows, columns, at):
    return [pl.BlockSpec((rows, columns), lambda *ids: (0, at(*ids)))] * len(weights)


def heads_kernel(target_ref, perm_ref, a_ref, *refs, parts, turned):
    weights = refs[:parts]
    tables = refs[parts : parts + 3]
    outs = refs[parts + 3 :]
    total = blocks_dot(a_ref.at[0], weights)
    kind, step = pl.program_id(0), pl.program_id(1)
    for s, out_ref in enumerate(outs):

        @pl.when((step == s) & (kind < turned))
        def _():
            tabs = [t[...] for t in tables]
            for h in range(total.shape[1] // HD):
                cols = slice(h * HD, (h + 1) * HD)
                out_ref[0, :, cols] = turn(total[:, cols], tabs, 1.0).astype(BF16)

        @pl.when((step == s) & (kind >= turned))
        def _():
            out_ref[0] = total.astype(BF16)


def to_chunks(target, perm, a, weights, tables, turned):
    kinds, tokens, width = a.shape
    parts = perm.shape[0]
    chunks = target.shape[0]
    columns = weights[0].shape[1] // chunks // kinds
    specs = block_specs(
        weights, width // parts, columns, lambda s, n, target, _: s * chunks + target[n]
    )
    return pl.pallas_call(
        partial(heads_kernel, parts=parts, turned=turned),
        name="heads",
        grid_spec=pltpu.PrefetchScalarGridSpec(
            num_scalar_prefetch=2,
            grid=(kinds, chunks),
            in_specs=[pl.BlockSpec((1, tokens, width), lambda s, n, *_: (s, 0, 0))]
            + specs
            + [pl.BlockSpec((tokens, HD), lambda s, n, *_: (0, 0))] * 3,
            out_specs=[pl.BlockSpec((1, tokens, columns), lambda s, n, *_: (s, 0, 0))] * chunks,
        ),
        out_shape=[jax.ShapeDtypeStruct((kinds, tokens, columns), BF16)] * chunks,
        cost_estimate=cost(2 * kinds * chunks),
        compiler_params=params(2),
    )(target, perm, a, *weights, *tables)


def join_kernel(target_ref, *refs):
    for s in range(len(refs) - 1):

        @pl.when(pl.program_id(0) == s)
        def _():
            refs[-1][...] = refs[s][...]


def join(target, pieces):
    kinds, count, columns = pieces[0].shape
    chunks = len(pieces)
    return pl.pallas_call(
        join_kernel,
        name="join",
        grid_spec=pltpu.PrefetchScalarGridSpec(
            num_scalar_prefetch=1,
            grid=(chunks,),
            in_specs=[pl.BlockSpec((kinds, count, columns), lambda n, _: (0, 0, 0))] * chunks,
            out_specs=pl.BlockSpec((kinds, count, columns), lambda n, target: (0, 0, target[n])),
        ),
        out_shape=jax.ShapeDtypeStruct((kinds, count, columns * chunks), BF16),
        cost_estimate=cost(2),
        compiler_params=params(1),
    )(target, *pieces)


def weights_of(query, keys, tile_index, tile, length, scale):
    count = keys.shape[0]
    scores = (
        lax.dot_general(query, keys, (((1,), (1,)), ((), ())), preferred_element_type=F32) * scale
    )
    row = tile_index * tile + lax.broadcasted_iota(jnp.int32, (tile, count), 0)
    col = lax.broadcasted_iota(jnp.int32, (tile, count), 1)
    masked = jnp.where((col <= row) & (col < length), scores, NEGATIVE)
    expo = jnp.exp(masked - jnp.max(masked, axis=-1, keepdims=True))
    return expo / jnp.sum(expo, axis=-1, keepdims=True)


def collect(source_ref, pieces, scratch, span):
    for s, piece in enumerate(pieces):
        at = pl.ds(pl.multiple_of(source_ref[s] * span, span), span)
        scratch[at, :] = piece[...]


def spread_out(source_ref, scratch, pieces, span):
    for s, piece in enumerate(pieces):
        at = pl.ds(pl.multiple_of(source_ref[s] * span, span), span)
        piece[...] = scratch[at, :]


def collect(source_ref, pieces, kind, scratch):
    span = pieces[0].shape[1]
    for s, piece in enumerate(pieces):
        at = pl.ds(pl.multiple_of(source_ref[s] * span, span), span)
        scratch[at, :] = piece[kind]


def spread_out(source_ref, scratch, pieces, kind):
    span = pieces[0].shape[1]
    for s, piece in enumerate(pieces):
        at = pl.ds(pl.multiple_of(source_ref[s] * span, span), span)
        piece[kind] = scratch[at, :]


def attend_kernel(source_ref, length_ref, *refs, chunks):
    ins, outs = refs[:chunks], refs[chunks : 2 * chunks]
    q_all, k_all, v_all, o_all = refs[2 * chunks :]
    span = ins[0].shape[1]
    length = length_ref[pl.program_id(0)]
    scale = 1.0 / math.sqrt(HD)
    for kind, scratch in enumerate((q_all, k_all, v_all)):
        collect(source_ref, ins, kind, scratch)
    for h in range(q_all.shape[1] // HD):
        cols = slice(h * HD, (h + 1) * HD)
        for i in range(chunks):
            rows = slice(i * span, (i + 1) * span)
            seen = slice(0, (i + 1) * span)
            probs = weights_of(q_all[rows, cols], k_all[seen, cols], i, span, length, scale)
            o_all[rows, cols] = jnp.dot(
                probs.astype(BF16), v_all[seen, cols], preferred_element_type=F32
            ).astype(BF16)
    spread_out(source_ref, o_all, outs, 0)


def attend(source, lengths, pieces):
    chunks = len(pieces)
    rows = lengths.shape[0]
    kinds, tokens, columns = pieces[0].shape
    span = tokens // rows
    return pl.pallas_call(
        partial(attend_kernel, chunks=chunks),
        name="attend",
        grid_spec=pltpu.PrefetchScalarGridSpec(
            num_scalar_prefetch=2,
            grid=(rows,),
            in_specs=[pl.BlockSpec((kinds, span, columns), lambda r, *_: (0, r, 0))] * chunks,
            out_specs=[pl.BlockSpec((1, span, columns), lambda r, *_: (0, r, 0))] * chunks,
            scratch_shapes=[pltpu.VMEM((span * chunks, columns), BF16)] * 4,
        ),
        out_shape=[jax.ShapeDtypeStruct((1, tokens, columns), BF16)] * chunks,
        cost_estimate=cost(6 * rows),
        compiler_params=params(1),
    )(source, lengths, *pieces)


def attend_back_kernel(source_ref, length_ref, *refs, chunks, row):
    ins, grads = refs[:chunks], refs[chunks : 2 * chunks]
    tabs = refs[2 * chunks : 2 * chunks + 3]
    outs = refs[2 * chunks + 3 : 3 * chunks + 3]
    q_all, k_all, v_all, g_all, dk_sum, dv_sum, dq_all, dk_all, dv_all = refs[3 * chunks + 3 :]
    span = ins[0].shape[1]
    length = length_ref[row]
    scale = 1.0 / math.sqrt(HD)
    for kind, scratch in enumerate((q_all, k_all, v_all)):
        collect(source_ref, ins, kind, scratch)
    collect(source_ref, grads, 0, g_all)
    for h in range(q_all.shape[1] // HD):
        cols = slice(h * HD, (h + 1) * HD)
        for i in reversed(range(chunks)):
            rows = slice(i * span, (i + 1) * span)
            seen = slice(0, (i + 1) * span)
            query, grad = q_all[rows, cols], g_all[rows, cols]
            keys, values = k_all[seen, cols], v_all[seen, cols]
            probs = weights_of(query, keys, i, span, length, scale)
            grad_probs = lax.dot_general(grad, values, NT, preferred_element_type=F32)
            delta = jnp.sum(probs * grad_probs, axis=-1, keepdims=True)
            scores = (probs * (grad_probs - delta) * scale).astype(BF16)
            turned = [t[rows, :] for t in tabs]
            dq_all[rows, cols] = turn(
                jnp.dot(scores, keys, preferred_element_type=F32), turned, -1.0
            ).astype(BF16)
            dk = lax.dot_general(scores, query, TN, preferred_element_type=F32)
            dv = lax.dot_general(probs.astype(BF16), grad, TN, preferred_element_type=F32)
            if i == chunks - 1:
                dk_sum[...] = dk
                dv_sum[...] = dv
            else:
                dk_sum[seen, :] += dk
                dv_sum[seen, :] += dv
        dk_all[:, cols] = turn(dk_sum[...], [t[...] for t in tabs], -1.0).astype(BF16)
        dv_all[:, cols] = dv_sum[...].astype(BF16)
    for kind, scratch in enumerate((dq_all, dk_all, dv_all)):
        spread_out(source_ref, scratch, outs, kind)


def attend_back(source, lengths, pieces, grads, tables, row):
    chunks = len(pieces)
    rows = lengths.shape[0]
    kinds, tokens, columns = pieces[0].shape
    span = tokens // rows
    seq = span * chunks
    wide = pltpu.VMEM((seq, columns), BF16)
    return pl.pallas_call(
        partial(attend_back_kernel, chunks=chunks, row=row),
        name="attend_back",
        grid_spec=pltpu.PrefetchScalarGridSpec(
            num_scalar_prefetch=2,
            grid=(1,),
            in_specs=[pl.BlockSpec((kinds, span, columns), lambda r, *_: (0, row, 0))] * chunks
            + [pl.BlockSpec((1, span, columns), lambda r, *_: (0, row, 0))] * chunks
            + [pl.BlockSpec((seq, HD), lambda r, *_: (0, 0))] * 3,
            out_specs=[pl.BlockSpec((kinds, span, columns), lambda r, *_: (0, 0, 0))] * chunks,
            scratch_shapes=[wide] * 4 + [pltpu.VMEM((seq, HD), F32)] * 2 + [wide] * 3,
        ),
        out_shape=[jax.ShapeDtypeStruct((kinds, span, columns), BF16)] * chunks,
        cost_estimate=cost(12),
        compiler_params=params(1),
    )(source, lengths, *pieces, *grads, *tables)


def up_kernel(perm_ref, a_ref, *refs, parts):
    weights = refs[:parts]
    active_ref, slope_ref = refs[parts:]
    u = blocks_dot(a_ref, weights)
    half = 0.5 * (1.0 + lax.erf(u * math.sqrt(0.5)))
    active_ref[...] = (u * half).astype(BF16)
    slope_ref[...] = half + u * jnp.exp(-0.5 * u * u) * (1.0 / math.sqrt(2.0 * math.pi))


def up_stage(perm, a, weights, part, columns, tile=512):
    tokens, width = a.shape
    parts = perm.shape[0]
    tile = min(tile, columns)
    specs = block_specs(weights, width // parts, tile, lambda n, *_: part * (columns // tile) + n)
    out = pl.BlockSpec((tokens, tile), lambda n, *_: (0, n))
    return pl.pallas_call(
        partial(up_kernel, parts=parts),
        name="up",
        grid_spec=pltpu.PrefetchScalarGridSpec(
            num_scalar_prefetch=1,
            grid=(columns // tile,),
            in_specs=[pl.BlockSpec((tokens, width), lambda n, *_: (0, 0))] + specs,
            out_specs=[out, out],
        ),
        out_shape=[
            jax.ShapeDtypeStruct((tokens, columns), BF16),
            jax.ShapeDtypeStruct((tokens, columns), F32),
        ],
        cost_estimate=cost(columns / 200),
        compiler_params=params(1),
    )(perm, a, *weights)


def up_back_kernel(perm_ref, a_ref, slope_ref, *refs, parts):
    weights = refs[:parts]
    refs[parts][...] = (blocks_dot(a_ref, weights) * slope_ref[...]).astype(BF16)


def up_back(perm, a, slope, weights, offset, tile=512):
    tokens, width = a.shape
    parts = perm.shape[0]
    columns = slope.shape[1]
    tile = min(tile, columns)
    specs = block_specs(
        weights, width // parts, tile, lambda n, *_: offset // tile + n
    )
    out = pl.BlockSpec((tokens, tile), lambda n, *_: (0, n))
    return pl.pallas_call(
        partial(up_back_kernel, parts=parts),
        name="up_back",
        grid_spec=pltpu.PrefetchScalarGridSpec(
            num_scalar_prefetch=1,
            grid=(columns // tile,),
            in_specs=[pl.BlockSpec((tokens, width), lambda n, *_: (0, 0)), out] + specs,
            out_specs=out,
        ),
        out_shape=jax.ShapeDtypeStruct((tokens, columns), BF16),
        cost_estimate=cost(columns / 200),
        compiler_params=params(1),
    )(perm, a, slope, *weights)


def back_kernel(*refs, lefts, parts, adds):
    out_ref = refs[-1]
    block = out_ref.shape[1] // parts
    tile = refs[lefts].shape[0]
    n = pl.program_id(0)
    for p in range(parts):
        at = pl.ds(pl.multiple_of(p * block + n * tile, 128), tile)
        total = refs[-2][:, at] if adds else None
        for h in range(lefts):
            term = lax.dot_general(
                refs[h][...], refs[lefts + h * parts + p][...], NT, preferred_element_type=F32
            )
            total = term if total is None else total + term
        out_ref[:, at] = total.astype(out_ref.dtype)


def to_width(lefts, weights, width, added=(), dtype=BF16, across=(0,)):
    parts = len(weights[0])
    block = width // parts
    tile = min(block, 256)
    tokens = lefts[0].shape[0]
    left_specs, specs, arrays = [], [], []
    for left, weight, at in zip(lefts, weights, across):
        columns = left.shape[1]
        left_specs.append(pl.BlockSpec((tokens, columns), lambda n: (0, 0)))
        specs += [pl.BlockSpec((tile, columns), lambda n, at=at: (n, at))] * parts
        arrays += weight
    whole = pl.BlockSpec((tokens, width), lambda n: (0, 0))
    return pl.pallas_call(
        partial(back_kernel, lefts=len(lefts), parts=parts, adds=len(added)),
        name="to_width",
        grid=(block // tile,),
        in_specs=left_specs + specs + [whole] * len(added),
        out_specs=whole,
        out_shape=jax.ShapeDtypeStruct((tokens, width), dtype),
        cost_estimate=cost(sum(a.shape[1] for a in lefts) / 256),
        compiler_params=params(1),
    )(*lefts, *arrays, *added)


def grad_kernel(*refs, count, rights, adds):
    lefts, fars = refs[:count], refs[count : 2 * count]
    sides = refs[2 * count : 2 * count + rights], refs[2 * count + rights : 2 * count + 2 * rights]
    add_refs, out_ref = refs[2 * count + 2 * rights : -1], refs[-1]
    at = 0
    for b in range(count):
        total = None
        for left, right_refs in zip((lefts[b], fars[b]), sides):
            start = 0
            for right in right_refs:
                size = right.shape[1]
                term = lax.dot_general(
                    left[0, start : start + size, :], right[0], TN, preferred_element_type=F32
                )
                total = term if total is None else total + term
                start += size
        for n in range(adds[b]):
            total = total + add_refs[at + n][0].astype(F32)
        at += adds[b]
        out_ref[b] = total.astype(BF16)


def grad_blocks(left, left_far, near, far, parts, chosen, added, first, kinds, tile=512):
    _, tokens, width = left.shape
    columns = near[0].shape[2]
    tile = min(tile, columns)
    steps = columns // tile
    block = width // parts

    def place(start, row):
        return lambda s, n: (row, 0, (first - start + s) * steps + n)

    flat = [a for arrays in added for a in arrays]
    left_specs = [
        pl.BlockSpec((1, tokens, block), lambda s, n, p=p: (first + s, 0, p)) for p in chosen
    ]
    return pl.pallas_call(
        partial(
            grad_kernel,
            count=len(chosen),
            rights=len(near),
            adds=tuple(len(a) for a in added),
        ),
        name="grad",
        grid=(kinds, steps),
        in_specs=left_specs * 2
        + [
            pl.BlockSpec((1, r.shape[1], tile), lambda s, n: (first + s, 0, n))
            for r in (*near, *far)
        ]
        + [pl.BlockSpec((1, block, tile), place(start, row)) for _, row, start in flat],
        out_specs=pl.BlockSpec((len(chosen), block, tile), lambda s, n: (0, 0, s * steps + n)),
        out_shape=jax.ShapeDtypeStruct((len(chosen), block, kinds * columns), BF16),
        cost_estimate=cost(len(chosen) * kinds * columns / 512),
        compiler_params=params(2),
    )(*[left] * len(chosen), *[left_far] * len(chosen), *near, *far, *[a for a, _, _ in flat])


def part_kernel(in_ref, out_ref, *, turned):
    values = in_ref[...]
    out_ref[...] = values.astype(F32).T.astype(BF16) if turned else values


def shard_part(shard, n, size, turned):
    short = shard.shape[1] if turned else shard.shape[0]
    spec = pl.BlockSpec((size, short), lambda i: (n, 0))
    if not turned:
        spec = pl.BlockSpec((short, size), lambda i: (0, n))
    return pl.pallas_call(
        partial(part_kernel, turned=turned),
        name="part",
        grid=(1,),
        in_specs=[spec],
        out_specs=pl.BlockSpec((short, size), lambda i: (0, 0)),
        out_shape=jax.ShapeDtypeStruct((short, size), BF16),
        cost_estimate=cost(1),
        compiler_params=params(1),
    )(shard)


def hat_of(z):
    center = z - jnp.mean(z, axis=-1, keepdims=True)
    inverse = lax.rsqrt(jnp.mean(center * center, axis=-1, keepdims=True) + EPSILON)
    return center * inverse, inverse


def own_kernel(perm_ref, grad_ref, z_ref, *refs, parts):
    weights = refs[:parts]
    out_ref, sum_ref = refs[parts:]
    block = weights[0].shape[0]
    for p in range(parts):
        out_ref[0, :, p * block : (p + 1) * block] = lax.dot_general(
            grad_ref[0], weights[p][...], NT, preferred_element_type=F32
        )
    tile = 32
    tokens, width = out_ref.shape[1:]
    gain = jnp.zeros((8, width), F32)
    shift = jnp.zeros((8, width), F32)
    for t in range(0, tokens, tile):
        d = out_ref[0, t : t + tile, :]
        hat, _ = hat_of(z_ref[0, t : t + tile, :])
        gain = gain + jnp.sum((d * hat).reshape(tile // 8, 8, width), axis=0)
        shift = shift + jnp.sum(d.reshape(tile // 8, 8, width), axis=0)
    sum_ref[0, :8] = gain
    sum_ref[0, 8:] = shift


def own_part(perm, grads, streams, weights, row):
    kinds, span, columns = grads.shape
    width = streams.shape[2]
    parts = perm.shape[0]
    specs = block_specs(weights, width // parts, columns, lambda s, *_: s)
    return pl.pallas_call(
        partial(own_kernel, parts=parts),
        name="own",
        grid_spec=pltpu.PrefetchScalarGridSpec(
            num_scalar_prefetch=1,
            grid=(kinds,),
            in_specs=[
                pl.BlockSpec((1, span, columns), lambda s, *_: (s, 0, 0)),
                pl.BlockSpec((1, span, width), lambda s, *_: (s, row, 0)),
            ]
            + specs,
            out_specs=[
                pl.BlockSpec((1, span, width), lambda s, *_: (s, 0, 0)),
                pl.BlockSpec((1, 16, width), lambda s, *_: (s, 0, 0)),
            ],
        ),
        out_shape=[
            jax.ShapeDtypeStruct((kinds, span, width), F32),
            jax.ShapeDtypeStruct((kinds, 16, width), F32),
        ],
        cost_estimate=cost(12),
        compiler_params=params(1),
    )(perm, grads, streams, *weights)


def other_kernel(grad_ref, part_ref, z_ref, gain_ref, *refs, parts):
    weights = refs[:parts]
    out_ref, total_ref = refs[parts:]
    block = weights[0].shape[0]
    for p in range(parts):
        cols = slice(p * block, (p + 1) * block)
        total_ref[:, cols] = part_ref[0, :, cols] + lax.dot_general(
            grad_ref[0], weights[p][...], NT, preferred_element_type=F32
        )
    tile = 32
    for t in range(0, total_ref.shape[0], tile):
        rows = slice(t, t + tile)
        hat, inverse = hat_of(z_ref[0, rows, :])
        e = total_ref[rows, :] * gain_ref[...]
        first = jnp.mean(e, axis=-1, keepdims=True)
        second = jnp.mean(e * hat, axis=-1, keepdims=True)
        out_ref[0, rows, :] = ((e - first - hat * second) * inverse).astype(BF16)


def other_part(grads, own, streams, gain, weights, row):
    kinds, span, columns = grads.shape
    width = streams.shape[2]
    parts = len(weights)
    block = width // parts
    return pl.pallas_call(
        partial(other_kernel, parts=parts),
        name="other",
        grid=(kinds,),
        in_specs=[
            pl.BlockSpec((1, span, columns), lambda s: (s, 0, 0)),
            pl.BlockSpec((1, span, width), lambda s: (s, 0, 0)),
            pl.BlockSpec((1, span, width), lambda s: (s, row, 0)),
            pl.BlockSpec((1, width), lambda s: (0, 0)),
        ]
        + [pl.BlockSpec((block, columns), lambda s: (0, s))] * parts,
        out_specs=pl.BlockSpec((1, span, width), lambda s: (s, 0, 0)),
        out_shape=jax.ShapeDtypeStruct((kinds, span, width), BF16),
        scratch_shapes=[pltpu.VMEM((span, width), F32)],
        cost_estimate=cost(14),
        compiler_params=params(1),
    )(grads, own, streams, gain, *weights)


def last_kernel(perm_ref, earlier_ref, coeff_ref, dz_ref, dr_ref, *refs):
    out_ref, mix_ref = refs[-2:]
    prev, tile, width = earlier_ref.shape
    parts = perm_ref.shape[0]
    block = width // parts
    count, half = prev * GROUP, STREAMS * GROUP
    for g in range(tile // GROUP):
        rows = slice(g * GROUP, (g + 1) * GROUP)
        high, low = spread(coeff_ref[g])
        pairs = jnp.zeros((count, half), F32)
        for p in range(parts):
            here = slice(p * block, (p + 1) * block)
            there = pl.ds(pl.multiple_of(perm_ref[p] * block, 128), block)
            grads = jnp.concatenate(
                [dz_ref[s, rows, here] for s in range(STREAMS - 1)] + [dr_ref[rows, here]], axis=0
            )
            x = earlier_ref[:, rows, there].reshape(count, block)
            pairs = pairs + lax.dot_general(x, grads, NT, preferred_element_type=F32)
            total = jnp.dot(high, grads, preferred_element_type=F32) + jnp.dot(
                low, grads, preferred_element_type=F32
            )
            out_ref[:, rows, there] = total.astype(BF16).reshape(prev, GROUP, block)
        token = lax.broadcasted_iota(jnp.int32, (count, half), 0) % GROUP
        lane = lax.broadcasted_iota(jnp.int32, (count, half), 1)
        wide = lax.broadcasted_iota(jnp.int32, (count, 128), 1)
        mixed = jnp.zeros((count, 128), F32)
        for s in range(STREAMS):
            own = jnp.where(lane == token + s * GROUP, pairs, 0.0)
            mixed = jnp.where(wide == s, jnp.sum(own, axis=-1, keepdims=True), mixed)
        mix_ref[g] = mixed


def last_stage(perm, inputs, coeff, dz, dr, row, rows, before, tile=64):
    prev, tokens, width = inputs.shape
    steps = tokens // rows // tile
    count = prev * GROUP
    here = lambda t, *_: (0, row * steps + t, 0)
    return pl.pallas_call(
        last_kernel,
        name="last",
        grid_spec=pltpu.PrefetchScalarGridSpec(
            num_scalar_prefetch=1,
            grid=(steps,),
            in_specs=[
                pl.BlockSpec((prev, tile, width), here),
                pl.BlockSpec(
                    (tile // GROUP,) + coeff.shape[1:], lambda t, *_: (row * steps + t, 0, 0)
                ),
                pl.BlockSpec((STREAMS - 1, tile, width), lambda t, *_: (0, t, 0)),
                pl.BlockSpec((tile, width), lambda t, *_: (row * steps + t, 0)),
            ]
            + [pl.BlockSpec(memory_space=pl.ANY)] * len(before),
            out_specs=[
                pl.BlockSpec((prev, tile, width), here),
                pl.BlockSpec(
                    (tile // GROUP, count, 128), lambda t, *_: (row * steps + t, 0, 0)
                ),
            ],
        ),
        out_shape=[
            jax.ShapeDtypeStruct((prev, tokens, width), BF16),
            jax.ShapeDtypeStruct((tokens // GROUP, count, 128), F32),
        ],
        input_output_aliases={5 + n: n for n in range(len(before))},
        cost_estimate=cost(12),
        compiler_params=params(1),
    )(perm, inputs, coeff, dz, dr, *before)


def two_terms(values):
    high = values.astype(BF16)
    return high, (values - high.astype(F32)).astype(BF16)


def final_kernel(res_ref, mine_ref, theirs_ref, out_ref, cot_ref, valid_ref, in_ref, mix_ref, *refs):
    final_ref, grad_ref, low_ref, far_ref, high_ref, rest_ref, back_ref, inverse_ref = refs
    tile, width = res_ref.shape
    step = 16
    for t in range(0, tile, step):
        rows = slice(t, t + step)
        final = res_ref[rows, :] + (
            mine_ref[rows, :].astype(F32) + theirs_ref[rows, :].astype(F32)
        )
        inverse = lax.rsqrt(jnp.mean(final * final, axis=-1, keepdims=True) + RMS_EPSILON)
        final_ref[rows, :] = final
        inverse_ref[rows, :] = jnp.broadcast_to(inverse, (step, HD))
        high_ref[rows, :], rest_ref[rows, :] = two_terms(final * inverse)
    pre = sum(
        lax.dot_general(n[...], in_ref[...], NT, preferred_element_type=F32)
        for n in (high_ref, rest_ref)
    )
    grad_pre = lax.dot_general(
        cot_ref[...], mix_ref[...], NT, precision=HIGHEST, preferred_element_type=F32
    ) * (
        0.5 * (1.0 + lax.erf(pre * math.sqrt(0.5)))
        + pre * jnp.exp(-0.5 * pre * pre) * (1.0 / math.sqrt(2.0 * math.pi))
    )
    back_ref[...] = sum(
        jnp.dot(g, in_ref[...], preferred_element_type=F32) for g in two_terms(grad_pre)
    )
    for t in range(0, tile, step):
        rows = slice(t, t + step)
        inverse = inverse_ref[rows, :1]
        normed = final_ref[rows, :] * inverse
        grad = back_ref[rows, :]
        grad = inverse * (grad - normed * jnp.mean(grad * normed, axis=-1, keepdims=True))
        grad = out_ref[rows, :].astype(F32) * valid_ref[rows, :] + grad
        grad_ref[rows, :] = grad
        low = grad.astype(BF16)
        low_ref[rows, :] = low
        far_ref[rows, :] = low[:, width // 2 :]


def final_stage(residual, mine, theirs, grad_out, cotangent, valid, weight_in, weight_out, tile=128):
    tokens, width = residual.shape
    rows = pl.BlockSpec((tile, width), lambda t: (t, 0))
    cotangent = jnp.pad(cotangent, ((0, 0), (0, HD - MIXW)))
    weight_in = jnp.pad(weight_in, ((0, HD - MIXW), (0, 0))).astype(BF16)
    weight_out = jnp.pad(weight_out, ((0, HD - MIXW), (0, HD - MIXW)))
    return pl.pallas_call(
        final_kernel,
        name="final",
        grid=(tokens // tile,),
        in_specs=[
            rows,
            rows,
            rows,
            rows,
            pl.BlockSpec((tile, HD), lambda t: (t, 0)),
            pl.BlockSpec((tile, 1), lambda t: (t, 0)),
            pl.BlockSpec((HD, width), lambda t: (0, 0)),
            pl.BlockSpec((HD, HD), lambda t: (0, 0)),
        ],
        out_specs=[rows, rows, rows, pl.BlockSpec((tile, width // 2), lambda t: (t, 0))],
        out_shape=[
            jax.ShapeDtypeStruct((tokens, width), F32),
            jax.ShapeDtypeStruct((tokens, width), F32),
            jax.ShapeDtypeStruct((tokens, width), BF16),
            jax.ShapeDtypeStruct((tokens, width // 2), BF16),
        ],
        scratch_shapes=[
            pltpu.VMEM((tile, width), BF16),
            pltpu.VMEM((tile, width), BF16),
            pltpu.VMEM((tile, width), F32),
            pltpu.VMEM((tile, HD), F32),
        ],
        cost_estimate=cost(8),
        compiler_params=params(1),
    )(residual, mine, theirs, grad_out, cotangent, valid, weight_in, weight_out)


def second_kernel(res_ref, mine_ref, theirs_ref, grad_ref, gain_ref, out_ref, sum_ref):
    @pl.when(pl.program_id(0) == 0)
    def _():
        sum_ref[...] = jnp.zeros_like(sum_ref)

    step = 32
    width = res_ref.shape[1]
    for t in range(0, res_ref.shape[0], step):
        rows = slice(t, t + step)
        hat, inverse = hat_of(res_ref[rows, :])
        d = mine_ref[rows, :].astype(F32) + theirs_ref[rows, :].astype(F32)
        sum_ref[:8] += jnp.sum((d * hat).reshape(step // 8, 8, width), axis=0)
        sum_ref[8:] += jnp.sum(d.reshape(step // 8, 8, width), axis=0)
        e = d * gain_ref[...]
        first = jnp.mean(e, axis=-1, keepdims=True)
        second = jnp.mean(e * hat, axis=-1, keepdims=True)
        out_ref[rows, :] = (grad_ref[rows, :] + (e - first - hat * second) * inverse).astype(BF16)


def second_norm_back(residual, mine, theirs, grad, gain, tile=128):
    tokens, width = residual.shape
    rows = pl.BlockSpec((tile, width), lambda t: (t, 0))
    return pl.pallas_call(
        second_kernel,
        name="second",
        grid=(tokens // tile,),
        in_specs=[rows, rows, rows, rows, pl.BlockSpec((1, width), lambda t: (0, 0))],
        out_specs=[rows, pl.BlockSpec((16, width), lambda t: (0, 0))],
        out_shape=[
            jax.ShapeDtypeStruct((tokens, width), BF16),
            jax.ShapeDtypeStruct((16, width), F32),
        ],
        cost_estimate=cost(6),
        compiler_params=params(1),
    )(residual, mine, theirs, grad, gain)


def layer_norm(values, gain, shift):
    center = values - jnp.mean(values, axis=-1, keepdims=True)
    spread = jnp.mean(center * center, axis=-1, keepdims=True)
    return center * lax.rsqrt(spread + EPSILON) * gain + shift


def activate(values):
    return jax.nn.gelu(values, approximate=False)


def mixer(final, weight_in, weight_out, bias):
    normed = final * lax.rsqrt(jnp.mean(final * final, axis=-1, keepdims=True) + RMS_EPSILON)
    hidden = activate(
        lax.dot_general(
            normed, weight_in, NT, precision=HIGHEST, preferred_element_type=F32
        )
    )
    return jnp.dot(hidden, weight_out, precision=HIGHEST, preferred_element_type=F32) + bias


def turn_tables(positions):
    half = ROT // 2
    frequency = 10000.0 ** (-2.0 * jnp.arange(half, dtype=F32) / ROT)
    angles = positions.astype(F32)[:, None] * frequency[None, :]
    cosine, sine = jnp.cos(angles), jnp.sin(angles)
    count = positions.shape[0]
    rest = HD - ROT
    base = jnp.concatenate([cosine, cosine, jnp.ones((count, rest), F32)], axis=1)
    up = jnp.concatenate([jnp.zeros((count, half), F32), sine, jnp.zeros((count, rest), F32)], 1)
    down = jnp.concatenate([-sine, jnp.zeros((count, half + rest), F32)], axis=1)
    return base, up, down


def group_coeff(mix_in, count_prev, tokens):
    groups = tokens // GROUP
    c = mix_in.reshape(STREAMS, count_prev, groups, GROUP).transpose(2, 1, 3, 0)
    return c.reshape(groups, count_prev * GROUP, STREAMS)


def body(
    earlier,
    mix_in,
    lengths,
    w_query,
    w_key,
    w_value,
    w_proj,
    w_up,
    w_down,
    first_gain,
    first_shift,
    second_gain,
    second_shift,
    mixer_in,
    mixer_out,
    mixer_bias,
    grad_out,
    grad_mix,
):
    count_prev, rows, span, width = earlier.shape
    tokens = rows * span
    fsdp, ctx = lax.axis_size("fsdp"), lax.axis_size("ctx")
    me, z = lax.axis_index("fsdp"), lax.axis_index("ctx")
    masks = block_masks(fsdp)
    place_of = [masks.index(m) for m in range(fsdp)]
    block = width // fsdp
    piece = block // ctx
    heads_width = w_query.shape[1]
    hidden = w_up.shape[1]
    perm = jnp.stack([me ^ m for m in masks]).astype(jnp.int32)
    table = jnp.array(place_of, jnp.int32)
    ring = jnp.arange(ctx, dtype=jnp.int32)
    source = (z - ring + ctx) % ctx
    slots = z * span + jnp.arange(span, dtype=jnp.int32)
    valid = (slots[None, :] < lengths[:, None]).astype(F32).reshape(tokens)

    def relative(values):
        return jnp.concatenate(
            [
                lax.dynamic_slice_in_dim(values, perm[p] * block, block, values.ndim - 1)
                for p in range(fsdp)
            ],
            axis=-1,
        )

    def absolute(values):
        return jnp.concatenate(
            [
                lax.dynamic_slice_in_dim(values, table[a ^ me] * block, block, values.ndim - 1)
                for a in range(fsdp)
            ],
            axis=-1,
        )

    def part(values, p):
        return values[:, p * block : (p + 1) * block]

    small = jnp.concatenate(
        [mixer_in.T, first_gain[None], first_shift[None], second_gain[None], second_shift[None]], 0
    )
    around = jnp.zeros((ctx,) + small.shape, BF16)
    for s in range(ctx):
        got = small if s == 0 else shift_ctx(small, s)
        around = lax.dynamic_update_slice(around, got[None], (source[s], 0, 0))
    around = cross(around)
    around = jnp.stack(around + [over_fsdp(a, 1) for a in around])
    small_all = around.transpose(2, 0, 1, 3).reshape(small.shape[0], width).astype(F32)
    mixer_full = small_all[:MIXW]
    gain_first, shift_first, gain_second, shift_second = [
        small_all[MIXW + n : MIXW + n + 1] for n in range(4)
    ]

    half = hidden // 2
    ctx_qkv = gather_ctx(jnp.concatenate([w_query, w_key, w_value], axis=1))
    ctx_both = gather_ctx(jnp.concatenate([w_up, w_proj.T], axis=1))

    order = Order()
    Pace.value = FORWARD_PACE
    inputs = earlier.reshape(count_prev, tokens, width)
    coeff = group_coeff(mix_in, count_prev, tokens)
    def far_half(values):
        return over_fsdp(values[..., width // 2 :], 1)

    normed_in, streams = order.keep(
        mix_streams(perm, inputs, coeff, gain_first, shift_first)
    )
    tables_here = turn_tables(jnp.tile(slots, rows))
    tables_all = turn_tables(jnp.arange(span * ctx, dtype=jnp.int32))
    target = (z + ring) % ctx
    tables_here, tables_all = order.wait((tables_here, tables_all))
    normed_in_far = order.wait(far_half(order(normed_in)))

    def to_heads(chunks):
        return [chunks[0]] + [shift_ctx(chunks[s], s) for s in range(1, ctx)]

    def to_slots(pieces):
        return [pieces[0]] + [shift_ctx(pieces[s], -s) for s in range(1, ctx)]

    def to_core(parts):
        return [over_fsdp(p, 1) for p in parts]

    near_qkv = cross(order.wait(ctx_qkv))
    far_qkv = to_core(near_qkv[:1])
    other = [over_tp(near_qkv[0])]
    far_qkv = order.wait(far_qkv)
    other = order.wait(other)
    near_qkv = order.wait(near_qkv)
    far_qkv = order.wait(far_qkv + to_core(near_qkv[1:]))
    blocks_qkv = near_qkv + far_qkv
    pieces = to_heads(
        order.keep(to_chunks(target, perm, order(normed_in), blocks_qkv, tables_here, 2))
    )
    other = other + [over_tp(p) for p in near_qkv[1:]]
    near_both = cross(order.wait(ctx_both))
    pieces = order.wait(pieces)
    other = order.wait(other)
    outs = to_slots(order.keep(attend(source, lengths, order(pieces))))
    ctx_down = [
        gather_ctx(order.keep(shard_part(order(w_down), n, half, True))) for n in range(2)
    ]
    outs = order.wait(outs)
    attended = order.keep(join(target, order(outs)))[0]
    near_both = order.wait(near_both)
    near_proj = order.wait([b[:, hidden:] for b in near_both])
    blocks_proj = near_proj + order.wait(to_core(near_proj))
    near_down = [cross(order.wait(ctx_down[0]))]
    far_both = to_core(order(near_both))
    branch_mine = order.keep(to_width([order(attended)], [blocks_proj], width))
    branch_theirs = over_tp(branch_mine)
    blocks_up = near_both + order.wait(far_both)
    near_down[0] = order.wait(near_down[0])
    near_down.append(cross(order.wait(ctx_down[1])))
    branch_theirs = order.wait(branch_theirs)
    residual = streams[STREAMS - 1] + tp_sum(branch_mine, branch_theirs)

    normed = layer_norm(residual, gain_second, shift_second).astype(BF16)
    normed = order.wait(normed)
    far_down = [to_core(near_down[0])]
    other_far = to_core(other)
    active, slope = [], []
    for n in range(2):
        a, b = order.keep(up_stage(perm, order(normed), blocks_up, n, half))
        active.append(a)
        slope.append(b)
    far_down[0] = order.wait(far_down[0])
    other = other + order.wait(other_far)
    down_first = order.keep(
        to_width([order(active[0])], [near_down[0] + far_down[0]], width, (), F32)
    )
    near_down[1] = order.wait(near_down[1])
    far_down.append(order.wait(to_core(near_down[1])))
    blocks_down = [near + far for near, far in zip(near_down, far_down)]
    down_mine = order.keep(
        to_width([order(active[1])], blocks_down[1:], width, (down_first,))
    )
    down_theirs = over_tp(down_mine)
    grad_out_here = order.wait(relative(grad_out.reshape(tokens, width)))
    mix_cotangent = order.wait((grad_mix.reshape(MIXW, tokens) * valid[None]).T)
    down_theirs = order.wait(down_theirs)

    final, grad_final, grad_down_b, grad_down_near = order.keep(
        final_stage(
            residual,
            down_mine,
            order(down_theirs),
            grad_out_here,
            mix_cotangent,
            valid[:, None],
            mixer_full,
            mixer_out,
        )
    )

    Pace.value = BACKWARD_PACE
    active_far = [over_fsdp(a, 1) for a in active]
    normed_far = far_half(normed)
    attended_far = over_fsdp(attended, 1)
    grad_down_far = over_fsdp(grad_down_near, 1)
    active_far, normed_far, attended_far, grad_down_far = order.wait(
        (active_far, normed_far, attended_far, grad_down_far)
    )
    down = [
        Scatter(order, grad_down_b[None], [a[None]], grad_down_far[None], [f[None]])
        for a, f in zip(active, active_far)
    ]
    for d in down:
        d.launch()
    grad_upward, upward_far = [], []
    for n in range(2):
        grad_upward.append(
            order.keep(up_back(perm, order(grad_down_b), slope[n], blocks_down[n], 0))
        )
        upward_far.append(over_fsdp(grad_upward[n], 1))
    normed_mine = order.keep(to_width(order(grad_upward), [blocks_up] * 2, width, (), BF16, (0, 1)))
    normed_theirs = over_tp(normed_mine)
    Pace.value = 3 * BACKWARD_PACE
    grad_down = [scatter_ctx(down[0].finish())]
    Pace.value = BACKWARD_PACE
    upward_far = order.wait(upward_far)
    up = [
        Scatter(order, normed[None], [u[None]], normed_far[None], [f[None]])
        for u, f in zip(grad_upward, upward_far)
    ]
    up[0].launch()
    mix_value, mix_pull = jax.vjp(
        lambda *weights: mixer(order(final), *weights), mixer_full, mixer_out, mixer_bias
    )
    mix_out = mix_value.T.reshape(MIXW, rows, span)
    grad_mixer_first, grad_mixer_second, grad_mixer_shift = mix_pull(mix_cotangent)
    output = absolute(order(final).astype(BF16)).reshape(rows, span, width)
    tail = jnp.concatenate([grad_mixer_second, grad_mixer_shift[None]], axis=0)
    tail, grad_mixer_first, output, mix_out = order.wait(
        (tail, grad_mixer_first, output, mix_out)
    )
    normed_theirs = order.wait(normed_theirs)
    grad_branch_b, second_sums = order.keep(
        second_norm_back(residual, normed_mine, order(normed_theirs), grad_final, gain_second)
    )
    second_pair = second_sums.reshape(2, 8, width).sum(1)

    grad_branch_far = far_half(grad_branch_b)
    grad_chunks = order.keep(
        to_chunks(target, perm, order(grad_branch_b)[None], blocks_proj, tables_here, 0)
    )
    grad_branch_far = order.wait(grad_branch_far)
    grad_pieces = to_heads(grad_chunks)
    grad_down.append(scatter_ctx(down[1].finish()))
    up[1].launch()
    proj = Scatter(
        order, grad_branch_b[None], [attended[None]], grad_branch_far[None], [attended_far[None]]
    )
    made_proj = proj.make(1)
    grad_up = [scatter_ctx(up[0].finish())]
    proj.launch(0, None, order(made_proj))
    grad_pieces = order.wait(grad_pieces)
    back = [
        order.keep(attend_back(source, lengths, pieces, order(grad_pieces), tables_all, 0))
    ]
    sent = [to_slots(back[0])]
    back.append(
        order.keep(attend_back(source, lengths, pieces, order(grad_pieces), tables_all, 1))
    )
    grad_down[0] = order.wait(grad_down[0])
    mine, theirs, own = [], [], []
    sent[0] = order.wait(sent[0])
    mine.append(order.keep(join(target, sent[0])))
    theirs.append(over_tp(mine[0]))
    sent.append(to_slots(order(back[1])))
    own.append(order.keep(own_part(perm, order(mine[0]), streams, blocks_qkv, 0)))
    grad_down[1] = order.wait(grad_down[1])
    sent[1] = order.wait(sent[1])
    mine.append(order.keep(join(target, sent[1])))
    theirs.append(over_tp(mine[1]))
    mine_far = [over_fsdp(m, 1) for m in order(mine)]
    grad_proj = scatter_ctx(proj.finish())
    grad_up.append(scatter_ctx(up[1].finish()))
    mine_far = order.wait(mine_far)
    qkv = Scatter(order, normed_in, mine, normed_in_far, mine_far)
    qkv.launch(0, 1)
    qkv.launch(1, 2)
    own.append(order.keep(own_part(perm, order(mine[1]), streams, blocks_qkv, 1)))
    grad_up[0] = order.wait(grad_up[0])
    theirs[0] = order.wait(theirs[0])
    grad_query = scatter_ctx(qkv.finish(0, 1))
    sums = (own[0][1] + own[1][1]).sum(0).reshape(2, 8, width).sum(1)
    sums = order.wait(sums)

    dz = order.keep(other_part(order(theirs[0]), own[0][0], streams, gain_first, other, 0))
    done = order.keep(
        last_stage(perm, inputs, coeff, order(dz), grad_branch_b, 0, rows, ())
    )
    grad_proj = order.wait(grad_proj)
    theirs[1] = order.wait(theirs[1])
    grad_rest = scatter_ctx(qkv.finish(1, 2))
    Pace.value = FORWARD_PACE
    sums_far = over_tp(order(sums))
    dz = order.keep(other_part(order(theirs[1]), own[1][0], streams, gain_first, other, 1))
    sums_far = order.wait(sums_far)
    packed = jnp.concatenate(
        [grad_mixer_first, sums + sums_far, second_pair], axis=0
    )
    packed = packed.reshape(packed.shape[0], fsdp, ctx, piece)
    packed = jnp.stack(
        [lax.dynamic_index_in_dim(packed, z ^ m, 2, keepdims=False) for m in block_masks(ctx)]
    ).transpose(0, 2, 1, 3)
    tail = jnp.pad(tail, ((0, 0), (0, HD - MIXW)))
    packed, tail = order.wait((packed, tail))

    def fold(packed, tail, move):
        split = packed.shape[0] // 2
        return packed[:split], tail, move(packed[split:]), move(tail)

    def landed(packed, tail, got_packed, got_tail):
        got_packed, got_tail = order.wait((got_packed, got_tail))
        return packed + got_packed, tail + got_tail

    ctx_steps = [
        (lambda v, bit=bit: lax.ppermute(v, "ctx", xor_pairs(ctx, bit)))
        for bit in reversed(bits_of(ctx))
    ]
    fsdp_steps = [(lambda v, bit=bit: over_fsdp(v, bit)) for bit in reversed(bits_of(fsdp))]
    moving = fold(packed, tail, ctx_steps[0])
    grad_up[1] = order.wait(grad_up[1])
    for step in ctx_steps[1:]:
        moving = fold(*landed(*moving), step)
    grad_inputs, grad_coeff = order.keep(
        last_stage(perm, inputs, coeff, order(dz), grad_branch_b, 1, rows, done)
    )
    packed, tail = landed(*moving)
    moving = fold(packed[0], tail, fsdp_steps[0])
    for step in fsdp_steps[1:]:
        moving = fold(*landed(*moving), step)
    packed, tail = landed(*moving)
    norms = packed[0]
    grad_key, grad_value = jnp.split(grad_rest, 2, axis=1)
    grad_proj = grad_proj.T
    grad_earlier = grad_inputs.reshape(earlier.shape)
    grad_mix_in = (
        grad_coeff[:, :, :STREAMS]
        .reshape(tokens // GROUP, count_prev, GROUP, STREAMS)
        .transpose(3, 1, 0, 2)
        .reshape(mix_in.shape)
    )
    return (
        output,
        mix_out,
        grad_earlier,
        grad_mix_in,
        grad_query,
        grad_key,
        grad_value,
        grad_proj,
        jnp.concatenate(grad_up, axis=1),
        jnp.concatenate(grad_down, axis=1).T,
        norms[MIXW],
        norms[MIXW + 1],
        norms[MIXW + 2],
        norms[MIXW + 3],
        norms[:MIXW].T,
        tail[:MIXW, :MIXW],
        tail[MIXW, :MIXW],
    )


def solution(mesh):
    placed = (
        P(None, "fsdp", "ctx", None),
        P(None, "fsdp", "ctx"),
        P("fsdp"),
        P(("fsdp", "ctx"), "tp"),
        P(("fsdp", "ctx"), "tp"),
        P(("fsdp", "ctx"), "tp"),
        P("tp", ("fsdp", "ctx")),
        P(("fsdp", "ctx"), "tp"),
        P("tp", ("fsdp", "ctx")),
        P(("fsdp", "ctx")),
        P(("fsdp", "ctx")),
        P(("fsdp", "ctx")),
        P(("fsdp", "ctx")),
        P(("fsdp", "ctx"), None),
        P(),
        P(),
        P("fsdp", "ctx", None),
        P(None, "fsdp", "ctx"),
    )
    return jax.shard_map(
        body,
        mesh=mesh,
        in_specs=placed,
        out_specs=(
            P("fsdp", "ctx", None),
            P(None, "fsdp", "ctx"),
            P(None, "fsdp", "ctx", None),
            P(None, "fsdp", "ctx"),
            P(("fsdp", "ctx"), "tp"),
            P(("fsdp", "ctx"), "tp"),
            P(("fsdp", "ctx"), "tp"),
            P("tp", ("fsdp", "ctx")),
            P(("fsdp", "ctx"), "tp"),
            P("tp", ("fsdp", "ctx")),
            P(("fsdp", "ctx")),
            P(("fsdp", "ctx")),
            P(("fsdp", "ctx")),
            P(("fsdp", "ctx")),
            P(("fsdp", "ctx"), None),
            P(),
            P(),
        ),
        check_vma=False,
    )
```

```python
from functools import partial
import math

import jax
import jax.numpy as jnp
from jax import lax
from jax.experimental import pallas as pl
from jax.experimental.pallas import tpu as pltpu
from jax.sharding import PartitionSpec as P

HD = 128
ROT = 32
STREAMS = 4
MIXW = 36
EPSILON = 1e-05
RMS_EPSILON = 1e-06
HIGHEST = lax.Precision.HIGHEST
NEGATIVE = -1e30
F32 = jnp.float32
BF16 = jnp.bfloat16
GROUP = 32
FORWARD_PACE = 3.0e7
BACKWARD_PACE = 1.5e9


def params(grid_rank):
    return pltpu.CompilerParams(
        dimension_semantics=("arbitrary",) * grid_rank, vmem_limit_bytes=56 * 1024 * 1024
    )


class Pace:
    value = FORWARD_PACE


def cost(time):
    return pl.CostEstimate(flops=int(time * Pace.value), transcendentals=0, bytes_accessed=1024)


def xor_pairs(size, mask):
    return [(i, i ^ mask) for i in range(size)]


def over_fsdp(values, mask):
    return lax.ppermute(values, "fsdp", xor_pairs(lax.axis_size("fsdp"), mask))


def over_tp(values):
    return lax.ppermute(values, "tp", xor_pairs(lax.axis_size("tp"), 1))


def shift_ctx(values, step):
    size = lax.axis_size("ctx")
    return lax.ppermute(values, "ctx", [(i, (i + step) % size) for i in range(size)])


def bits_of(size):
    return [1 << b for b in reversed(range(size.bit_length() - 1))]


def block_masks(size):
    masks = [0]
    for bit in bits_of(size):
        masks = masks + [m ^ bit for m in masks]
    return masks


def after(values, *earlier):
    return lax.optimization_barrier((values, earlier))[0]


class Order:
    def __init__(self):
        self.last = ()

    def __call__(self, values):
        return after(values, self.last)

    def keep(self, values):
        self.last = values
        return values

    def wait(self, values):
        return self.keep(self(values))


def gather_ctx(shard):
    return lax.all_gather(shard, "ctx", axis=0, tiled=True)


def cross(own):
    parts = [own]
    for bit in bits_of(lax.axis_size("fsdp"))[:-1]:
        parts = parts + [over_fsdp(p, bit) for p in parts]
    return parts


class Scatter:
    def __init__(self, order, left, rights, left_far, rights_far):
        self.order, self.left, self.far, self.rights = order, left, left_far, (rights, rights_far)
        self.count = lax.axis_size("fsdp")
        self.received = [[] for _ in range(self.count)]

    def blocks(self, chosen, first, kinds):
        near, far = self.order(self.rights)
        added = [[r for r in self.received[p] if r[2] == first] for p in chosen]
        made = grad_blocks(self.left, self.far, near, far, self.count, chosen, added, first, kinds)
        return self.order.keep(made)

    def make(self, level, first=0, kinds=None):
        half = self.count >> (level + 1)
        chosen = list(range(half, 2 * half))
        return self.blocks(chosen, first, kinds or self.left.shape[0])

    def send(self, level, made, first=0):
        half = self.count >> (level + 1)
        bit = bits_of(self.count)[::-1][level]
        got = over_fsdp(made, bit)
        for n in range(half):
            self.received[n].append((got, n, first))
        return got

    def launch(self, first=0, kinds=None, made=None):
        for level in range(1, len(bits_of(self.count))):
            if made is None:
                made = self.make(level, first, kinds)
            self.send(level, made, first)
            made = None

    def finish(self, first=0, kinds=None):
        return self.blocks([0], first, kinds or self.left.shape[0])[0]


def scatter_ctx(total):
    return lax.psum_scatter(total, "ctx", scatter_dimension=0, tiled=True).astype(F32)


def tp_sum(mine, theirs):
    return mine.astype(F32) + theirs.astype(F32)


NT = (((1,), (1,)), ((), ()))
TN = (((0,), (0,)), ((), ()))


def spread(coeff):
    count = coeff.shape[0]
    token = lax.broadcasted_iota(jnp.int32, (count, STREAMS * GROUP), 0) % GROUP
    lane = lax.broadcasted_iota(jnp.int32, (count, STREAMS * GROUP), 1)
    out = jnp.zeros((count, STREAMS * GROUP), F32)
    for s in range(STREAMS):
        out = jnp.where(lane == token + s * GROUP, coeff[:, s : s + 1], out)
    high = out.astype(BF16)
    return high, (out - high.astype(F32)).astype(BF16)


def mix_kernel(perm_ref, earlier_ref, coeff_ref, gain_ref, shift_ref, a_ref, z_ref):
    prev, tile, width = earlier_ref.shape
    parts = perm_ref.shape[0]
    block = width // parts
    for g in range(tile // GROUP):
        rows = slice(g * GROUP, (g + 1) * GROUP)
        high, low = spread(coeff_ref[g])
        for p in range(parts):
            source = pl.ds(pl.multiple_of(perm_ref[p] * block, 128), block)
            x = earlier_ref[:, rows, source].reshape(prev * GROUP, block)
            z_ref[:, rows, p * block : (p + 1) * block] = (
                lax.dot_general(high, x, TN, preferred_element_type=F32)
                + lax.dot_general(low, x, TN, preferred_element_type=F32)
            ).reshape(STREAMS, GROUP, block)
        for s in range(STREAMS - 1):
            z = z_ref[s, rows, :]
            center = z - jnp.mean(z, axis=-1, keepdims=True)
            spread_of = jnp.mean(center * center, axis=-1, keepdims=True)
            a_ref[s, rows, :] = (
                center * lax.rsqrt(spread_of + EPSILON) * gain_ref[...] + shift_ref[...]
            ).astype(BF16)


def mix_streams(perm, inputs, coeff, gain, shift, tile=64):
    prev, tokens, width = inputs.shape
    return pl.pallas_call(
        mix_kernel,
        name="mix",
        grid_spec=pltpu.PrefetchScalarGridSpec(
            num_scalar_prefetch=1,
            grid=(tokens // tile,),
            in_specs=[
                pl.BlockSpec((prev, tile, width), lambda t, *_: (0, t, 0)),
                pl.BlockSpec((tile // GROUP,) + coeff.shape[1:], lambda t, *_: (t, 0, 0)),
                pl.BlockSpec((1, width), lambda t, *_: (0, 0)),
                pl.BlockSpec((1, width), lambda t, *_: (0, 0)),
            ],
            out_specs=[
                pl.BlockSpec((STREAMS - 1, tile, width), lambda t, *_: (0, t, 0)),
                pl.BlockSpec((STREAMS, tile, width), lambda t, *_: (0, t, 0)),
            ],
        ),
        out_shape=[
            jax.ShapeDtypeStruct((STREAMS - 1, tokens, width), BF16),
            jax.ShapeDtypeStruct((STREAMS, tokens, width), F32),
        ],
        cost_estimate=cost(14),
        compiler_params=params(1),
    )(perm, inputs, coeff, gain, shift)


def turn(values, tables, sign):
    base, up, down = tables
    return (
        values * base
        + sign * (pltpu.roll(values, ROT // 2, 1) * up)
        + sign * (pltpu.roll(values, HD - ROT // 2, 1) * down)
    )


def blocks_dot(a_ref, weights):
    parts = len(weights)
    block = a_ref.shape[-1] // parts
    total = None
    for p in range(parts):
        term = jnp.dot(
            a_ref[:, p * block : (p + 1) * block], weights[p][...], preferred_element_type=F32
        )
        total = term if total is None else total + term
    return total


def block_specs(weights, rows, columns, at):
    return [pl.BlockSpec((rows, columns), lambda *ids: (0, at(*ids)))] * len(weights)


def heads_kernel(target_ref, perm_ref, a_ref, *refs, parts, turned):
    weights = refs[:parts]
    tables = refs[parts : parts + 3]
    outs = refs[parts + 3 :]
    total = blocks_dot(a_ref.at[0], weights)
    kind, step = pl.program_id(0), pl.program_id(1)
    for s, out_ref in enumerate(outs):

        @pl.when((step == s) & (kind < turned))
        def _():
            tabs = [t[...] for t in tables]
            for h in range(total.shape[1] // HD):
                cols = slice(h * HD, (h + 1) * HD)
                out_ref[0, :, cols] = turn(total[:, cols], tabs, 1.0).astype(BF16)

        @pl.when((step == s) & (kind >= turned))
        def _():
            out_ref[0] = total.astype(BF16)


def to_chunks(target, perm, a, weights, tables, turned):
    kinds, tokens, width = a.shape
    parts = perm.shape[0]
    chunks = target.shape[0]
    columns = weights[0].shape[1] // chunks // kinds
    specs = block_specs(
        weights, width // parts, columns, lambda s, n, target, _: s * chunks + target[n]
    )
    return pl.pallas_call(
        partial(heads_kernel, parts=parts, turned=turned),
        name="heads",
        grid_spec=pltpu.PrefetchScalarGridSpec(
            num_scalar_prefetch=2,
            grid=(kinds, chunks),
            in_specs=[pl.BlockSpec((1, tokens, width), lambda s, n, *_: (s, 0, 0))]
            + specs
            + [pl.BlockSpec((tokens, HD), lambda s, n, *_: (0, 0))] * 3,
            out_specs=[pl.BlockSpec((1, tokens, columns), lambda s, n, *_: (s, 0, 0))] * chunks,
        ),
        out_shape=[jax.ShapeDtypeStruct((kinds, tokens, columns), BF16)] * chunks,
        cost_estimate=cost(2 * kinds * chunks),
        compiler_params=params(2),
    )(target, perm, a, *weights, *tables)


def join_kernel(target_ref, *refs):
    for s in range(len(refs) - 1):

        @pl.when(pl.program_id(0) == s)
        def _():
            refs[-1][...] = refs[s][...]


def join(target, pieces):
    kinds, count, columns = pieces[0].shape
    chunks = len(pieces)
    return pl.pallas_call(
        join_kernel,
        name="join",
        grid_spec=pltpu.PrefetchScalarGridSpec(
            num_scalar_prefetch=1,
            grid=(chunks,),
            in_specs=[pl.BlockSpec((kinds, count, columns), lambda n, _: (0, 0, 0))] * chunks,
            out_specs=pl.BlockSpec((kinds, count, columns), lambda n, target: (0, 0, target[n])),
        ),
        out_shape=jax.ShapeDtypeStruct((kinds, count, columns * chunks), BF16),
        cost_estimate=cost(2),
        compiler_params=params(1),
    )(target, *pieces)


def weights_of(query, keys, tile_index, tile, length, scale):
    count = keys.shape[0]
    scores = (
        lax.dot_general(query, keys, (((1,), (1,)), ((), ())), preferred_element_type=F32) * scale
    )
    row = tile_index * tile + lax.broadcasted_iota(jnp.int32, (tile, count), 0)
    col = lax.broadcasted_iota(jnp.int32, (tile, count), 1)
    masked = jnp.where((col <= row) & (col < length), scores, NEGATIVE)
    expo = jnp.exp(masked - jnp.max(masked, axis=-1, keepdims=True))
    return expo / jnp.sum(expo, axis=-1, keepdims=True)


def collect(source_ref, pieces, scratch, span):
    for s, piece in enumerate(pieces):
        at = pl.ds(pl.multiple_of(source_ref[s] * span, span), span)
        scratch[at, :] = piece[...]


def spread_out(source_ref, scratch, pieces, span):
    for s, piece in enumerate(pieces):
        at = pl.ds(pl.multiple_of(source_ref[s] * span, span), span)
        piece[...] = scratch[at, :]


def collect(source_ref, pieces, kind, scratch):
    span = pieces[0].shape[1]
    for s, piece in enumerate(pieces):
        at = pl.ds(pl.multiple_of(source_ref[s] * span, span), span)
        scratch[at, :] = piece[kind]


def spread_out(source_ref, scratch, pieces, kind):
    span = pieces[0].shape[1]
    for s, piece in enumerate(pieces):
        at = pl.ds(pl.multiple_of(source_ref[s] * span, span), span)
        piece[kind] = scratch[at, :]


def attend_kernel(source_ref, length_ref, *refs, chunks):
    ins, outs = refs[:chunks], refs[chunks : 2 * chunks]
    q_all, k_all, v_all, o_all = refs[2 * chunks :]
    span = ins[0].shape[1]
    length = length_ref[pl.program_id(0)]
    scale = 1.0 / math.sqrt(HD)
    for kind, scratch in enumerate((q_all, k_all, v_all)):
        collect(source_ref, ins, kind, scratch)
    for h in range(q_all.shape[1] // HD):
        cols = slice(h * HD, (h + 1) * HD)
        for i in range(chunks):
            rows = slice(i * span, (i + 1) * span)
            seen = slice(0, (i + 1) * span)
            probs = weights_of(q_all[rows, cols], k_all[seen, cols], i, span, length, scale)
            o_all[rows, cols] = jnp.dot(
                probs.astype(BF16), v_all[seen, cols], preferred_element_type=F32
            ).astype(BF16)
    spread_out(source_ref, o_all, outs, 0)


def attend(source, lengths, pieces):
    chunks = len(pieces)
    rows = lengths.shape[0]
    kinds, tokens, columns = pieces[0].shape
    span = tokens // rows
    return pl.pallas_call(
        partial(attend_kernel, chunks=chunks),
        name="attend",
        grid_spec=pltpu.PrefetchScalarGridSpec(
            num_scalar_prefetch=2,
            grid=(rows,),
            in_specs=[pl.BlockSpec((kinds, span, columns), lambda r, *_: (0, r, 0))] * chunks,
            out_specs=[pl.BlockSpec((1, span, columns), lambda r, *_: (0, r, 0))] * chunks,
            scratch_shapes=[pltpu.VMEM((span * chunks, columns), BF16)] * 4,
        ),
        out_shape=[jax.ShapeDtypeStruct((1, tokens, columns), BF16)] * chunks,
        cost_estimate=cost(6 * rows),
        compiler_params=params(1),
    )(source, lengths, *pieces)


def attend_back_kernel(source_ref, length_ref, *refs, chunks, row):
    ins, grads = refs[:chunks], refs[chunks : 2 * chunks]
    tabs = refs[2 * chunks : 2 * chunks + 3]
    outs = refs[2 * chunks + 3 : 3 * chunks + 3]
    q_all, k_all, v_all, g_all, dk_sum, dv_sum, dq_all, dk_all, dv_all = refs[3 * chunks + 3 :]
    span = ins[0].shape[1]
    length = length_ref[row]
    scale = 1.0 / math.sqrt(HD)
    for kind, scratch in enumerate((q_all, k_all, v_all)):
        collect(source_ref, ins, kind, scratch)
    collect(source_ref, grads, 0, g_all)
    for h in range(q_all.shape[1] // HD):
        cols = slice(h * HD, (h + 1) * HD)
        for i in reversed(range(chunks)):
            rows = slice(i * span, (i + 1) * span)
            seen = slice(0, (i + 1) * span)
            query, grad = q_all[rows, cols], g_all[rows, cols]
            keys, values = k_all[seen, cols], v_all[seen, cols]
            probs = weights_of(query, keys, i, span, length, scale)
            grad_probs = lax.dot_general(grad, values, NT, preferred_element_type=F32)
            delta = jnp.sum(probs * grad_probs, axis=-1, keepdims=True)
            scores = (probs * (grad_probs - delta) * scale).astype(BF16)
            turned = [t[rows, :] for t in tabs]
            dq_all[rows, cols] = turn(
                jnp.dot(scores, keys, preferred_element_type=F32), turned, -1.0
            ).astype(BF16)
            dk = lax.dot_general(scores, query, TN, preferred_element_type=F32)
            dv = lax.dot_general(probs.astype(BF16), grad, TN, preferred_element_type=F32)
            if i == chunks - 1:
                dk_sum[...] = dk
                dv_sum[...] = dv
            else:
                dk_sum[seen, :] += dk
                dv_sum[seen, :] += dv
        dk_all[:, cols] = turn(dk_sum[...], [t[...] for t in tabs], -1.0).astype(BF16)
        dv_all[:, cols] = dv_sum[...].astype(BF16)
    for kind, scratch in enumerate((dq_all, dk_all, dv_all)):
        spread_out(source_ref, scratch, outs, kind)


def attend_back(source, lengths, pieces, grads, tables, row):
    chunks = len(pieces)
    rows = lengths.shape[0]
    kinds, tokens, columns = pieces[0].shape
    span = tokens // rows
    seq = span * chunks
    wide = pltpu.VMEM((seq, columns), BF16)
    return pl.pallas_call(
        partial(attend_back_kernel, chunks=chunks, row=row),
        name="attend_back",
        grid_spec=pltpu.PrefetchScalarGridSpec(
            num_scalar_prefetch=2,
            grid=(1,),
            in_specs=[pl.BlockSpec((kinds, span, columns), lambda r, *_: (0, row, 0))] * chunks
            + [pl.BlockSpec((1, span, columns), lambda r, *_: (0, row, 0))] * chunks
            + [pl.BlockSpec((seq, HD), lambda r, *_: (0, 0))] * 3,
            out_specs=[pl.BlockSpec((kinds, span, columns), lambda r, *_: (0, 0, 0))] * chunks,
            scratch_shapes=[wide] * 4 + [pltpu.VMEM((seq, HD), F32)] * 2 + [wide] * 3,
        ),
        out_shape=[jax.ShapeDtypeStruct((kinds, span, columns), BF16)] * chunks,
        cost_estimate=cost(12),
        compiler_params=params(1),
    )(source, lengths, *pieces, *grads, *tables)


def up_kernel(perm_ref, a_ref, *refs, parts):
    weights = refs[:parts]
    active_ref, slope_ref = refs[parts:]
    u = blocks_dot(a_ref, weights)
    half = 0.5 * (1.0 + lax.erf(u * math.sqrt(0.5)))
    active_ref[...] = (u * half).astype(BF16)
    slope_ref[...] = half + u * jnp.exp(-0.5 * u * u) * (1.0 / math.sqrt(2.0 * math.pi))


def up_stage(perm, a, weights, part, columns, tile=512):
    tokens, width = a.shape
    parts = perm.shape[0]
    tile = min(tile, columns)
    specs = block_specs(weights, width // parts, tile, lambda n, *_: part * (columns // tile) + n)
    out = pl.BlockSpec((tokens, tile), lambda n, *_: (0, n))
    return pl.pallas_call(
        partial(up_kernel, parts=parts),
        name="up",
        grid_spec=pltpu.PrefetchScalarGridSpec(
            num_scalar_prefetch=1,
            grid=(columns // tile,),
            in_specs=[pl.BlockSpec((tokens, width), lambda n, *_: (0, 0))] + specs,
            out_specs=[out, out],
        ),
        out_shape=[
            jax.ShapeDtypeStruct((tokens, columns), BF16),
            jax.ShapeDtypeStruct((tokens, columns), F32),
        ],
        cost_estimate=cost(columns / 200),
        compiler_params=params(1),
    )(perm, a, *weights)


def up_back_kernel(perm_ref, a_ref, slope_ref, *refs, parts):
    weights = refs[:parts]
    refs[parts][...] = (blocks_dot(a_ref, weights) * slope_ref[...]).astype(BF16)


def up_back(perm, a, slope, weights, offset, tile=512):
    tokens, width = a.shape
    parts = perm.shape[0]
    columns = slope.shape[1]
    tile = min(tile, columns)
    specs = block_specs(
        weights, width // parts, tile, lambda n, *_: offset // tile + n
    )
    out = pl.BlockSpec((tokens, tile), lambda n, *_: (0, n))
    return pl.pallas_call(
        partial(up_back_kernel, parts=parts),
        name="up_back",
        grid_spec=pltpu.PrefetchScalarGridSpec(
            num_scalar_prefetch=1,
            grid=(columns // tile,),
            in_specs=[pl.BlockSpec((tokens, width), lambda n, *_: (0, 0)), out] + specs,
            out_specs=out,
        ),
        out_shape=jax.ShapeDtypeStruct((tokens, columns), BF16),
        cost_estimate=cost(columns / 200),
        compiler_params=params(1),
    )(perm, a, slope, *weights)


def back_kernel(*refs, lefts, parts, adds):
    out_ref = refs[-1]
    block = out_ref.shape[1] // parts
    tile = refs[lefts].shape[0]
    n = pl.program_id(0)
    for p in range(parts):
        at = pl.ds(pl.multiple_of(p * block + n * tile, 128), tile)
        total = refs[-2][:, at] if adds else None
        for h in range(lefts):
            term = lax.dot_general(
                refs[h][...], refs[lefts + h * parts + p][...], NT, preferred_element_type=F32
            )
            total = term if total is None else total + term
        out_ref[:, at] = total.astype(out_ref.dtype)


def to_width(lefts, weights, width, added=(), dtype=BF16, across=(0,)):
    parts = len(weights[0])
    block = width // parts
    tile = min(block, 256)
    tokens = lefts[0].shape[0]
    left_specs, specs, arrays = [], [], []
    for left, weight, at in zip(lefts, weights, across):
        columns = left.shape[1]
        left_specs.append(pl.BlockSpec((tokens, columns), lambda n: (0, 0)))
        specs += [pl.BlockSpec((tile, columns), lambda n, at=at: (n, at))] * parts
        arrays += weight
    whole = pl.BlockSpec((tokens, width), lambda n: (0, 0))
    return pl.pallas_call(
        partial(back_kernel, lefts=len(lefts), parts=parts, adds=len(added)),
        name="to_width",
        grid=(block // tile,),
        in_specs=left_specs + specs + [whole] * len(added),
        out_specs=whole,
        out_shape=jax.ShapeDtypeStruct((tokens, width), dtype),
        cost_estimate=cost(sum(a.shape[1] for a in lefts) / 256),
        compiler_params=params(1),
    )(*lefts, *arrays, *added)


def grad_kernel(*refs, count, rights, adds):
    lefts, fars = refs[:count], refs[count : 2 * count]
    sides = refs[2 * count : 2 * count + rights], refs[2 * count + rights : 2 * count + 2 * rights]
    add_refs, out_ref = refs[2 * count + 2 * rights : -1], refs[-1]
    at = 0
    for b in range(count):
        total = None
        for left, right_refs in zip((lefts[b], fars[b]), sides):
            start = 0
            for right in right_refs:
                size = right.shape[1]
                term = lax.dot_general(
                    left[0, start : start + size, :], right[0], TN, preferred_element_type=F32
                )
                total = term if total is None else total + term
                start += size
        for n in range(adds[b]):
            total = total + add_refs[at + n][0].astype(F32)
        at += adds[b]
        out_ref[b] = total.astype(BF16)


def grad_blocks(left, left_far, near, far, parts, chosen, added, first, kinds, tile=512):
    _, tokens, width = left.shape
    columns = near[0].shape[2]
    tile = min(tile, columns)
    steps = columns // tile
    block = width // parts

    def place(start, row):
        return lambda s, n: (row, 0, (first - start + s) * steps + n)

    flat = [a for arrays in added for a in arrays]
    left_specs = [
        pl.BlockSpec((1, tokens, block), lambda s, n, p=p: (first + s, 0, p)) for p in chosen
    ]
    return pl.pallas_call(
        partial(
            grad_kernel,
            count=len(chosen),
            rights=len(near),
            adds=tuple(len(a) for a in added),
        ),
        name="grad",
        grid=(kinds, steps),
        in_specs=left_specs * 2
        + [
            pl.BlockSpec((1, r.shape[1], tile), lambda s, n: (first + s, 0, n))
            for r in (*near, *far)
        ]
        + [pl.BlockSpec((1, block, tile), place(start, row)) for _, row, start in flat],
        out_specs=pl.BlockSpec((len(chosen), block, tile), lambda s, n: (0, 0, s * steps + n)),
        out_shape=jax.ShapeDtypeStruct((len(chosen), block, kinds * columns), BF16),
        cost_estimate=cost(len(chosen) * kinds * columns / 512),
        compiler_params=params(2),
    )(*[left] * len(chosen), *[left_far] * len(chosen), *near, *far, *[a for a, _, _ in flat])


def part_kernel(in_ref, out_ref, *, turned):
    values = in_ref[...]
    out_ref[...] = values.astype(F32).T.astype(BF16) if turned else values


def shard_part(shard, n, size, turned):
    short = shard.shape[1] if turned else shard.shape[0]
    spec = pl.BlockSpec((size, short), lambda i: (n, 0))
    if not turned:
        spec = pl.BlockSpec((short, size), lambda i: (0, n))
    return pl.pallas_call(
        partial(part_kernel, turned=turned),
        name="part",
        grid=(1,),
        in_specs=[spec],
        out_specs=pl.BlockSpec((short, size), lambda i: (0, 0)),
        out_shape=jax.ShapeDtypeStruct((short, size), BF16),
        cost_estimate=cost(1),
        compiler_params=params(1),
    )(shard)


def hat_of(z):
    center = z - jnp.mean(z, axis=-1, keepdims=True)
    inverse = lax.rsqrt(jnp.mean(center * center, axis=-1, keepdims=True) + EPSILON)
    return center * inverse, inverse


def own_kernel(perm_ref, grad_ref, z_ref, *refs, parts):
    weights = refs[:parts]
    out_ref, sum_ref = refs[parts:]
    block = weights[0].shape[0]
    for p in range(parts):
        out_ref[0, :, p * block : (p + 1) * block] = lax.dot_general(
            grad_ref[0], weights[p][...], NT, preferred_element_type=F32
        )
    tile = 32
    tokens, width = out_ref.shape[1:]
    gain = jnp.zeros((8, width), F32)
    shift = jnp.zeros((8, width), F32)
    for t in range(0, tokens, tile):
        d = out_ref[0, t : t + tile, :]
        hat, _ = hat_of(z_ref[0, t : t + tile, :])
        gain = gain + jnp.sum((d * hat).reshape(tile // 8, 8, width), axis=0)
        shift = shift + jnp.sum(d.reshape(tile // 8, 8, width), axis=0)
    sum_ref[0, :8] = gain
    sum_ref[0, 8:] = shift


def own_part(perm, grads, streams, weights, row):
    kinds, span, columns = grads.shape
    width = streams.shape[2]
    parts = perm.shape[0]
    specs = block_specs(weights, width // parts, columns, lambda s, *_: s)
    return pl.pallas_call(
        partial(own_kernel, parts=parts),
        name="own",
        grid_spec=pltpu.PrefetchScalarGridSpec(
            num_scalar_prefetch=1,
            grid=(kinds,),
            in_specs=[
                pl.BlockSpec((1, span, columns), lambda s, *_: (s, 0, 0)),
                pl.BlockSpec((1, span, width), lambda s, *_: (s, row, 0)),
            ]
            + specs,
            out_specs=[
                pl.BlockSpec((1, span, width), lambda s, *_: (s, 0, 0)),
                pl.BlockSpec((1, 16, width), lambda s, *_: (s, 0, 0)),
            ],
        ),
        out_shape=[
            jax.ShapeDtypeStruct((kinds, span, width), F32),
            jax.ShapeDtypeStruct((kinds, 16, width), F32),
        ],
        cost_estimate=cost(12),
        compiler_params=params(1),
    )(perm, grads, streams, *weights)


def other_kernel(grad_ref, part_ref, z_ref, gain_ref, *refs, parts):
    weights = refs[:parts]
    out_ref, total_ref = refs[parts:]
    block = weights[0].shape[0]
    for p in range(parts):
        cols = slice(p * block, (p + 1) * block)
        total_ref[:, cols] = part_ref[0, :, cols] + lax.dot_general(
            grad_ref[0], weights[p][...], NT, preferred_element_type=F32
        )
    tile = 32
    for t in range(0, total_ref.shape[0], tile):
        rows = slice(t, t + tile)
        hat, inverse = hat_of(z_ref[0, rows, :])
        e = total_ref[rows, :] * gain_ref[...]
        first = jnp.mean(e, axis=-1, keepdims=True)
        second = jnp.mean(e * hat, axis=-1, keepdims=True)
        out_ref[0, rows, :] = ((e - first - hat * second) * inverse).astype(BF16)


def other_part(grads, own, streams, gain, weights, row):
    kinds, span, columns = grads.shape
    width = streams.shape[2]
    parts = len(weights)
    block = width // parts
    return pl.pallas_call(
        partial(other_kernel, parts=parts),
        name="other",
        grid=(kinds,),
        in_specs=[
            pl.BlockSpec((1, span, columns), lambda s: (s, 0, 0)),
            pl.BlockSpec((1, span, width), lambda s: (s, 0, 0)),
            pl.BlockSpec((1, span, width), lambda s: (s, row, 0)),
            pl.BlockSpec((1, width), lambda s: (0, 0)),
        ]
        + [pl.BlockSpec((block, columns), lambda s: (0, s))] * parts,
        out_specs=pl.BlockSpec((1, span, width), lambda s: (s, 0, 0)),
        out_shape=jax.ShapeDtypeStruct((kinds, span, width), BF16),
        scratch_shapes=[pltpu.VMEM((span, width), F32)],
        cost_estimate=cost(14),
        compiler_params=params(1),
    )(grads, own, streams, gain, *weights)


def last_kernel(perm_ref, earlier_ref, coeff_ref, dz_ref, dr_ref, *refs):
    out_ref, mix_ref = refs[-2:]
    prev, tile, width = earlier_ref.shape
    parts = perm_ref.shape[0]
    block = width // parts
    count, half = prev * GROUP, STREAMS * GROUP
    for g in range(tile // GROUP):
        rows = slice(g * GROUP, (g + 1) * GROUP)
        high, low = spread(coeff_ref[g])
        pairs = jnp.zeros((count, half), F32)
        for p in range(parts):
            here = slice(p * block, (p + 1) * block)
            there = pl.ds(pl.multiple_of(perm_ref[p] * block, 128), block)
            grads = jnp.concatenate(
                [dz_ref[s, rows, here] for s in range(STREAMS - 1)] + [dr_ref[rows, here]], axis=0
            )
            x = earlier_ref[:, rows, there].reshape(count, block)
            pairs = pairs + lax.dot_general(x, grads, NT, preferred_element_type=F32)
            total = jnp.dot(high, grads, preferred_element_type=F32) + jnp.dot(
                low, grads, preferred_element_type=F32
            )
            out_ref[:, rows, there] = total.astype(BF16).reshape(prev, GROUP, block)
        token = lax.broadcasted_iota(jnp.int32, (count, half), 0) % GROUP
        lane = lax.broadcasted_iota(jnp.int32, (count, half), 1)
        wide = lax.broadcasted_iota(jnp.int32, (count, 128), 1)
        mixed = jnp.zeros((count, 128), F32)
        for s in range(STREAMS):
            own = jnp.where(lane == token + s * GROUP, pairs, 0.0)
            mixed = jnp.where(wide == s, jnp.sum(own, axis=-1, keepdims=True), mixed)
        mix_ref[g] = mixed


def last_stage(perm, inputs, coeff, dz, dr, row, rows, before, tile=64):
    prev, tokens, width = inputs.shape
    steps = tokens // rows // tile
    count = prev * GROUP
    here = lambda t, *_: (0, row * steps + t, 0)
    return pl.pallas_call(
        last_kernel,
        name="last",
        grid_spec=pltpu.PrefetchScalarGridSpec(
            num_scalar_prefetch=1,
            grid=(steps,),
            in_specs=[
                pl.BlockSpec((prev, tile, width), here),
                pl.BlockSpec(
                    (tile // GROUP,) + coeff.shape[1:], lambda t, *_: (row * steps + t, 0, 0)
                ),
                pl.BlockSpec((STREAMS - 1, tile, width), lambda t, *_: (0, t, 0)),
                pl.BlockSpec((tile, width), lambda t, *_: (row * steps + t, 0)),
            ]
            + [pl.BlockSpec(memory_space=pl.ANY)] * len(before),
            out_specs=[
                pl.BlockSpec((prev, tile, width), here),
                pl.BlockSpec(
                    (tile // GROUP, count, 128), lambda t, *_: (row * steps + t, 0, 0)
                ),
            ],
        ),
        out_shape=[
            jax.ShapeDtypeStruct((prev, tokens, width), BF16),
            jax.ShapeDtypeStruct((tokens // GROUP, count, 128), F32),
        ],
        input_output_aliases={5 + n: n for n in range(len(before))},
        cost_estimate=cost(12),
        compiler_params=params(1),
    )(perm, inputs, coeff, dz, dr, *before)


def two_terms(values):
    high = values.astype(BF16)
    return high, (values - high.astype(F32)).astype(BF16)


def final_kernel(res_ref, mine_ref, theirs_ref, out_ref, cot_ref, valid_ref, in_ref, mix_ref, *refs):
    final_ref, grad_ref, low_ref, far_ref, high_ref, rest_ref, back_ref, inverse_ref = refs
    tile, width = res_ref.shape
    step = 16
    for t in range(0, tile, step):
        rows = slice(t, t + step)
        final = res_ref[rows, :] + (
            mine_ref[rows, :].astype(F32) + theirs_ref[rows, :].astype(F32)
        )
        inverse = lax.rsqrt(jnp.mean(final * final, axis=-1, keepdims=True) + RMS_EPSILON)
        final_ref[rows, :] = final
        inverse_ref[rows, :] = jnp.broadcast_to(inverse, (step, HD))
        high_ref[rows, :], rest_ref[rows, :] = two_terms(final * inverse)
    pre = sum(
        lax.dot_general(n[...], in_ref[...], NT, preferred_element_type=F32)
        for n in (high_ref, rest_ref)
    )
    grad_pre = lax.dot_general(
        cot_ref[...], mix_ref[...], NT, precision=HIGHEST, preferred_element_type=F32
    ) * (
        0.5 * (1.0 + lax.erf(pre * math.sqrt(0.5)))
        + pre * jnp.exp(-0.5 * pre * pre) * (1.0 / math.sqrt(2.0 * math.pi))
    )
    back_ref[...] = sum(
        jnp.dot(g, in_ref[...], preferred_element_type=F32) for g in two_terms(grad_pre)
    )
    for t in range(0, tile, step):
        rows = slice(t, t + step)
        inverse = inverse_ref[rows, :1]
        normed = final_ref[rows, :] * inverse
        grad = back_ref[rows, :]
        grad = inverse * (grad - normed * jnp.mean(grad * normed, axis=-1, keepdims=True))
        grad = out_ref[rows, :].astype(F32) * valid_ref[rows, :] + grad
        grad_ref[rows, :] = grad
        low = grad.astype(BF16)
        low_ref[rows, :] = low
        far_ref[rows, :] = low[:, width // 2 :]


def final_stage(residual, mine, theirs, grad_out, cotangent, valid, weight_in, weight_out, tile=128):
    tokens, width = residual.shape
    rows = pl.BlockSpec((tile, width), lambda t: (t, 0))
    cotangent = jnp.pad(cotangent, ((0, 0), (0, HD - MIXW)))
    weight_in = jnp.pad(weight_in, ((0, HD - MIXW), (0, 0))).astype(BF16)
    weight_out = jnp.pad(weight_out, ((0, HD - MIXW), (0, HD - MIXW)))
    return pl.pallas_call(
        final_kernel,
        name="final",
        grid=(tokens // tile,),
        in_specs=[
            rows,
            rows,
            rows,
            rows,
            pl.BlockSpec((tile, HD), lambda t: (t, 0)),
            pl.BlockSpec((tile, 1), lambda t: (t, 0)),
            pl.BlockSpec((HD, width), lambda t: (0, 0)),
            pl.BlockSpec((HD, HD), lambda t: (0, 0)),
        ],
        out_specs=[rows, rows, rows, pl.BlockSpec((tile, width // 2), lambda t: (t, 0))],
        out_shape=[
            jax.ShapeDtypeStruct((tokens, width), F32),
            jax.ShapeDtypeStruct((tokens, width), F32),
            jax.ShapeDtypeStruct((tokens, width), BF16),
            jax.ShapeDtypeStruct((tokens, width // 2), BF16),
        ],
        scratch_shapes=[
            pltpu.VMEM((tile, width), BF16),
            pltpu.VMEM((tile, width), BF16),
            pltpu.VMEM((tile, width), F32),
            pltpu.VMEM((tile, HD), F32),
        ],
        cost_estimate=cost(8),
        compiler_params=params(1),
    )(residual, mine, theirs, grad_out, cotangent, valid, weight_in, weight_out)


def second_kernel(res_ref, mine_ref, theirs_ref, grad_ref, gain_ref, out_ref, sum_ref):
    @pl.when(pl.program_id(0) == 0)
    def _():
        sum_ref[...] = jnp.zeros_like(sum_ref)

    step = 32
    width = res_ref.shape[1]
    for t in range(0, res_ref.shape[0], step):
        rows = slice(t, t + step)
        hat, inverse = hat_of(res_ref[rows, :])
        d = mine_ref[rows, :].astype(F32) + theirs_ref[rows, :].astype(F32)
        sum_ref[:8] += jnp.sum((d * hat).reshape(step // 8, 8, width), axis=0)
        sum_ref[8:] += jnp.sum(d.reshape(step // 8, 8, width), axis=0)
        e = d * gain_ref[...]
        first = jnp.mean(e, axis=-1, keepdims=True)
        second = jnp.mean(e * hat, axis=-1, keepdims=True)
        out_ref[rows, :] = (grad_ref[rows, :] + (e - first - hat * second) * inverse).astype(BF16)


def second_norm_back(residual, mine, theirs, grad, gain, tile=128):
    tokens, width = residual.shape
    rows = pl.BlockSpec((tile, width), lambda t: (t, 0))
    return pl.pallas_call(
        second_kernel,
        name="second",
        grid=(tokens // tile,),
        in_specs=[rows, rows, rows, rows, pl.BlockSpec((1, width), lambda t: (0, 0))],
        out_specs=[rows, pl.BlockSpec((16, width), lambda t: (0, 0))],
        out_shape=[
            jax.ShapeDtypeStruct((tokens, width), BF16),
            jax.ShapeDtypeStruct((16, width), F32),
        ],
        cost_estimate=cost(6),
        compiler_params=params(1),
    )(residual, mine, theirs, grad, gain)


def layer_norm(values, gain, shift):
    center = values - jnp.mean(values, axis=-1, keepdims=True)
    spread = jnp.mean(center * center, axis=-1, keepdims=True)
    return center * lax.rsqrt(spread + EPSILON) * gain + shift


def activate(values):
    return jax.nn.gelu(values, approximate=False)


def mixer(final, weight_in, weight_out, bias):
    normed = final * lax.rsqrt(jnp.mean(final * final, axis=-1, keepdims=True) + RMS_EPSILON)
    hidden = activate(
        lax.dot_general(
            normed, weight_in, NT, precision=HIGHEST, preferred_element_type=F32
        )
    )
    return jnp.dot(hidden, weight_out, precision=HIGHEST, preferred_element_type=F32) + bias


def turn_tables(positions):
    half = ROT // 2
    frequency = 10000.0 ** (-2.0 * jnp.arange(half, dtype=F32) / ROT)
    angles = positions.astype(F32)[:, None] * frequency[None, :]
    cosine, sine = jnp.cos(angles), jnp.sin(angles)
    count = positions.shape[0]
    rest = HD - ROT
    base = jnp.concatenate([cosine, cosine, jnp.ones((count, rest), F32)], axis=1)
    up = jnp.concatenate([jnp.zeros((count, half), F32), sine, jnp.zeros((count, rest), F32)], 1)
    down = jnp.concatenate([-sine, jnp.zeros((count, half + rest), F32)], axis=1)
    return base, up, down


def group_coeff(mix_in, count_prev, tokens):
    groups = tokens // GROUP
    c = mix_in.reshape(STREAMS, count_prev, groups, GROUP).transpose(2, 1, 3, 0)
    return c.reshape(groups, count_prev * GROUP, STREAMS)


def body(
    earlier,
    mix_in,
    lengths,
    w_query,
    w_key,
    w_value,
    w_proj,
    w_up,
    w_down,
    first_gain,
    first_shift,
    second_gain,
    second_shift,
    mixer_in,
    mixer_out,
    mixer_bias,
    grad_out,
    grad_mix,
):
    count_prev, rows, span, width = earlier.shape
    tokens = rows * span
    fsdp, ctx = lax.axis_size("fsdp"), lax.axis_size("ctx")
    me, z = lax.axis_index("fsdp"), lax.axis_index("ctx")
    masks = block_masks(fsdp)
    place_of = [masks.index(m) for m in range(fsdp)]
    block = width // fsdp
    piece = block // ctx
    heads_width = w_query.shape[1]
    hidden = w_up.shape[1]
    perm = jnp.stack([me ^ m for m in masks]).astype(jnp.int32)
    table = jnp.array(place_of, jnp.int32)
    ring = jnp.arange(ctx, dtype=jnp.int32)
    source = (z - ring + ctx) % ctx
    slots = z * span + jnp.arange(span, dtype=jnp.int32)
    valid = (slots[None, :] < lengths[:, None]).astype(F32).reshape(tokens)

    def relative(values):
        return jnp.concatenate(
            [
                lax.dynamic_slice_in_dim(values, perm[p] * block, block, values.ndim - 1)
                for p in range(fsdp)
            ],
            axis=-1,
        )

    def absolute(values):
        return jnp.concatenate(
            [
                lax.dynamic_slice_in_dim(values, table[a ^ me] * block, block, values.ndim - 1)
                for a in range(fsdp)
            ],
            axis=-1,
        )

    def part(values, p):
        return values[:, p * block : (p + 1) * block]

    small = jnp.concatenate(
        [mixer_in.T, first_gain[None], first_shift[None], second_gain[None], second_shift[None]], 0
    )
    around = jnp.zeros((ctx,) + small.shape, BF16)
    for s in range(ctx):
        got = small if s == 0 else shift_ctx(small, s)
        around = lax.dynamic_update_slice(around, got[None], (source[s], 0, 0))
    around = cross(around)
    around = jnp.stack(around + [over_fsdp(a, 1) for a in around])
    small_all = around.transpose(2, 0, 1, 3).reshape(small.shape[0], width).astype(F32)
    mixer_full = small_all[:MIXW]
    gain_first, shift_first, gain_second, shift_second = [
        small_all[MIXW + n : MIXW + n + 1] for n in range(4)
    ]

    half = hidden // 2
    ctx_qkv = gather_ctx(jnp.concatenate([w_query, w_key, w_value], axis=1))
    ctx_both = gather_ctx(jnp.concatenate([w_up, w_proj.T], axis=1))

    order = Order()
    Pace.value = FORWARD_PACE
    inputs = earlier.reshape(count_prev, tokens, width)
    coeff = group_coeff(mix_in, count_prev, tokens)
    def far_half(values):
        return over_fsdp(values[..., width // 2 :], 1)

    normed_in, streams = order.keep(
        mix_streams(perm, inputs, coeff, gain_first, shift_first)
    )
    tables_here = turn_tables(jnp.tile(slots, rows))
    tables_all = turn_tables(jnp.arange(span * ctx, dtype=jnp.int32))
    target = (z + ring) % ctx
    tables_here, tables_all = order.wait((tables_here, tables_all))
    normed_in_far = order.wait(far_half(order(normed_in)))

    def to_heads(chunks):
        return [chunks[0]] + [shift_ctx(chunks[s], s) for s in range(1, ctx)]

    def to_slots(pieces):
        return [pieces[0]] + [shift_ctx(pieces[s], -s) for s in range(1, ctx)]

    def to_core(parts):
        return [over_fsdp(p, 1) for p in parts]

    near_qkv = cross(order.wait(ctx_qkv))
    far_qkv = to_core(near_qkv[:1])
    other = [over_tp(near_qkv[0])]
    far_qkv = order.wait(far_qkv)
    other = order.wait(other)
    near_qkv = order.wait(near_qkv)
    far_qkv = order.wait(far_qkv + to_core(near_qkv[1:]))
    blocks_qkv = near_qkv + far_qkv
    pieces = to_heads(
        order.keep(to_chunks(target, perm, order(normed_in), blocks_qkv, tables_here, 2))
    )
    other = other + [over_tp(p) for p in near_qkv[1:]]
    near_both = cross(order.wait(ctx_both))
    pieces = order.wait(pieces)
    other = order.wait(other)
    outs = to_slots(order.keep(attend(source, lengths, order(pieces))))
    ctx_down = [
        gather_ctx(order.keep(shard_part(order(w_down), n, half, True))) for n in range(2)
    ]
    outs = order.wait(outs)
    attended = order.keep(join(target, order(outs)))[0]
    near_both = order.wait(near_both)
    near_proj = order.wait([b[:, hidden:] for b in near_both])
    blocks_proj = near_proj + order.wait(to_core(near_proj))
    near_down = [cross(order.wait(ctx_down[0]))]
    far_both = to_core(order(near_both))
    branch_mine = order.keep(to_width([order(attended)], [blocks_proj], width))
    branch_theirs = over_tp(branch_mine)
    blocks_up = near_both + order.wait(far_both)
    near_down[0] = order.wait(near_down[0])
    near_down.append(cross(order.wait(ctx_down[1])))
    branch_theirs = order.wait(branch_theirs)
    residual = streams[STREAMS - 1] + tp_sum(branch_mine, branch_theirs)

    normed = layer_norm(residual, gain_second, shift_second).astype(BF16)
    normed = order.wait(normed)
    far_down = [to_core(near_down[0])]
    other_far = to_core(other)
    active, slope = [], []
    for n in range(2):
        a, b = order.keep(up_stage(perm, order(normed), blocks_up, n, half))
        active.append(a)
        slope.append(b)
    far_down[0] = order.wait(far_down[0])
    other = other + order.wait(other_far)
    down_first = order.keep(
        to_width([order(active[0])], [near_down[0] + far_down[0]], width, (), F32)
    )
    near_down[1] = order.wait(near_down[1])
    far_down.append(order.wait(to_core(near_down[1])))
    blocks_down = [near + far for near, far in zip(near_down, far_down)]
    down_mine = order.keep(
        to_width([order(active[1])], blocks_down[1:], width, (down_first,))
    )
    down_theirs = over_tp(down_mine)
    grad_out_here = order.wait(relative(grad_out.reshape(tokens, width)))
    mix_cotangent = order.wait((grad_mix.reshape(MIXW, tokens) * valid[None]).T)
    down_theirs = order.wait(down_theirs)

    final, grad_final, grad_down_b, grad_down_near = order.keep(
        final_stage(
            residual,
            down_mine,
            order(down_theirs),
            grad_out_here,
            mix_cotangent,
            valid[:, None],
            mixer_full,
            mixer_out,
        )
    )

    Pace.value = BACKWARD_PACE
    active_far = [over_fsdp(a, 1) for a in active]
    normed_far = far_half(normed)
    attended_far = over_fsdp(attended, 1)
    grad_down_far = over_fsdp(grad_down_near, 1)
    active_far, normed_far, attended_far, grad_down_far = order.wait(
        (active_far, normed_far, attended_far, grad_down_far)
    )
    down = [
        Scatter(order, grad_down_b[None], [a[None]], grad_down_far[None], [f[None]])
        for a, f in zip(active, active_far)
    ]
    down[0].launch()
    grad_upward, upward_far = [], []
    for n in range(2):
        grad_upward.append(
            order.keep(up_back(perm, order(grad_down_b), slope[n], blocks_down[n], 0))
        )
        upward_far.append(over_fsdp(grad_upward[n], 1))
    normed_mine = order.keep(to_width(order(grad_upward), [blocks_up] * 2, width, (), BF16, (0, 1)))
    normed_theirs = over_tp(normed_mine)
    down[1].launch()
    Pace.value = 3 * BACKWARD_PACE
    grad_down = [scatter_ctx(down[0].finish())]
    Pace.value = BACKWARD_PACE
    upward_far = order.wait(upward_far)
    up = [
        Scatter(order, normed[None], [u[None]], normed_far[None], [f[None]])
        for u, f in zip(grad_upward, upward_far)
    ]
    up[0].launch()
    mix_value, mix_pull = jax.vjp(
        lambda *weights: mixer(order(final), *weights), mixer_full, mixer_out, mixer_bias
    )
    mix_out = mix_value.T.reshape(MIXW, rows, span)
    grad_mixer_first, grad_mixer_second, grad_mixer_shift = mix_pull(mix_cotangent)
    output = absolute(order(final).astype(BF16)).reshape(rows, span, width)
    tail = jnp.concatenate([grad_mixer_second, grad_mixer_shift[None]], axis=0)
    tail, grad_mixer_first, output, mix_out = order.wait(
        (tail, grad_mixer_first, output, mix_out)
    )
    normed_theirs = order.wait(normed_theirs)
    grad_branch_b, second_sums = order.keep(
        second_norm_back(residual, normed_mine, order(normed_theirs), grad_final, gain_second)
    )
    second_pair = second_sums.reshape(2, 8, width).sum(1)

    grad_branch_far = far_half(grad_branch_b)
    grad_chunks = order.keep(
        to_chunks(target, perm, order(grad_branch_b)[None], blocks_proj, tables_here, 0)
    )
    grad_branch_far = order.wait(grad_branch_far)
    grad_pieces = to_heads(grad_chunks)
    grad_down.append(scatter_ctx(down[1].finish()))
    up[1].launch()
    proj = Scatter(
        order, grad_branch_b[None], [attended[None]], grad_branch_far[None], [attended_far[None]]
    )
    made_proj = proj.make(1)
    grad_up = [scatter_ctx(up[0].finish())]
    proj.launch(0, None, order(made_proj))
    grad_pieces = order.wait(grad_pieces)
    back = [
        order.keep(attend_back(source, lengths, pieces, order(grad_pieces), tables_all, 0))
    ]
    sent = [to_slots(back[0])]
    back.append(
        order.keep(attend_back(source, lengths, pieces, order(grad_pieces), tables_all, 1))
    )
    grad_down[0] = order.wait(grad_down[0])
    mine, theirs, own = [], [], []
    sent[0] = order.wait(sent[0])
    mine.append(order.keep(join(target, sent[0])))
    theirs.append(over_tp(mine[0]))
    sent.append(to_slots(order(back[1])))
    own.append(order.keep(own_part(perm, order(mine[0]), streams, blocks_qkv, 0)))
    grad_down[1] = order.wait(grad_down[1])
    sent[1] = order.wait(sent[1])
    mine.append(order.keep(join(target, sent[1])))
    theirs.append(over_tp(mine[1]))
    mine_far = [over_fsdp(m, 1) for m in order(mine)]
    grad_proj = scatter_ctx(proj.finish())
    grad_up.append(scatter_ctx(up[1].finish()))
    mine_far = order.wait(mine_far)
    qkv = Scatter(order, normed_in, mine, normed_in_far, mine_far)
    qkv.launch(0, 1)
    qkv.launch(1, 2)
    own.append(order.keep(own_part(perm, order(mine[1]), streams, blocks_qkv, 1)))
    grad_up[0] = order.wait(grad_up[0])
    theirs[0] = order.wait(theirs[0])
    grad_query = scatter_ctx(qkv.finish(0, 1))
    sums = (own[0][1] + own[1][1]).sum(0).reshape(2, 8, width).sum(1)
    sums = order.wait(sums)

    dz = order.keep(other_part(order(theirs[0]), own[0][0], streams, gain_first, other, 0))
    done = order.keep(
        last_stage(perm, inputs, coeff, order(dz), grad_branch_b, 0, rows, ())
    )
    grad_proj = order.wait(grad_proj)
    theirs[1] = order.wait(theirs[1])
    grad_rest = scatter_ctx(qkv.finish(1, 2))
    Pace.value = FORWARD_PACE
    sums_far = over_tp(order(sums))
    dz = order.keep(other_part(order(theirs[1]), own[1][0], streams, gain_first, other, 1))
    sums_far = order.wait(sums_far)
    packed = jnp.concatenate(
        [grad_mixer_first, sums + sums_far, second_pair], axis=0
    )
    packed = packed.reshape(packed.shape[0], fsdp, ctx, piece)
    packed = jnp.stack(
        [lax.dynamic_index_in_dim(packed, z ^ m, 2, keepdims=False) for m in block_masks(ctx)]
    ).transpose(0, 2, 1, 3)
    tail = jnp.pad(tail, ((0, 0), (0, HD - MIXW)))
    packed, tail = order.wait((packed, tail))

    def fold(packed, tail, move):
        split = packed.shape[0] // 2
        return packed[:split], tail, move(packed[split:]), move(tail)

    def landed(packed, tail, got_packed, got_tail):
        got_packed, got_tail = order.wait((got_packed, got_tail))
        return packed + got_packed, tail + got_tail

    ctx_steps = [
        (lambda v, bit=bit: lax.ppermute(v, "ctx", xor_pairs(ctx, bit)))
        for bit in reversed(bits_of(ctx))
    ]
    fsdp_steps = [(lambda v, bit=bit: over_fsdp(v, bit)) for bit in reversed(bits_of(fsdp))]
    moving = fold(packed, tail, ctx_steps[0])
    grad_up[1] = order.wait(grad_up[1])
    for step in ctx_steps[1:]:
        moving = fold(*landed(*moving), step)
    grad_inputs, grad_coeff = order.keep(
        last_stage(perm, inputs, coeff, order(dz), grad_branch_b, 1, rows, done)
    )
    packed, tail = landed(*moving)
    moving = fold(packed[0], tail, fsdp_steps[0])
    for step in fsdp_steps[1:]:
        moving = fold(*landed(*moving), step)
    packed, tail = landed(*moving)
    norms = packed[0]
    grad_key, grad_value = jnp.split(grad_rest, 2, axis=1)
    grad_proj = grad_proj.T
    grad_earlier = grad_inputs.reshape(earlier.shape)
    grad_mix_in = (
        grad_coeff[:, :, :STREAMS]
        .reshape(tokens // GROUP, count_prev, GROUP, STREAMS)
        .transpose(3, 1, 0, 2)
        .reshape(mix_in.shape)
    )
    return (
        output,
        mix_out,
        grad_earlier,
        grad_mix_in,
        grad_query,
        grad_key,
        grad_value,
        grad_proj,
        jnp.concatenate(grad_up, axis=1),
        jnp.concatenate(grad_down, axis=1).T,
        norms[MIXW],
        norms[MIXW + 1],
        norms[MIXW + 2],
        norms[MIXW + 3],
        norms[:MIXW].T,
        tail[:MIXW, :MIXW],
        tail[MIXW, :MIXW],
    )


def solution(mesh):
    placed = (
        P(None, "fsdp", "ctx", None),
        P(None, "fsdp", "ctx"),
        P("fsdp"),
        P(("fsdp", "ctx"), "tp"),
        P(("fsdp", "ctx"), "tp"),
        P(("fsdp", "ctx"), "tp"),
        P("tp", ("fsdp", "ctx")),
        P(("fsdp", "ctx"), "tp"),
        P("tp", ("fsdp", "ctx")),
        P(("fsdp", "ctx")),
        P(("fsdp", "ctx")),
        P(("fsdp", "ctx")),
        P(("fsdp", "ctx")),
        P(("fsdp", "ctx"), None),
        P(),
        P(),
        P("fsdp", "ctx", None),
        P(None, "fsdp", "ctx"),
    )
    return jax.shard_map(
        body,
        mesh=mesh,
        in_specs=placed,
        out_specs=(
            P("fsdp", "ctx", None),
            P(None, "fsdp", "ctx"),
            P(None, "fsdp", "ctx", None),
            P(None, "fsdp", "ctx"),
            P(("fsdp", "ctx"), "tp"),
            P(("fsdp", "ctx"), "tp"),
            P(("fsdp", "ctx"), "tp"),
            P("tp", ("fsdp", "ctx")),
            P(("fsdp", "ctx"), "tp"),
            P("tp", ("fsdp", "ctx")),
            P(("fsdp", "ctx")),
            P(("fsdp", "ctx")),
            P(("fsdp", "ctx")),
            P(("fsdp", "ctx")),
            P(("fsdp", "ctx"), None),
            P(),
            P(),
        ),
        check_vma=False,
    )
```

```python
from functools import partial
import math

import jax
import jax.numpy as jnp
from jax import lax
from jax.experimental import pallas as pl
from jax.experimental.pallas import tpu as pltpu
from jax.sharding import PartitionSpec as P

HD = 128
ROT = 32
STREAMS = 4
MIXW = 36
EPSILON = 1e-05
RMS_EPSILON = 1e-06
HIGHEST = lax.Precision.HIGHEST
NEGATIVE = -1e30
F32 = jnp.float32
BF16 = jnp.bfloat16
GROUP = 32
FORWARD_PACE = 3.0e7
BACKWARD_PACE = 2.2e9


def params(grid_rank):
    return pltpu.CompilerParams(
        dimension_semantics=("arbitrary",) * grid_rank, vmem_limit_bytes=56 * 1024 * 1024
    )


class Pace:
    value = FORWARD_PACE


def cost(time):
    return pl.CostEstimate(flops=int(time * Pace.value), transcendentals=0, bytes_accessed=1024)


def xor_pairs(size, mask):
    return [(i, i ^ mask) for i in range(size)]


def over_fsdp(values, mask):
    return lax.ppermute(values, "fsdp", xor_pairs(lax.axis_size("fsdp"), mask))


def over_tp(values):
    return lax.ppermute(values, "tp", xor_pairs(lax.axis_size("tp"), 1))


def shift_ctx(values, step):
    size = lax.axis_size("ctx")
    return lax.ppermute(values, "ctx", [(i, (i + step) % size) for i in range(size)])


def bits_of(size):
    return [1 << b for b in reversed(range(size.bit_length() - 1))]


def block_masks(size):
    masks = [0]
    for bit in bits_of(size):
        masks = masks + [m ^ bit for m in masks]
    return masks


def after(values, *earlier):
    return lax.optimization_barrier((values, earlier))[0]


class Order:
    def __init__(self):
        self.last = ()

    def __call__(self, values):
        return after(values, self.last)

    def keep(self, values):
        self.last = values
        return values

    def wait(self, values):
        return self.keep(self(values))


def gather_ctx(shard):
    return lax.all_gather(shard, "ctx", axis=0, tiled=True)


def cross(own):
    parts = [own]
    for bit in bits_of(lax.axis_size("fsdp"))[:-1]:
        parts = parts + [over_fsdp(p, bit) for p in parts]
    return parts


class Scatter:
    def __init__(self, order, left, rights, left_far, rights_far):
        self.order, self.left, self.far, self.rights = order, left, left_far, (rights, rights_far)
        self.count = lax.axis_size("fsdp")
        self.received = [[] for _ in range(self.count)]

    def blocks(self, chosen, first, kinds):
        near, far = self.order(self.rights)
        added = [[r for r in self.received[p] if r[2] == first] for p in chosen]
        made = grad_blocks(self.left, self.far, near, far, self.count, chosen, added, first, kinds)
        return self.order.keep(made)

    def make(self, level, first=0, kinds=None):
        half = self.count >> (level + 1)
        chosen = list(range(half, 2 * half))
        return self.blocks(chosen, first, kinds or self.left.shape[0])

    def send(self, level, made, first=0):
        half = self.count >> (level + 1)
        bit = bits_of(self.count)[::-1][level]
        got = over_fsdp(made, bit)
        for n in range(half):
            self.received[n].append((got, n, first))
        return got

    def launch(self, first=0, kinds=None, made=None):
        for level in range(1, len(bits_of(self.count))):
            if made is None:
                made = self.make(level, first, kinds)
            self.send(level, made, first)
            made = None

    def finish(self, first=0, kinds=None):
        return self.blocks([0], first, kinds or self.left.shape[0])[0]


def scatter_ctx(total):
    return lax.psum_scatter(total, "ctx", scatter_dimension=0, tiled=True).astype(F32)


def tp_sum(mine, theirs):
    return mine.astype(F32) + theirs.astype(F32)


NT = (((1,), (1,)), ((), ()))
TN = (((0,), (0,)), ((), ()))


def spread(coeff):
    count = coeff.shape[0]
    token = lax.broadcasted_iota(jnp.int32, (count, STREAMS * GROUP), 0) % GROUP
    lane = lax.broadcasted_iota(jnp.int32, (count, STREAMS * GROUP), 1)
    out = jnp.zeros((count, STREAMS * GROUP), F32)
    for s in range(STREAMS):
        out = jnp.where(lane == token + s * GROUP, coeff[:, s : s + 1], out)
    high = out.astype(BF16)
    return high, (out - high.astype(F32)).astype(BF16)


def mix_kernel(perm_ref, earlier_ref, coeff_ref, gain_ref, shift_ref, a_ref, z_ref):
    prev, tile, width = earlier_ref.shape
    parts = perm_ref.shape[0]
    block = width // parts
    for g in range(tile // GROUP):
        rows = slice(g * GROUP, (g + 1) * GROUP)
        high, low = spread(coeff_ref[g])
        for p in range(parts):
            source = pl.ds(pl.multiple_of(perm_ref[p] * block, 128), block)
            x = earlier_ref[:, rows, source].reshape(prev * GROUP, block)
            z_ref[:, rows, p * block : (p + 1) * block] = (
                lax.dot_general(high, x, TN, preferred_element_type=F32)
                + lax.dot_general(low, x, TN, preferred_element_type=F32)
            ).reshape(STREAMS, GROUP, block)
        for s in range(STREAMS - 1):
            z = z_ref[s, rows, :]
            center = z - jnp.mean(z, axis=-1, keepdims=True)
            spread_of = jnp.mean(center * center, axis=-1, keepdims=True)
            a_ref[s, rows, :] = (
                center * lax.rsqrt(spread_of + EPSILON) * gain_ref[...] + shift_ref[...]
            ).astype(BF16)


def mix_streams(perm, inputs, coeff, gain, shift, tile=64):
    prev, tokens, width = inputs.shape
    return pl.pallas_call(
        mix_kernel,
        name="mix",
        grid_spec=pltpu.PrefetchScalarGridSpec(
            num_scalar_prefetch=1,
            grid=(tokens // tile,),
            in_specs=[
                pl.BlockSpec((prev, tile, width), lambda t, *_: (0, t, 0)),
                pl.BlockSpec((tile // GROUP,) + coeff.shape[1:], lambda t, *_: (t, 0, 0)),
                pl.BlockSpec((1, width), lambda t, *_: (0, 0)),
                pl.BlockSpec((1, width), lambda t, *_: (0, 0)),
            ],
            out_specs=[
                pl.BlockSpec((STREAMS - 1, tile, width), lambda t, *_: (0, t, 0)),
                pl.BlockSpec((STREAMS, tile, width), lambda t, *_: (0, t, 0)),
            ],
        ),
        out_shape=[
            jax.ShapeDtypeStruct((STREAMS - 1, tokens, width), BF16),
            jax.ShapeDtypeStruct((STREAMS, tokens, width), F32),
        ],
        cost_estimate=cost(14),
        compiler_params=params(1),
    )(perm, inputs, coeff, gain, shift)


def turn(values, tables, sign):
    base, up, down = tables
    return (
        values * base
        + sign * (pltpu.roll(values, ROT // 2, 1) * up)
        + sign * (pltpu.roll(values, HD - ROT // 2, 1) * down)
    )


def blocks_dot(a_ref, weights):
    parts = len(weights)
    block = a_ref.shape[-1] // parts
    total = None
    for p in range(parts):
        term = jnp.dot(
            a_ref[:, p * block : (p + 1) * block], weights[p][...], preferred_element_type=F32
        )
        total = term if total is None else total + term
    return total


def block_specs(weights, rows, columns, at):
    return [pl.BlockSpec((rows, columns), lambda *ids: (0, at(*ids)))] * len(weights)


def heads_kernel(target_ref, perm_ref, a_ref, *refs, parts, turned):
    weights = refs[:parts]
    tables = refs[parts : parts + 3]
    outs = refs[parts + 3 :]
    total = blocks_dot(a_ref.at[0], weights)
    kind, step = pl.program_id(0), pl.program_id(1)
    for s, out_ref in enumerate(outs):

        @pl.when((step == s) & (kind < turned))
        def _():
            tabs = [t[...] for t in tables]
            for h in range(total.shape[1] // HD):
                cols = slice(h * HD, (h + 1) * HD)
                out_ref[0, :, cols] = turn(total[:, cols], tabs, 1.0).astype(BF16)

        @pl.when((step == s) & (kind >= turned))
        def _():
            out_ref[0] = total.astype(BF16)


def to_chunks(target, perm, a, weights, tables, turned):
    kinds, tokens, width = a.shape
    parts = perm.shape[0]
    chunks = target.shape[0]
    columns = weights[0].shape[1] // chunks // kinds
    specs = block_specs(
        weights, width // parts, columns, lambda s, n, target, _: s * chunks + target[n]
    )
    return pl.pallas_call(
        partial(heads_kernel, parts=parts, turned=turned),
        name="heads",
        grid_spec=pltpu.PrefetchScalarGridSpec(
            num_scalar_prefetch=2,
            grid=(kinds, chunks),
            in_specs=[pl.BlockSpec((1, tokens, width), lambda s, n, *_: (s, 0, 0))]
            + specs
            + [pl.BlockSpec((tokens, HD), lambda s, n, *_: (0, 0))] * 3,
            out_specs=[pl.BlockSpec((1, tokens, columns), lambda s, n, *_: (s, 0, 0))] * chunks,
        ),
        out_shape=[jax.ShapeDtypeStruct((kinds, tokens, columns), BF16)] * chunks,
        cost_estimate=cost(2 * kinds * chunks),
        compiler_params=params(2),
    )(target, perm, a, *weights, *tables)


def join_kernel(target_ref, *refs):
    for s in range(len(refs) - 1):

        @pl.when(pl.program_id(0) == s)
        def _():
            refs[-1][...] = refs[s][...]


def join(target, pieces):
    kinds, count, columns = pieces[0].shape
    chunks = len(pieces)
    return pl.pallas_call(
        join_kernel,
        name="join",
        grid_spec=pltpu.PrefetchScalarGridSpec(
            num_scalar_prefetch=1,
            grid=(chunks,),
            in_specs=[pl.BlockSpec((kinds, count, columns), lambda n, _: (0, 0, 0))] * chunks,
            out_specs=pl.BlockSpec((kinds, count, columns), lambda n, target: (0, 0, target[n])),
        ),
        out_shape=jax.ShapeDtypeStruct((kinds, count, columns * chunks), BF16),
        cost_estimate=cost(2),
        compiler_params=params(1),
    )(target, *pieces)


def weights_of(query, keys, tile_index, tile, length, scale):
    count = keys.shape[0]
    scores = (
        lax.dot_general(query, keys, (((1,), (1,)), ((), ())), preferred_element_type=F32) * scale
    )
    row = tile_index * tile + lax.broadcasted_iota(jnp.int32, (tile, count), 0)
    col = lax.broadcasted_iota(jnp.int32, (tile, count), 1)
    masked = jnp.where((col <= row) & (col < length), scores, NEGATIVE)
    expo = jnp.exp(masked - jnp.max(masked, axis=-1, keepdims=True))
    return expo / jnp.sum(expo, axis=-1, keepdims=True)


def collect(source_ref, pieces, scratch, span):
    for s, piece in enumerate(pieces):
        at = pl.ds(pl.multiple_of(source_ref[s] * span, span), span)
        scratch[at, :] = piece[...]


def spread_out(source_ref, scratch, pieces, span):
    for s, piece in enumerate(pieces):
        at = pl.ds(pl.multiple_of(source_ref[s] * span, span), span)
        piece[...] = scratch[at, :]


def collect(source_ref, pieces, kind, scratch):
    span = pieces[0].shape[1]
    for s, piece in enumerate(pieces):
        at = pl.ds(pl.multiple_of(source_ref[s] * span, span), span)
        scratch[at, :] = piece[kind]


def spread_out(source_ref, scratch, pieces, kind):
    span = pieces[0].shape[1]
    for s, piece in enumerate(pieces):
        at = pl.ds(pl.multiple_of(source_ref[s] * span, span), span)
        piece[kind] = scratch[at, :]


def attend_kernel(source_ref, length_ref, *refs, chunks):
    ins, outs = refs[:chunks], refs[chunks : 2 * chunks]
    q_all, k_all, v_all, o_all = refs[2 * chunks :]
    span = ins[0].shape[1]
    length = length_ref[pl.program_id(0)]
    scale = 1.0 / math.sqrt(HD)
    for kind, scratch in enumerate((q_all, k_all, v_all)):
        collect(source_ref, ins, kind, scratch)
    for h in range(q_all.shape[1] // HD):
        cols = slice(h * HD, (h + 1) * HD)
        for i in range(chunks):
            rows = slice(i * span, (i + 1) * span)
            seen = slice(0, (i + 1) * span)
            probs = weights_of(q_all[rows, cols], k_all[seen, cols], i, span, length, scale)
            o_all[rows, cols] = jnp.dot(
                probs.astype(BF16), v_all[seen, cols], preferred_element_type=F32
            ).astype(BF16)
    spread_out(source_ref, o_all, outs, 0)


def attend(source, lengths, pieces):
    chunks = len(pieces)
    rows = lengths.shape[0]
    kinds, tokens, columns = pieces[0].shape
    span = tokens // rows
    return pl.pallas_call(
        partial(attend_kernel, chunks=chunks),
        name="attend",
        grid_spec=pltpu.PrefetchScalarGridSpec(
            num_scalar_prefetch=2,
            grid=(rows,),
            in_specs=[pl.BlockSpec((kinds, span, columns), lambda r, *_: (0, r, 0))] * chunks,
            out_specs=[pl.BlockSpec((1, span, columns), lambda r, *_: (0, r, 0))] * chunks,
            scratch_shapes=[pltpu.VMEM((span * chunks, columns), BF16)] * 4,
        ),
        out_shape=[jax.ShapeDtypeStruct((1, tokens, columns), BF16)] * chunks,
        cost_estimate=cost(6 * rows),
        compiler_params=params(1),
    )(source, lengths, *pieces)


def attend_back_kernel(source_ref, length_ref, *refs, chunks, row):
    ins, grads = refs[:chunks], refs[chunks : 2 * chunks]
    tabs = refs[2 * chunks : 2 * chunks + 3]
    outs = refs[2 * chunks + 3 : 3 * chunks + 3]
    q_all, k_all, v_all, g_all, dk_sum, dv_sum, dq_all, dk_all, dv_all = refs[3 * chunks + 3 :]
    span = ins[0].shape[1]
    length = length_ref[row]
    scale = 1.0 / math.sqrt(HD)
    for kind, scratch in enumerate((q_all, k_all, v_all)):
        collect(source_ref, ins, kind, scratch)
    collect(source_ref, grads, 0, g_all)
    for h in range(q_all.shape[1] // HD):
        cols = slice(h * HD, (h + 1) * HD)
        for i in reversed(range(chunks)):
            rows = slice(i * span, (i + 1) * span)
            seen = slice(0, (i + 1) * span)
            query, grad = q_all[rows, cols], g_all[rows, cols]
            keys, values = k_all[seen, cols], v_all[seen, cols]
            probs = weights_of(query, keys, i, span, length, scale)
            grad_probs = lax.dot_general(grad, values, NT, preferred_element_type=F32)
            delta = jnp.sum(probs * grad_probs, axis=-1, keepdims=True)
            scores = (probs * (grad_probs - delta) * scale).astype(BF16)
            turned = [t[rows, :] for t in tabs]
            dq_all[rows, cols] = turn(
                jnp.dot(scores, keys, preferred_element_type=F32), turned, -1.0
            ).astype(BF16)
            dk = lax.dot_general(scores, query, TN, preferred_element_type=F32)
            dv = lax.dot_general(probs.astype(BF16), grad, TN, preferred_element_type=F32)
            if i == chunks - 1:
                dk_sum[...] = dk
                dv_sum[...] = dv
            else:
                dk_sum[seen, :] += dk
                dv_sum[seen, :] += dv
        dk_all[:, cols] = turn(dk_sum[...], [t[...] for t in tabs], -1.0).astype(BF16)
        dv_all[:, cols] = dv_sum[...].astype(BF16)
    for kind, scratch in enumerate((dq_all, dk_all, dv_all)):
        spread_out(source_ref, scratch, outs, kind)


def attend_back(source, lengths, pieces, grads, tables, row):
    chunks = len(pieces)
    rows = lengths.shape[0]
    kinds, tokens, columns = pieces[0].shape
    span = tokens // rows
    seq = span * chunks
    wide = pltpu.VMEM((seq, columns), BF16)
    return pl.pallas_call(
        partial(attend_back_kernel, chunks=chunks, row=row),
        name="attend_back",
        grid_spec=pltpu.PrefetchScalarGridSpec(
            num_scalar_prefetch=2,
            grid=(1,),
            in_specs=[pl.BlockSpec((kinds, span, columns), lambda r, *_: (0, row, 0))] * chunks
            + [pl.BlockSpec((1, span, columns), lambda r, *_: (0, row, 0))] * chunks
            + [pl.BlockSpec((seq, HD), lambda r, *_: (0, 0))] * 3,
            out_specs=[pl.BlockSpec((kinds, span, columns), lambda r, *_: (0, 0, 0))] * chunks,
            scratch_shapes=[wide] * 4 + [pltpu.VMEM((seq, HD), F32)] * 2 + [wide] * 3,
        ),
        out_shape=[jax.ShapeDtypeStruct((kinds, span, columns), BF16)] * chunks,
        cost_estimate=cost(12),
        compiler_params=params(1),
    )(source, lengths, *pieces, *grads, *tables)


def up_kernel(perm_ref, a_ref, *refs, parts):
    weights = refs[:parts]
    active_ref, slope_ref = refs[parts:]
    u = blocks_dot(a_ref, weights)
    half = 0.5 * (1.0 + lax.erf(u * math.sqrt(0.5)))
    active_ref[...] = (u * half).astype(BF16)
    slope_ref[...] = half + u * jnp.exp(-0.5 * u * u) * (1.0 / math.sqrt(2.0 * math.pi))


def up_stage(perm, a, weights, part, columns, tile=512):
    tokens, width = a.shape
    parts = perm.shape[0]
    tile = min(tile, columns)
    specs = block_specs(weights, width // parts, tile, lambda n, *_: part * (columns // tile) + n)
    out = pl.BlockSpec((tokens, tile), lambda n, *_: (0, n))
    return pl.pallas_call(
        partial(up_kernel, parts=parts),
        name="up",
        grid_spec=pltpu.PrefetchScalarGridSpec(
            num_scalar_prefetch=1,
            grid=(columns // tile,),
            in_specs=[pl.BlockSpec((tokens, width), lambda n, *_: (0, 0))] + specs,
            out_specs=[out, out],
        ),
        out_shape=[
            jax.ShapeDtypeStruct((tokens, columns), BF16),
            jax.ShapeDtypeStruct((tokens, columns), F32),
        ],
        cost_estimate=cost(columns / 200),
        compiler_params=params(1),
    )(perm, a, *weights)


def up_back_kernel(perm_ref, a_ref, slope_ref, *refs, parts):
    weights = refs[:parts]
    refs[parts][...] = (blocks_dot(a_ref, weights) * slope_ref[...]).astype(BF16)


def up_back(perm, a, slope, weights, offset, tile=512):
    tokens, width = a.shape
    parts = perm.shape[0]
    columns = slope.shape[1]
    tile = min(tile, columns)
    specs = block_specs(
        weights, width // parts, tile, lambda n, *_: offset // tile + n
    )
    out = pl.BlockSpec((tokens, tile), lambda n, *_: (0, n))
    return pl.pallas_call(
        partial(up_back_kernel, parts=parts),
        name="up_back",
        grid_spec=pltpu.PrefetchScalarGridSpec(
            num_scalar_prefetch=1,
            grid=(columns // tile,),
            in_specs=[pl.BlockSpec((tokens, width), lambda n, *_: (0, 0)), out] + specs,
            out_specs=out,
        ),
        out_shape=jax.ShapeDtypeStruct((tokens, columns), BF16),
        cost_estimate=cost(columns / 200),
        compiler_params=params(1),
    )(perm, a, slope, *weights)


def back_kernel(*refs, lefts, parts, adds):
    out_ref = refs[-1]
    block = out_ref.shape[1] // parts
    tile = refs[lefts].shape[0]
    n = pl.program_id(0)
    for p in range(parts):
        at = pl.ds(pl.multiple_of(p * block + n * tile, 128), tile)
        total = refs[-2][:, at] if adds else None
        for h in range(lefts):
            term = lax.dot_general(
                refs[h][...], refs[lefts + h * parts + p][...], NT, preferred_element_type=F32
            )
            total = term if total is None else total + term
        out_ref[:, at] = total.astype(out_ref.dtype)


def to_width(lefts, weights, width, added=(), dtype=BF16, across=(0,)):
    parts = len(weights[0])
    block = width // parts
    tile = min(block, 256)
    tokens = lefts[0].shape[0]
    left_specs, specs, arrays = [], [], []
    for left, weight, at in zip(lefts, weights, across):
        columns = left.shape[1]
        left_specs.append(pl.BlockSpec((tokens, columns), lambda n: (0, 0)))
        specs += [pl.BlockSpec((tile, columns), lambda n, at=at: (n, at))] * parts
        arrays += weight
    whole = pl.BlockSpec((tokens, width), lambda n: (0, 0))
    return pl.pallas_call(
        partial(back_kernel, lefts=len(lefts), parts=parts, adds=len(added)),
        name="to_width",
        grid=(block // tile,),
        in_specs=left_specs + specs + [whole] * len(added),
        out_specs=whole,
        out_shape=jax.ShapeDtypeStruct((tokens, width), dtype),
        cost_estimate=cost(sum(a.shape[1] for a in lefts) / 256),
        compiler_params=params(1),
    )(*lefts, *arrays, *added)


def grad_kernel(*refs, count, rights, adds):
    lefts, fars = refs[:count], refs[count : 2 * count]
    sides = refs[2 * count : 2 * count + rights], refs[2 * count + rights : 2 * count + 2 * rights]
    add_refs, out_ref = refs[2 * count + 2 * rights : -1], refs[-1]
    at = 0
    for b in range(count):
        total = None
        for left, right_refs in zip((lefts[b], fars[b]), sides):
            start = 0
            for right in right_refs:
                size = right.shape[1]
                term = lax.dot_general(
                    left[0, start : start + size, :], right[0], TN, preferred_element_type=F32
                )
                total = term if total is None else total + term
                start += size
        for n in range(adds[b]):
            total = total + add_refs[at + n][0].astype(F32)
        at += adds[b]
        out_ref[b] = total.astype(BF16)


def grad_blocks(left, left_far, near, far, parts, chosen, added, first, kinds, tile=512):
    _, tokens, width = left.shape
    columns = near[0].shape[2]
    tile = min(tile, columns)
    steps = columns // tile
    block = width // parts

    def place(start, row):
        return lambda s, n: (row, 0, (first - start + s) * steps + n)

    flat = [a for arrays in added for a in arrays]
    left_specs = [
        pl.BlockSpec((1, tokens, block), lambda s, n, p=p: (first + s, 0, p)) for p in chosen
    ]
    return pl.pallas_call(
        partial(
            grad_kernel,
            count=len(chosen),
            rights=len(near),
            adds=tuple(len(a) for a in added),
        ),
        name="grad",
        grid=(kinds, steps),
        in_specs=left_specs * 2
        + [
            pl.BlockSpec((1, r.shape[1], tile), lambda s, n: (first + s, 0, n))
            for r in (*near, *far)
        ]
        + [pl.BlockSpec((1, block, tile), place(start, row)) for _, row, start in flat],
        out_specs=pl.BlockSpec((len(chosen), block, tile), lambda s, n: (0, 0, s * steps + n)),
        out_shape=jax.ShapeDtypeStruct((len(chosen), block, kinds * columns), BF16),
        cost_estimate=cost(len(chosen) * kinds * columns / 512),
        compiler_params=params(2),
    )(*[left] * len(chosen), *[left_far] * len(chosen), *near, *far, *[a for a, _, _ in flat])


def part_kernel(in_ref, out_ref, *, turned):
    values = in_ref[...]
    out_ref[...] = values.astype(F32).T.astype(BF16) if turned else values


def shard_part(shard, n, size, turned):
    short = shard.shape[1] if turned else shard.shape[0]
    spec = pl.BlockSpec((size, short), lambda i: (n, 0))
    if not turned:
        spec = pl.BlockSpec((short, size), lambda i: (0, n))
    return pl.pallas_call(
        partial(part_kernel, turned=turned),
        name="part",
        grid=(1,),
        in_specs=[spec],
        out_specs=pl.BlockSpec((short, size), lambda i: (0, 0)),
        out_shape=jax.ShapeDtypeStruct((short, size), BF16),
        cost_estimate=cost(1),
        compiler_params=params(1),
    )(shard)


def hat_of(z):
    center = z - jnp.mean(z, axis=-1, keepdims=True)
    inverse = lax.rsqrt(jnp.mean(center * center, axis=-1, keepdims=True) + EPSILON)
    return center * inverse, inverse


def own_kernel(perm_ref, grad_ref, z_ref, *refs, parts):
    weights = refs[:parts]
    out_ref, sum_ref = refs[parts:]
    block = weights[0].shape[0]
    for p in range(parts):
        out_ref[0, :, p * block : (p + 1) * block] = lax.dot_general(
            grad_ref[0], weights[p][...], NT, preferred_element_type=F32
        )
    tile = 32
    tokens, width = out_ref.shape[1:]
    gain = jnp.zeros((8, width), F32)
    shift = jnp.zeros((8, width), F32)
    for t in range(0, tokens, tile):
        d = out_ref[0, t : t + tile, :]
        hat, _ = hat_of(z_ref[0, t : t + tile, :])
        gain = gain + jnp.sum((d * hat).reshape(tile // 8, 8, width), axis=0)
        shift = shift + jnp.sum(d.reshape(tile // 8, 8, width), axis=0)
    sum_ref[0, :8] = gain
    sum_ref[0, 8:] = shift


def own_part(perm, grads, streams, weights, row):
    kinds, span, columns = grads.shape
    width = streams.shape[2]
    parts = perm.shape[0]
    specs = block_specs(weights, width // parts, columns, lambda s, *_: s)
    return pl.pallas_call(
        partial(own_kernel, parts=parts),
        name="own",
        grid_spec=pltpu.PrefetchScalarGridSpec(
            num_scalar_prefetch=1,
            grid=(kinds,),
            in_specs=[
                pl.BlockSpec((1, span, columns), lambda s, *_: (s, 0, 0)),
                pl.BlockSpec((1, span, width), lambda s, *_: (s, row, 0)),
            ]
            + specs,
            out_specs=[
                pl.BlockSpec((1, span, width), lambda s, *_: (s, 0, 0)),
                pl.BlockSpec((1, 16, width), lambda s, *_: (s, 0, 0)),
            ],
        ),
        out_shape=[
            jax.ShapeDtypeStruct((kinds, span, width), F32),
            jax.ShapeDtypeStruct((kinds, 16, width), F32),
        ],
        cost_estimate=cost(12),
        compiler_params=params(1),
    )(perm, grads, streams, *weights)


def other_kernel(grad_ref, part_ref, z_ref, gain_ref, *refs, parts):
    weights = refs[:parts]
    out_ref, total_ref = refs[parts:]
    block = weights[0].shape[0]
    for p in range(parts):
        cols = slice(p * block, (p + 1) * block)
        total_ref[:, cols] = part_ref[0, :, cols] + lax.dot_general(
            grad_ref[0], weights[p][...], NT, preferred_element_type=F32
        )
    tile = 32
    for t in range(0, total_ref.shape[0], tile):
        rows = slice(t, t + tile)
        hat, inverse = hat_of(z_ref[0, rows, :])
        e = total_ref[rows, :] * gain_ref[...]
        first = jnp.mean(e, axis=-1, keepdims=True)
        second = jnp.mean(e * hat, axis=-1, keepdims=True)
        out_ref[0, rows, :] = ((e - first - hat * second) * inverse).astype(BF16)


def other_part(grads, own, streams, gain, weights, row):
    kinds, span, columns = grads.shape
    width = streams.shape[2]
    parts = len(weights)
    block = width // parts
    return pl.pallas_call(
        partial(other_kernel, parts=parts),
        name="other",
        grid=(kinds,),
        in_specs=[
            pl.BlockSpec((1, span, columns), lambda s: (s, 0, 0)),
            pl.BlockSpec((1, span, width), lambda s: (s, 0, 0)),
            pl.BlockSpec((1, span, width), lambda s: (s, row, 0)),
            pl.BlockSpec((1, width), lambda s: (0, 0)),
        ]
        + [pl.BlockSpec((block, columns), lambda s: (0, s))] * parts,
        out_specs=pl.BlockSpec((1, span, width), lambda s: (s, 0, 0)),
        out_shape=jax.ShapeDtypeStruct((kinds, span, width), BF16),
        scratch_shapes=[pltpu.VMEM((span, width), F32)],
        cost_estimate=cost(14),
        compiler_params=params(1),
    )(grads, own, streams, gain, *weights)


def last_kernel(perm_ref, earlier_ref, coeff_ref, dz_ref, dr_ref, *refs):
    out_ref, mix_ref = refs[-2:]
    prev, tile, width = earlier_ref.shape
    parts = perm_ref.shape[0]
    block = width // parts
    count, half = prev * GROUP, STREAMS * GROUP
    for g in range(tile // GROUP):
        rows = slice(g * GROUP, (g + 1) * GROUP)
        high, low = spread(coeff_ref[g])
        pairs = jnp.zeros((count, half), F32)
        for p in range(parts):
            here = slice(p * block, (p + 1) * block)
            there = pl.ds(pl.multiple_of(perm_ref[p] * block, 128), block)
            grads = jnp.concatenate(
                [dz_ref[s, rows, here] for s in range(STREAMS - 1)] + [dr_ref[rows, here]], axis=0
            )
            x = earlier_ref[:, rows, there].reshape(count, block)
            pairs = pairs + lax.dot_general(x, grads, NT, preferred_element_type=F32)
            total = jnp.dot(high, grads, preferred_element_type=F32) + jnp.dot(
                low, grads, preferred_element_type=F32
            )
            out_ref[:, rows, there] = total.astype(BF16).reshape(prev, GROUP, block)
        token = lax.broadcasted_iota(jnp.int32, (count, half), 0) % GROUP
        lane = lax.broadcasted_iota(jnp.int32, (count, half), 1)
        wide = lax.broadcasted_iota(jnp.int32, (count, 128), 1)
        mixed = jnp.zeros((count, 128), F32)
        for s in range(STREAMS):
            own = jnp.where(lane == token + s * GROUP, pairs, 0.0)
            mixed = jnp.where(wide == s, jnp.sum(own, axis=-1, keepdims=True), mixed)
        mix_ref[g] = mixed


def last_stage(perm, inputs, coeff, dz, dr, row, rows, before, tile=64):
    prev, tokens, width = inputs.shape
    steps = tokens // rows // tile
    count = prev * GROUP
    here = lambda t, *_: (0, row * steps + t, 0)
    return pl.pallas_call(
        last_kernel,
        name="last",
        grid_spec=pltpu.PrefetchScalarGridSpec(
            num_scalar_prefetch=1,
            grid=(steps,),
            in_specs=[
                pl.BlockSpec((prev, tile, width), here),
                pl.BlockSpec(
                    (tile // GROUP,) + coeff.shape[1:], lambda t, *_: (row * steps + t, 0, 0)
                ),
                pl.BlockSpec((STREAMS - 1, tile, width), lambda t, *_: (0, t, 0)),
                pl.BlockSpec((tile, width), lambda t, *_: (row * steps + t, 0)),
            ]
            + [pl.BlockSpec(memory_space=pl.ANY)] * len(before),
            out_specs=[
                pl.BlockSpec((prev, tile, width), here),
                pl.BlockSpec(
                    (tile // GROUP, count, 128), lambda t, *_: (row * steps + t, 0, 0)
                ),
            ],
        ),
        out_shape=[
            jax.ShapeDtypeStruct((prev, tokens, width), BF16),
            jax.ShapeDtypeStruct((tokens // GROUP, count, 128), F32),
        ],
        input_output_aliases={5 + n: n for n in range(len(before))},
        cost_estimate=cost(12),
        compiler_params=params(1),
    )(perm, inputs, coeff, dz, dr, *before)


def two_terms(values):
    high = values.astype(BF16)
    return high, (values - high.astype(F32)).astype(BF16)


def final_kernel(res_ref, mine_ref, theirs_ref, out_ref, cot_ref, valid_ref, in_ref, mix_ref, *refs):
    final_ref, grad_ref, low_ref, far_ref, high_ref, rest_ref, back_ref, inverse_ref = refs
    tile, width = res_ref.shape
    step = 16
    for t in range(0, tile, step):
        rows = slice(t, t + step)
        final = res_ref[rows, :] + (
            mine_ref[rows, :].astype(F32) + theirs_ref[rows, :].astype(F32)
        )
        inverse = lax.rsqrt(jnp.mean(final * final, axis=-1, keepdims=True) + RMS_EPSILON)
        final_ref[rows, :] = final
        inverse_ref[rows, :] = jnp.broadcast_to(inverse, (step, HD))
        high_ref[rows, :], rest_ref[rows, :] = two_terms(final * inverse)
    pre = sum(
        lax.dot_general(n[...], in_ref[...], NT, preferred_element_type=F32)
        for n in (high_ref, rest_ref)
    )
    grad_pre = lax.dot_general(
        cot_ref[...], mix_ref[...], NT, precision=HIGHEST, preferred_element_type=F32
    ) * (
        0.5 * (1.0 + lax.erf(pre * math.sqrt(0.5)))
        + pre * jnp.exp(-0.5 * pre * pre) * (1.0 / math.sqrt(2.0 * math.pi))
    )
    back_ref[...] = sum(
        jnp.dot(g, in_ref[...], preferred_element_type=F32) for g in two_terms(grad_pre)
    )
    for t in range(0, tile, step):
        rows = slice(t, t + step)
        inverse = inverse_ref[rows, :1]
        normed = final_ref[rows, :] * inverse
        grad = back_ref[rows, :]
        grad = inverse * (grad - normed * jnp.mean(grad * normed, axis=-1, keepdims=True))
        grad = out_ref[rows, :].astype(F32) * valid_ref[rows, :] + grad
        grad_ref[rows, :] = grad
        low = grad.astype(BF16)
        low_ref[rows, :] = low
        far_ref[rows, :] = low[:, width // 2 :]


def final_stage(residual, mine, theirs, grad_out, cotangent, valid, weight_in, weight_out, tile=128):
    tokens, width = residual.shape
    rows = pl.BlockSpec((tile, width), lambda t: (t, 0))
    cotangent = jnp.pad(cotangent, ((0, 0), (0, HD - MIXW)))
    weight_in = jnp.pad(weight_in, ((0, HD - MIXW), (0, 0))).astype(BF16)
    weight_out = jnp.pad(weight_out, ((0, HD - MIXW), (0, HD - MIXW)))
    return pl.pallas_call(
        final_kernel,
        name="final",
        grid=(tokens // tile,),
        in_specs=[
            rows,
            rows,
            rows,
            rows,
            pl.BlockSpec((tile, HD), lambda t: (t, 0)),
            pl.BlockSpec((tile, 1), lambda t: (t, 0)),
            pl.BlockSpec((HD, width), lambda t: (0, 0)),
            pl.BlockSpec((HD, HD), lambda t: (0, 0)),
        ],
        out_specs=[rows, rows, rows, pl.BlockSpec((tile, width // 2), lambda t: (t, 0))],
        out_shape=[
            jax.ShapeDtypeStruct((tokens, width), F32),
            jax.ShapeDtypeStruct((tokens, width), F32),
            jax.ShapeDtypeStruct((tokens, width), BF16),
            jax.ShapeDtypeStruct((tokens, width // 2), BF16),
        ],
        scratch_shapes=[
            pltpu.VMEM((tile, width), BF16),
            pltpu.VMEM((tile, width), BF16),
            pltpu.VMEM((tile, width), F32),
            pltpu.VMEM((tile, HD), F32),
        ],
        cost_estimate=cost(8),
        compiler_params=params(1),
    )(residual, mine, theirs, grad_out, cotangent, valid, weight_in, weight_out)


def second_kernel(res_ref, mine_ref, theirs_ref, grad_ref, gain_ref, out_ref, sum_ref):
    @pl.when(pl.program_id(0) == 0)
    def _():
        sum_ref[...] = jnp.zeros_like(sum_ref)

    step = 32
    width = res_ref.shape[1]
    for t in range(0, res_ref.shape[0], step):
        rows = slice(t, t + step)
        hat, inverse = hat_of(res_ref[rows, :])
        d = mine_ref[rows, :].astype(F32) + theirs_ref[rows, :].astype(F32)
        sum_ref[:8] += jnp.sum((d * hat).reshape(step // 8, 8, width), axis=0)
        sum_ref[8:] += jnp.sum(d.reshape(step // 8, 8, width), axis=0)
        e = d * gain_ref[...]
        first = jnp.mean(e, axis=-1, keepdims=True)
        second = jnp.mean(e * hat, axis=-1, keepdims=True)
        out_ref[rows, :] = (grad_ref[rows, :] + (e - first - hat * second) * inverse).astype(BF16)


def second_norm_back(residual, mine, theirs, grad, gain, tile=128):
    tokens, width = residual.shape
    rows = pl.BlockSpec((tile, width), lambda t: (t, 0))
    return pl.pallas_call(
        second_kernel,
        name="second",
        grid=(tokens // tile,),
        in_specs=[rows, rows, rows, rows, pl.BlockSpec((1, width), lambda t: (0, 0))],
        out_specs=[rows, pl.BlockSpec((16, width), lambda t: (0, 0))],
        out_shape=[
            jax.ShapeDtypeStruct((tokens, width), BF16),
            jax.ShapeDtypeStruct((16, width), F32),
        ],
        cost_estimate=cost(6),
        compiler_params=params(1),
    )(residual, mine, theirs, grad, gain)


def layer_norm(values, gain, shift):
    center = values - jnp.mean(values, axis=-1, keepdims=True)
    spread = jnp.mean(center * center, axis=-1, keepdims=True)
    return center * lax.rsqrt(spread + EPSILON) * gain + shift


def activate(values):
    return jax.nn.gelu(values, approximate=False)


def mixer(final, weight_in, weight_out, bias):
    normed = final * lax.rsqrt(jnp.mean(final * final, axis=-1, keepdims=True) + RMS_EPSILON)
    hidden = activate(
        lax.dot_general(
            normed, weight_in, NT, precision=HIGHEST, preferred_element_type=F32
        )
    )
    return jnp.dot(hidden, weight_out, precision=HIGHEST, preferred_element_type=F32) + bias


def turn_tables(positions):
    half = ROT // 2
    frequency = 10000.0 ** (-2.0 * jnp.arange(half, dtype=F32) / ROT)
    angles = positions.astype(F32)[:, None] * frequency[None, :]
    cosine, sine = jnp.cos(angles), jnp.sin(angles)
    count = positions.shape[0]
    rest = HD - ROT
    base = jnp.concatenate([cosine, cosine, jnp.ones((count, rest), F32)], axis=1)
    up = jnp.concatenate([jnp.zeros((count, half), F32), sine, jnp.zeros((count, rest), F32)], 1)
    down = jnp.concatenate([-sine, jnp.zeros((count, half + rest), F32)], axis=1)
    return base, up, down


def group_coeff(mix_in, count_prev, tokens):
    groups = tokens // GROUP
    c = mix_in.reshape(STREAMS, count_prev, groups, GROUP).transpose(2, 1, 3, 0)
    return c.reshape(groups, count_prev * GROUP, STREAMS)


def body(
    earlier,
    mix_in,
    lengths,
    w_query,
    w_key,
    w_value,
    w_proj,
    w_up,
    w_down,
    first_gain,
    first_shift,
    second_gain,
    second_shift,
    mixer_in,
    mixer_out,
    mixer_bias,
    grad_out,
    grad_mix,
):
    count_prev, rows, span, width = earlier.shape
    tokens = rows * span
    fsdp, ctx = lax.axis_size("fsdp"), lax.axis_size("ctx")
    me, z = lax.axis_index("fsdp"), lax.axis_index("ctx")
    masks = block_masks(fsdp)
    place_of = [masks.index(m) for m in range(fsdp)]
    block = width // fsdp
    piece = block // ctx
    heads_width = w_query.shape[1]
    hidden = w_up.shape[1]
    perm = jnp.stack([me ^ m for m in masks]).astype(jnp.int32)
    table = jnp.array(place_of, jnp.int32)
    ring = jnp.arange(ctx, dtype=jnp.int32)
    source = (z - ring + ctx) % ctx
    slots = z * span + jnp.arange(span, dtype=jnp.int32)
    valid = (slots[None, :] < lengths[:, None]).astype(F32).reshape(tokens)

    def relative(values):
        return jnp.concatenate(
            [
                lax.dynamic_slice_in_dim(values, perm[p] * block, block, values.ndim - 1)
                for p in range(fsdp)
            ],
            axis=-1,
        )

    def absolute(values):
        return jnp.concatenate(
            [
                lax.dynamic_slice_in_dim(values, table[a ^ me] * block, block, values.ndim - 1)
                for a in range(fsdp)
            ],
            axis=-1,
        )

    def part(values, p):
        return values[:, p * block : (p + 1) * block]

    small = jnp.concatenate(
        [mixer_in.T, first_gain[None], first_shift[None], second_gain[None], second_shift[None]], 0
    )
    around = jnp.zeros((ctx,) + small.shape, BF16)
    for s in range(ctx):
        got = small if s == 0 else shift_ctx(small, s)
        around = lax.dynamic_update_slice(around, got[None], (source[s], 0, 0))
    around = cross(around)
    around = jnp.stack(around + [over_fsdp(a, 1) for a in around])
    small_all = around.transpose(2, 0, 1, 3).reshape(small.shape[0], width).astype(F32)
    mixer_full = small_all[:MIXW]
    gain_first, shift_first, gain_second, shift_second = [
        small_all[MIXW + n : MIXW + n + 1] for n in range(4)
    ]

    half = hidden // 2
    ctx_qkv = gather_ctx(jnp.concatenate([w_query, w_key, w_value], axis=1))
    ctx_both = gather_ctx(jnp.concatenate([w_up, w_proj.T], axis=1))

    order = Order()
    Pace.value = FORWARD_PACE
    inputs = earlier.reshape(count_prev, tokens, width)
    coeff = group_coeff(mix_in, count_prev, tokens)
    def far_half(values):
        return over_fsdp(values[..., width // 2 :], 1)

    normed_in, streams = order.keep(
        mix_streams(perm, inputs, coeff, gain_first, shift_first)
    )
    tables_here = turn_tables(jnp.tile(slots, rows))
    tables_all = turn_tables(jnp.arange(span * ctx, dtype=jnp.int32))
    target = (z + ring) % ctx
    tables_here, tables_all = order.wait((tables_here, tables_all))
    normed_in_far = order.wait(far_half(order(normed_in)))

    def to_heads(chunks):
        return [chunks[0]] + [shift_ctx(chunks[s], s) for s in range(1, ctx)]

    def to_slots(pieces):
        return [pieces[0]] + [shift_ctx(pieces[s], -s) for s in range(1, ctx)]

    def to_core(parts):
        return [over_fsdp(p, 1) for p in parts]

    near_qkv = cross(order.wait(ctx_qkv))
    far_qkv = to_core(near_qkv[:1])
    other = [over_tp(near_qkv[0])]
    far_qkv = order.wait(far_qkv)
    other = order.wait(other)
    near_qkv = order.wait(near_qkv)
    far_qkv = order.wait(far_qkv + to_core(near_qkv[1:]))
    blocks_qkv = near_qkv + far_qkv
    pieces = to_heads(
        order.keep(to_chunks(target, perm, order(normed_in), blocks_qkv, tables_here, 2))
    )
    other = other + [over_tp(p) for p in near_qkv[1:]]
    near_both = cross(order.wait(ctx_both))
    pieces = order.wait(pieces)
    other = order.wait(other)
    outs = to_slots(order.keep(attend(source, lengths, order(pieces))))
    ctx_down = [
        gather_ctx(order.keep(shard_part(order(w_down), n, half, True))) for n in range(2)
    ]
    outs = order.wait(outs)
    attended = order.keep(join(target, order(outs)))[0]
    near_both = order.wait(near_both)
    near_proj = order.wait([b[:, hidden:] for b in near_both])
    blocks_proj = near_proj + order.wait(to_core(near_proj))
    near_down = [cross(order.wait(ctx_down[0]))]
    far_both = to_core(order(near_both))
    branch_mine = order.keep(to_width([order(attended)], [blocks_proj], width))
    branch_theirs = over_tp(branch_mine)
    blocks_up = near_both + order.wait(far_both)
    near_down[0] = order.wait(near_down[0])
    near_down.append(cross(order.wait(ctx_down[1])))
    branch_theirs = order.wait(branch_theirs)
    residual = streams[STREAMS - 1] + tp_sum(branch_mine, branch_theirs)

    normed = layer_norm(residual, gain_second, shift_second).astype(BF16)
    normed = order.wait(normed)
    far_down = [to_core(near_down[0])]
    other_far = to_core(other)
    active, slope = [], []
    for n in range(2):
        a, b = order.keep(up_stage(perm, order(normed), blocks_up, n, half))
        active.append(a)
        slope.append(b)
    far_down[0] = order.wait(far_down[0])
    other = other + order.wait(other_far)
    down_first = order.keep(
        to_width([order(active[0])], [near_down[0] + far_down[0]], width, (), F32)
    )
    near_down[1] = order.wait(near_down[1])
    far_down.append(order.wait(to_core(near_down[1])))
    blocks_down = [near + far for near, far in zip(near_down, far_down)]
    down_mine = order.keep(
        to_width([order(active[1])], blocks_down[1:], width, (down_first,))
    )
    down_theirs = over_tp(down_mine)
    grad_out_here = order.wait(relative(grad_out.reshape(tokens, width)))
    mix_cotangent = order.wait((grad_mix.reshape(MIXW, tokens) * valid[None]).T)
    down_theirs = order.wait(down_theirs)

    final, grad_final, grad_down_b, grad_down_near = order.keep(
        final_stage(
            residual,
            down_mine,
            order(down_theirs),
            grad_out_here,
            mix_cotangent,
            valid[:, None],
            mixer_full,
            mixer_out,
        )
    )

    Pace.value = BACKWARD_PACE
    active_far = [over_fsdp(a, 1) for a in active]
    normed_far = far_half(normed)
    attended_far = over_fsdp(attended, 1)
    grad_down_far = over_fsdp(grad_down_near, 1)
    active_far, normed_far, attended_far, grad_down_far = order.wait(
        (active_far, normed_far, attended_far, grad_down_far)
    )
    down = [
        Scatter(order, grad_down_b[None], [a[None]], grad_down_far[None], [f[None]])
        for a, f in zip(active, active_far)
    ]
    down[0].launch()
    grad_upward, upward_far = [], []
    for n in range(2):
        grad_upward.append(
            order.keep(up_back(perm, order(grad_down_b), slope[n], blocks_down[n], 0))
        )
        upward_far.append(over_fsdp(grad_upward[n], 1))
    normed_mine = order.keep(to_width(order(grad_upward), [blocks_up] * 2, width, (), BF16, (0, 1)))
    normed_theirs = over_tp(normed_mine)
    down[1].launch()
    Pace.value = 3 * BACKWARD_PACE
    grad_down = [scatter_ctx(down[0].finish())]
    Pace.value = BACKWARD_PACE
    upward_far = order.wait(upward_far)
    up = [
        Scatter(order, normed[None], [u[None]], normed_far[None], [f[None]])
        for u, f in zip(grad_upward, upward_far)
    ]
    up[0].launch()
    mix_value, mix_pull = jax.vjp(
        lambda *weights: mixer(order(final), *weights), mixer_full, mixer_out, mixer_bias
    )
    mix_out = mix_value.T.reshape(MIXW, rows, span)
    grad_mixer_first, grad_mixer_second, grad_mixer_shift = mix_pull(mix_cotangent)
    output = absolute(order(final).astype(BF16)).reshape(rows, span, width)
    tail = jnp.concatenate([grad_mixer_second, grad_mixer_shift[None]], axis=0)
    tail, grad_mixer_first, output, mix_out = order.wait(
        (tail, grad_mixer_first, output, mix_out)
    )
    normed_theirs = order.wait(normed_theirs)
    grad_branch_b, second_sums = order.keep(
        second_norm_back(residual, normed_mine, order(normed_theirs), grad_final, gain_second)
    )
    second_pair = second_sums.reshape(2, 8, width).sum(1)

    grad_branch_far = far_half(grad_branch_b)
    grad_chunks = order.keep(
        to_chunks(target, perm, order(grad_branch_b)[None], blocks_proj, tables_here, 0)
    )
    grad_branch_far = order.wait(grad_branch_far)
    grad_pieces = to_heads(grad_chunks)
    grad_down.append(scatter_ctx(down[1].finish()))
    up[1].launch()
    proj = Scatter(
        order, grad_branch_b[None], [attended[None]], grad_branch_far[None], [attended_far[None]]
    )
    made_proj = proj.make(1)
    proj.launch(0, None, order(made_proj))
    grad_pieces = order.wait(grad_pieces)
    back = [
        order.keep(attend_back(source, lengths, pieces, order(grad_pieces), tables_all, 0))
    ]
    grad_up = [scatter_ctx(up[0].finish())]
    sent = [to_slots(order(back[0]))]
    back.append(
        order.keep(attend_back(source, lengths, pieces, order(grad_pieces), tables_all, 1))
    )
    grad_down[0] = order.wait(grad_down[0])
    mine, theirs, own = [], [], []
    sent[0] = order.wait(sent[0])
    mine.append(order.keep(join(target, sent[0])))
    theirs.append(over_tp(mine[0]))
    sent.append(to_slots(order(back[1])))
    own.append(order.keep(own_part(perm, order(mine[0]), streams, blocks_qkv, 0)))
    grad_down[1] = order.wait(grad_down[1])
    grad_up[0] = order.wait(grad_up[0])
    sent[1] = order.wait(sent[1])
    mine.append(order.keep(join(target, sent[1])))
    theirs.append(over_tp(mine[1]))
    mine_far = [over_fsdp(m, 1) for m in order(mine)]
    grad_proj = scatter_ctx(proj.finish())
    grad_up.append(scatter_ctx(up[1].finish()))
    mine_far = order.wait(mine_far)
    qkv = Scatter(order, normed_in, mine, normed_in_far, mine_far)
    qkv.launch(0, 1)
    qkv.launch(1, 2)
    own.append(order.keep(own_part(perm, order(mine[1]), streams, blocks_qkv, 1)))
    theirs[0] = order.wait(theirs[0])
    grad_query = scatter_ctx(qkv.finish(0, 1))
    sums = (own[0][1] + own[1][1]).sum(0).reshape(2, 8, width).sum(1)
    sums = order.wait(sums)

    dz = order.keep(other_part(order(theirs[0]), own[0][0], streams, gain_first, other, 0))
    done = order.keep(
        last_stage(perm, inputs, coeff, order(dz), grad_branch_b, 0, rows, ())
    )
    grad_proj = order.wait(grad_proj)
    theirs[1] = order.wait(theirs[1])
    grad_rest = scatter_ctx(qkv.finish(1, 2))
    Pace.value = FORWARD_PACE
    sums_far = over_tp(order(sums))
    dz = order.keep(other_part(order(theirs[1]), own[1][0], streams, gain_first, other, 1))
    sums_far = order.wait(sums_far)
    packed = jnp.concatenate(
        [grad_mixer_first, sums + sums_far, second_pair], axis=0
    )
    packed = packed.reshape(packed.shape[0], fsdp, ctx, piece)
    packed = jnp.stack(
        [lax.dynamic_index_in_dim(packed, z ^ m, 2, keepdims=False) for m in block_masks(ctx)]
    ).transpose(0, 2, 1, 3)
    tail = jnp.pad(tail, ((0, 0), (0, HD - MIXW)))
    packed, tail = order.wait((packed, tail))

    def fold(packed, tail, move):
        split = packed.shape[0] // 2
        return packed[:split], tail, move(packed[split:]), move(tail)

    def landed(packed, tail, got_packed, got_tail):
        got_packed, got_tail = order.wait((got_packed, got_tail))
        return packed + got_packed, tail + got_tail

    ctx_steps = [
        (lambda v, bit=bit: lax.ppermute(v, "ctx", xor_pairs(ctx, bit)))
        for bit in reversed(bits_of(ctx))
    ]
    fsdp_steps = [(lambda v, bit=bit: over_fsdp(v, bit)) for bit in reversed(bits_of(fsdp))]
    moving = fold(packed, tail, ctx_steps[0])
    grad_up[1] = order.wait(grad_up[1])
    for step in ctx_steps[1:]:
        moving = fold(*landed(*moving), step)
    grad_inputs, grad_coeff = order.keep(
        last_stage(perm, inputs, coeff, order(dz), grad_branch_b, 1, rows, done)
    )
    packed, tail = landed(*moving)
    moving = fold(packed[0], tail, fsdp_steps[0])
    for step in fsdp_steps[1:]:
        moving = fold(*landed(*moving), step)
    packed, tail = landed(*moving)
    norms = packed[0]
    grad_key, grad_value = jnp.split(grad_rest, 2, axis=1)
    grad_proj = grad_proj.T
    grad_earlier = grad_inputs.reshape(earlier.shape)
    grad_mix_in = (
        grad_coeff[:, :, :STREAMS]
        .reshape(tokens // GROUP, count_prev, GROUP, STREAMS)
        .transpose(3, 1, 0, 2)
        .reshape(mix_in.shape)
    )
    return (
        output,
        mix_out,
        grad_earlier,
        grad_mix_in,
        grad_query,
        grad_key,
        grad_value,
        grad_proj,
        jnp.concatenate(grad_up, axis=1),
        jnp.concatenate(grad_down, axis=1).T,
        norms[MIXW],
        norms[MIXW + 1],
        norms[MIXW + 2],
        norms[MIXW + 3],
        norms[:MIXW].T,
        tail[:MIXW, :MIXW],
        tail[MIXW, :MIXW],
    )


def solution(mesh):
    placed = (
        P(None, "fsdp", "ctx", None),
        P(None, "fsdp", "ctx"),
        P("fsdp"),
        P(("fsdp", "ctx"), "tp"),
        P(("fsdp", "ctx"), "tp"),
        P(("fsdp", "ctx"), "tp"),
        P("tp", ("fsdp", "ctx")),
        P(("fsdp", "ctx"), "tp"),
        P("tp", ("fsdp", "ctx")),
        P(("fsdp", "ctx")),
        P(("fsdp", "ctx")),
        P(("fsdp", "ctx")),
        P(("fsdp", "ctx")),
        P(("fsdp", "ctx"), None),
        P(),
        P(),
        P("fsdp", "ctx", None),
        P(None, "fsdp", "ctx"),
    )
    return jax.shard_map(
        body,
        mesh=mesh,
        in_specs=placed,
        out_specs=(
            P("fsdp", "ctx", None),
            P(None, "fsdp", "ctx"),
            P(None, "fsdp", "ctx", None),
            P(None, "fsdp", "ctx"),
            P(("fsdp", "ctx"), "tp"),
            P(("fsdp", "ctx"), "tp"),
            P(("fsdp", "ctx"), "tp"),
            P("tp", ("fsdp", "ctx")),
            P(("fsdp", "ctx"), "tp"),
            P("tp", ("fsdp", "ctx")),
            P(("fsdp", "ctx")),
            P(("fsdp", "ctx")),
            P(("fsdp", "ctx")),
            P(("fsdp", "ctx")),
            P(("fsdp", "ctx"), None),
            P(),
            P(),
        ),
        check_vma=False,
    )
```
